32 devices in a mesh: replica: 2 (over y), shard: 16 (over z, x, core).
Axes of the slice: x: 2, y: 2, z: 4, core: 2. Of those that a mesh axis runs over, the one named last changes fastest.
Arguments:
- inputs: bfloat16 [2, 2, 2048, 2048], P('replica', None, 'shard'), may hold values from -6 to 6
- cotangent: bfloat16 [2, 2, 2048, 2048], P('replica', None, 'shard'), may hold values from -6 to 6
- lengths: int32 [2, 2, 4], P('replica'), may hold values from 1 to 1024, 2048 in all within a row
- padding: int32 [2, 2, 2048], P('replica', None, 'shard'), may hold values 0 or 1
- attention_norm_gain: bfloat16 [2048], P('shard'), may hold values from 0.5 to 1.5
- joint_projection_weight: bfloat16 [2048, 3072], P('shard'), may hold values from -0.125 to 0.125
- adapter_down_factors: bfloat16 [2048, 24], P('shard'), may hold values from -0.125 to 0.125
- adapter_up_factors: bfloat16 [8, 3072], P(None, 'shard'), may hold values from -0.59765625 to 0.59765625
- output_weight: bfloat16 [2048, 2048], P('shard'), may hold values from -0.75 to 0.75
- adapter_output_down: bfloat16 [2048, 8], P('shard'), may hold values from -0.75 to 0.75
- adapter_output_upper: bfloat16 [8, 2048], P(None, 'shard'), may hold values from -1.796875 to 1.796875
- feature_query_map: bfloat16 [2048, 64], P('shard'), may hold values from -0.75 to 0.75
- feature_key_map: bfloat16 [512, 64], P('shard'), may hold values from -0.75 to 0.75
- feedforward_norm_gain: bfloat16 [2048], P('shard'), may hold values from 0.5 to 1.5
- gate_up_weight: bfloat16 [2048, 16384], P('shard'), may hold values from -0.125 to 0.125
- down_weight: bfloat16 [8192, 2048], P('shard'), may hold values from -0.0625 to 0.0625
Outputs:
- output: bfloat16 [2, 2, 2048, 2048], P('replica', None, 'shard')
- grad_inputs: bfloat16 [2, 2, 2048, 2048], P('replica', None, 'shard')
- grad_norm_attn: float32 [2048], P('shard')
- grad_w_qkv: float32 [2048, 3072], P('shard')
- grad_lora_down: float32 [2048, 24], P('shard')
- grad_lora_up: float32 [8, 3072], P(None, 'shard')
- grad_w_out: float32 [2048, 2048], P('shard')
- grad_lora_out_down: float32 [2048, 8], P('shard')
- grad_lora_out_up: float32 [8, 2048], P(None, 'shard')
- grad_feat_query: float32 [2048, 64], P('shard')
- grad_feat_key: float32 [512, 64], P('shard')
- grad_norm_ffn: float32 [2048], P('shard')
- grad_w_gate_up: float32 [2048, 16384], P('shard')
- grad_w_down: float32 [8192, 2048], P('shard')
The draws below stay inside these ranges and needn't reach their ends.
Inputs may be any that keep to these rules, and one draw needn't show every extreme that they name: Each row of lengths sums to 2048, and its largest entry is 1024.
All inputs are finite; a program needn't handle non-finite values. No bound on the sum of `padding` on one device may be relied on, other than what follows from the above.
Results may differ from the reference program's by a relative error of at most 0.015.
The reference program's roundings to bfloat16 on the way count: a program that leaves them out, or rounds other values in their place, can miss the bound.
Values may be sent and summed in bfloat16 or wider, within the bound.
No kernel may reach another device: no remote copies, remote signals or barrier semaphores. Data moves between devices by JAX's collectives and lax.ppermute only.
A program may use at most 576 MiB of HBM per device.

```python
import math
import jax
import jax.numpy as jnp
import numpy as np
from jax import lax

MODEL_WIDTH = 2048
HEADS = 32
KV_HEADS = 8
HEAD_DIM = 64
FF = 8192
ADAPTER_RANK = 8
WINDOW = 64
MAXLEN = 1024
MICRO = 2
REPLICAS = 2
STREAM = 2048
DOCS = 4
JOINT_COLUMNS = 3072


def touch_ends(values, stream_key, smallest, top_value):
    index_at = [jax.random.randint(jax.random.fold_in(stream_key, axis), (), 0, length) for axis, length in enumerate(values.shape)]
    widest = values.shape.index(max(values.shape))
    neighbour = index_at[:widest] + [(index_at[widest] + 1) % values.shape[widest]] + index_at[widest + 1:]
    return values.at[tuple(index_at)].set(smallest).at[tuple(neighbour)].set(top_value)


def block_scale(key, shape, shards, low, high):
    level = 1.0
    for axis_at, shards_of in shards:
        steps = jax.random.uniform(jax.random.fold_in(jax.random.fold_in(key, 6), axis_at), (shards_of,), jnp.float32, low / len(shards), high / len(shards))
        level = level * jnp.repeat(jnp.exp(steps), shape[axis_at] // shards_of).reshape((-1,) + (1,) * (len(shape) - 1 - axis_at))
    return level


def profile(count, total, reach, lean):
    portions = [(1 << 20) // math.isqrt(grade ** lean) + 1 for grade in range(2, count + 1)]
    spare, counts = total - reach - (count - 1), [1] * (count - 1)
    while spare > 0:
        candidates = [i for i in range(count - 1) if counts[i] < reach]
        mass, remaining = sum([portions[i] for i in candidates]), spare
        for i in candidates:
            addition = min(reach - counts[i], max(1, remaining * portions[i] // mass), spare)
            counts[i] = counts[i] + addition
            spare = spare - addition
    return np.array([reach] + counts)


def ragged(key, amount, total, bound, skew):
    if amount == 2:
        one = jax.random.randint(key, (), max(1, total - bound), min(bound, total - 1) + 1)
        return jnp.stack([one, total - one])
    tallies = jnp.asarray(profile(amount, total, bound, skew), jnp.int32)
    pairs = (amount - 1) // 2
    source_of, sink = tallies[1:1 + 2 * pairs:2], tallies[2:2 + 2 * pairs:2]
    margin = jnp.minimum(source_of - 1, bound - sink)
    passed = jax.random.randint(jax.random.fold_in(key, 1), (pairs,), 0, 1 << 20) % (margin + 1)
    tallies = tallies.at[1:1 + 2 * pairs:2].set(source_of - passed).at[2:2 + 2 * pairs:2].set(sink + passed)
    return tallies[jax.random.permutation(jax.random.fold_in(key, 2), amount)]


def gaussian(rng, shape, scale, limit, split=(), kind=jnp.bfloat16):
    drawn = jax.random.normal(rng, shape, jnp.float32) * scale
    if len(split) > 0:
        drawn = block_scale(rng, shape, split, -0.22, 0.18) * drawn
    return jnp.clip(drawn, min=-limit, max=limit).astype(kind)


def setup_inputs(seed: int = 0) -> dict:
    key_of = jax.random.split(jax.random.key(seed), 17)
    return {
        "inputs": gaussian(key_of[0], (REPLICAS, MICRO, STREAM, MODEL_WIDTH), 1.0, 6.0, ((0, 2), (2, 16))),
        "cotangent": gaussian(key_of[1], (REPLICAS, MICRO, STREAM, MODEL_WIDTH), 1.0, 6.0, ((0, 2), (2, 16))),
        "lengths": jax.vmap(lambda own: ragged(own, DOCS, STREAM, MAXLEN, 2))(jax.random.split(key_of[2], REPLICAS * MICRO)).reshape((REPLICAS, MICRO, DOCS)).astype(jnp.int32),
        "padding": touch_ends((jax.random.randint(key_of[3], (REPLICAS, MICRO, STREAM), 0, 8) < 7).astype(jnp.int32), jax.random.fold_in(key_of[3], 1), 0, 1),
        "attention_norm_gain": jnp.clip(1.0 + 0.1 * jax.random.normal(key_of[4], (MODEL_WIDTH,), jnp.float32), 0.5, 1.5).astype(jnp.bfloat16),
        "joint_projection_weight": gaussian(key_of[5], (MODEL_WIDTH, JOINT_COLUMNS), MODEL_WIDTH ** -0.5, 0.125, ((0, 16),)),
        "adapter_down_factors": gaussian(key_of[6], (MODEL_WIDTH, 3 * ADAPTER_RANK), MODEL_WIDTH ** -0.5, 0.125, ((0, 16),)),
        "adapter_up_factors": gaussian(key_of[7], (ADAPTER_RANK, JOINT_COLUMNS), 0.1, 0.59765625, ((1, 16),)),
        "output_weight": gaussian(key_of[8], (MODEL_WIDTH, MODEL_WIDTH), (MODEL_WIDTH // 32) ** -0.5, 0.75, ((0, 16),)),
        "adapter_output_down": gaussian(key_of[9], (MODEL_WIDTH, ADAPTER_RANK), (MODEL_WIDTH // 32) ** -0.5, 0.75, ((0, 16),)),
        "adapter_output_upper": gaussian(key_of[10], (ADAPTER_RANK, MODEL_WIDTH), 0.3, 1.796875, ((1, 16),)),
        "feature_query_map": gaussian(key_of[11], (HEADS * HEAD_DIM, HEAD_DIM), HEAD_DIM ** -0.5, 0.75, ((0, 16),)),
        "feature_key_map": gaussian(key_of[12], (KV_HEADS * HEAD_DIM, HEAD_DIM), HEAD_DIM ** -0.5, 0.75, ((0, 16),)),
        "feedforward_norm_gain": jnp.clip(1.0 + 0.1 * jax.random.normal(key_of[13], (MODEL_WIDTH,), jnp.float32), 0.5, 1.5).astype(jnp.bfloat16),
        "gate_up_weight": gaussian(key_of[14], (MODEL_WIDTH, 2 * FF), MODEL_WIDTH ** -0.5, 0.125, ((0, 16),)),
        "down_weight": gaussian(key_of[15], (FF, MODEL_WIDTH), FF ** -0.5, 0.0625, ((0, 16),)),
    }


@jax.custom_vjp
def low(v):
    return lax.optimization_barrier(v.astype(jnp.bfloat16)).astype(jnp.float32)

@jax.custom_vjp
def lowrank_backward(v):
    return v

def low_keep(v):
    return (low(v), None)

def low_pass(kept, grad):
    return (grad,)

def back_keep(v):
    return (v, None)

def back_low(kept, grad):
    return (low(grad),)
low.defvjp(low_keep, low_pass)
lowrank_backward.defvjp(back_keep, back_low)
HIGHEST = lax.Precision.HIGHEST
NORM_EPS = 1e-05
ADAPTER_SCALE = 2.0
ROPE_BASE = 500000.0
block_rows = 512

def matrix_product(left, right):
    return jnp.dot(left, right, precision=HIGHEST)

def rms_scale(values, gain):
    factor = lax.rsqrt(lax.optimization_barrier(jnp.mean(values * values, axis=-1, keepdims=True)) + NORM_EPS)
    return values * factor * gain

def rotate(values, doc_place, head_count, sign_factor):
    half_dim = HEAD_DIM // 2
    frequency = ROPE_BASE ** (-(jnp.arange(half_dim, dtype=jnp.float32) * 2.0) / HEAD_DIM)
    angles = doc_place.astype(jnp.float32)[:, None] * frequency[None, :]
    cosine = jnp.cos(angles)[:, None, :]
    sine_part = sign_factor * jnp.sin(angles)[:, None, :]
    shaped = values.reshape(values.shape[0], head_count, HEAD_DIM)
    first_half = shaped[..., :half_dim]
    second = shaped[..., half_dim:]
    turned = jnp.concatenate([first_half * cosine - second * sine_part, second * cosine + first_half * sine_part], axis=-1)
    return turned.reshape(values.shape[0], head_count * HEAD_DIM)

def feature_map(values, weight, head_count):
    shaped = values.reshape(values.shape[0], head_count, HEAD_DIM)
    table = weight.reshape(head_count, HEAD_DIM, HEAD_DIM)
    mixed = jnp.einsum('rhi,hij->rhj', shaped, table, precision=HIGHEST)
    return jnp.concatenate([jax.nn.softmax(mixed, axis=-1), jax.nn.softmax(-mixed, axis=-1)], axis=-1)

def attend(queries, keys_ext, values_ext, seg_query, seg_ext, live_query, live_ext, state_sum, state_norm, state_tag, feature_query_map, feature_key_map):
    row_count = queries.shape[0]
    extent = keys_ext.shape[0]
    window = extent - row_count
    groups = HEADS // KV_HEADS
    query_heads = queries.reshape(row_count, KV_HEADS, groups, HEAD_DIM)
    key_heads = keys_ext.reshape(extent, KV_HEADS, HEAD_DIM)
    value_heads = values_ext.reshape(extent, KV_HEADS, HEAD_DIM)
    scores = jnp.einsum('rkgd,jkd->kgrj', query_heads, key_heads, precision=HIGHEST) / math.sqrt(HEAD_DIM)
    offset = jnp.arange(row_count)[:, None] + window - jnp.arange(extent)[None, :]
    same_doc = seg_query[:, None] == seg_ext[None, :]
    live_key = live_ext[None, :] > 0
    in_window = (offset >= 0) & (offset < window) & same_doc & (live_key | (offset == 0))
    in_linear = (offset >= window) & same_doc & live_key
    row_top = lax.optimization_barrier(jnp.max(jnp.where(in_window, scores, -1e+30), axis=-1, keepdims=True))
    window_exp = jnp.exp(jnp.where(in_window, scores - row_top, -1e+30))
    phi_query = feature_map(queries, feature_query_map, HEADS).reshape(row_count, KV_HEADS, groups, 2 * HEAD_DIM)
    phi_key = feature_map(keys_ext, feature_key_map, KV_HEADS)
    linear = jnp.einsum('rkgf,jkf->kgrj', phi_query, phi_key, precision=HIGHEST) * in_linear
    far_scale = jnp.exp(-row_top)
    weights = window_exp + far_scale * linear
    numerator = jnp.einsum('kgrj,jkd->kgrd', weights, value_heads, precision=HIGHEST)
    denominator = lax.optimization_barrier(jnp.sum(weights, axis=-1))
    use_state = (seg_query == state_tag).astype(jnp.float32)
    carried = jnp.einsum('rkgf,kfd->kgrd', phi_query, state_sum, precision=HIGHEST)
    carried_norm = jnp.einsum('rkgf,kf->kgr', phi_query, state_norm, precision=HIGHEST)
    numerator = numerator + far_scale * use_state[:, None] * carried
    denominator = denominator + far_scale[..., 0] * use_state * carried_norm
    result = numerator / denominator[..., None] * live_query[:, None]
    return jnp.transpose(result, (2, 0, 1, 3)).reshape(row_count, HEADS * HEAD_DIM)

def state_terms(key_rows, value_rows, seg_rows, live_rows, state_tag, feature_key_map):
    phi_key = feature_map(key_rows, feature_key_map, KV_HEADS)
    chosen = ((seg_rows == state_tag) & (live_rows > 0)).astype(jnp.float32)
    phi_key = phi_key * chosen[:, None, None]
    value_heads = value_rows.reshape(value_rows.shape[0], KV_HEADS, HEAD_DIM)
    return (jnp.einsum('jkf,jkd->kfd', phi_key, value_heads, precision=HIGHEST), lax.optimization_barrier(jnp.sum(phi_key, axis=0)))

def stream_forward(activ, doc_lengths, live_mask, parameter_tree):
    gain_attn, merged_joint_weight, full_down, merged_up_factor, merged_output_weight, out_down, output_up_factor, feature_query_map, feature_key_map, gain_ffn, gate_up_w, down_w = parameter_tree
    key_value_width = KV_HEADS * HEAD_DIM
    places = jnp.arange(STREAM, dtype=jnp.int32)
    doc_ends = jnp.cumsum(doc_lengths).astype(jnp.int32)
    finished = doc_ends[None, :] <= places[:, None]
    segment = lax.optimization_barrier(jnp.sum(finished.astype(jnp.int32), axis=1)).astype(jnp.int32)
    doc_place = places - lax.optimization_barrier(jnp.sum(jnp.where(finished, doc_lengths[None, :], 0), axis=1)).astype(jnp.int32)
    normalized_input = low(rms_scale(activ, gain_attn))
    adapter_delta = lowrank_backward(low(matrix_product(normalized_input, full_down)))
    adapter_products = jnp.concatenate([matrix_product(adapter_delta[:, :ADAPTER_RANK], merged_up_factor[:, :MODEL_WIDTH]), matrix_product(adapter_delta[:, ADAPTER_RANK:2 * ADAPTER_RANK], merged_up_factor[:, MODEL_WIDTH:MODEL_WIDTH + key_value_width]), matrix_product(adapter_delta[:, 2 * ADAPTER_RANK:], merged_up_factor[:, MODEL_WIDTH + key_value_width:])], axis=1)
    projected_rows = lowrank_backward(matrix_product(normalized_input, merged_joint_weight) + ADAPTER_SCALE * adapter_products)
    queries = low(rotate(projected_rows[:, :MODEL_WIDTH], doc_place, HEADS, 1.0))
    keys = low(rotate(projected_rows[:, MODEL_WIDTH:MODEL_WIDTH + key_value_width], doc_place, KV_HEADS, 1.0))
    values = low(projected_rows[:, MODEL_WIDTH + key_value_width:])
    pad_keys = jnp.concatenate([jnp.zeros((WINDOW, key_value_width), activ.dtype), keys], axis=0)
    pad_values = jnp.concatenate([jnp.zeros((WINDOW, key_value_width), activ.dtype), values], axis=0)
    pad_seg = jnp.concatenate([jnp.full((WINDOW,), -1, jnp.int32), segment], axis=0)
    pad_live = jnp.concatenate([jnp.zeros((WINDOW,), activ.dtype), live_mask], axis=0)

    def one_block(carry_state, block_index):
        state_sum, state_norm, state_tag = carry_state
        block_start = (block_index * block_rows).astype(jnp.int32)
        query_rows = lax.dynamic_slice_in_dim(queries, block_start, block_rows, 0)
        seg_query = lax.dynamic_slice_in_dim(segment, block_start, block_rows, 0)
        live_query = lax.dynamic_slice_in_dim(live_mask, block_start, block_rows, 0)
        keys_ext = lax.dynamic_slice_in_dim(pad_keys, block_start, block_rows + WINDOW, 0)
        values_ext = lax.dynamic_slice_in_dim(pad_values, block_start, block_rows + WINDOW, 0)
        seg_ext = lax.dynamic_slice_in_dim(pad_seg, block_start, block_rows + WINDOW, 0)
        live_ext = lax.dynamic_slice_in_dim(pad_live, block_start, block_rows + WINDOW, 0)
        block_out = attend(query_rows, keys_ext, values_ext, seg_query, seg_ext, live_query, live_ext, state_sum, state_norm, state_tag, feature_query_map, feature_key_map)
        tag_new = seg_ext[block_rows - 1]
        add_sum, add_norm = state_terms(keys_ext[:block_rows], values_ext[:block_rows], seg_ext[:block_rows], live_ext[:block_rows], tag_new, feature_key_map)
        keep_old = (state_tag == tag_new.astype(state_tag.dtype)).astype(activ.dtype)
        return ((state_sum * keep_old + add_sum, state_norm * keep_old + add_norm, tag_new.astype(state_tag.dtype)), block_out)
    start_state = (jnp.zeros((KV_HEADS, 2 * HEAD_DIM, HEAD_DIM), activ.dtype), jnp.zeros((KV_HEADS, 2 * HEAD_DIM), activ.dtype), jnp.array(-1.0, activ.dtype))
    final_state, block_outs = lax.scan(jax.checkpoint(one_block), start_state, jnp.arange(STREAM // block_rows, dtype=jnp.int32))
    attn_heads = block_outs.reshape(STREAM, MODEL_WIDTH)
    attention_lowrank = low(attn_heads)
    adapter_output_delta = lowrank_backward(low(matrix_product(attention_lowrank, out_down)))
    branch_value = lowrank_backward(matrix_product(attention_lowrank, merged_output_weight) + ADAPTER_SCALE * matrix_product(adapter_output_delta, output_up_factor))
    hidden = activ + branch_value
    normed_two = low(rms_scale(hidden, gain_ffn))
    gate_up = lowrank_backward(matrix_product(normed_two, gate_up_w))
    acted = low(jax.nn.silu(gate_up[:, :FF]) * gate_up[:, FF:])
    ffn_out = lowrank_backward(matrix_product(acted, down_w))
    return hidden + ffn_out

def reference(inputs, cotangent, lengths, padding, attention_norm_gain, joint_projection_weight, adapter_down_factors, adapter_up_factors, output_weight, adapter_output_down, adapter_output_upper, feature_query_map, feature_key_map, feedforward_norm_gain, gate_up_weight, down_weight):
    parameter_tree = (attention_norm_gain.astype(jnp.float32), joint_projection_weight.astype(jnp.float32), adapter_down_factors.astype(jnp.float32), adapter_up_factors.astype(jnp.float32), output_weight.astype(jnp.float32), adapter_output_down.astype(jnp.float32), adapter_output_upper.astype(jnp.float32), feature_query_map.astype(jnp.float32), feature_key_map.astype(jnp.float32), feedforward_norm_gain.astype(jnp.float32), gate_up_weight.astype(jnp.float32), down_weight.astype(jnp.float32))
    activations = inputs.astype(jnp.float32)

    def forward(all_inputs, all_params):
        pieces = []
        for replica_index in range(REPLICAS):
            for micro_index in range(MICRO):
                pieces.append(stream_forward(all_inputs[replica_index, micro_index], lengths[replica_index, micro_index], padding[replica_index, micro_index].astype(jnp.float32), all_params))
        return jnp.stack(pieces).reshape(all_inputs.shape)
    result, pullback = jax.vjp(forward, activations, parameter_tree)
    grad_x, grad_params = pullback(cotangent.astype(jnp.float32))
    return (result.astype(jnp.bfloat16), grad_x.astype(jnp.bfloat16), grad_params[0], grad_params[1], grad_params[2], grad_params[3], grad_params[4], grad_params[5], grad_params[6], grad_params[7], grad_params[8], grad_params[9], grad_params[10], grad_params[11])
```

```python
import jax
import jax.numpy as jnp
from jax import lax
from jax.experimental import pallas as pl
from jax.experimental.pallas import tpu as pltpu
from jax.sharding import Mesh, PartitionSpec as P

D = 2048
HEADS = 32
KV = 8
HD = 64
FF = 8192
RANK = 8
WINDOW = 64
MAXLEN = 1024
KVW = KV * HD
COLS = D + 2 * KVW
GROUP = HEADS // KV
NORM_EPS = 1e-05
SCALE = 2.0
ROPE_BASE = 500000.0
SROWS = 80
PACK = 256
bf16 = jnp.bfloat16
f32 = jnp.float32


def mm(a, b):
    return jnp.dot(a, b, preferred_element_type=f32)


def mm_t(a, b):
    return lax.dot_general(a, b, (((1,), (1,)), ((), ())), preferred_element_type=f32)


def t_mm(a, b):
    return lax.dot_general(a, b, (((0,), (0,)), ((), ())), preferred_element_type=f32)


def swap(a, axis):
    return lax.ppermute(a, axis, [(0, 1), (1, 0)])


def line_gather(block):
    nz, z = lax.axis_size("z"), lax.axis_index("z")
    rights, lefts = [block], [block]
    for k in range(1, nz):
        rights.append(
            lax.ppermute(rights[-1], "z", [(i, i + 1) for i in range(k - 1, nz - 1)])
        )
        lefts.append(lax.ppermute(lefts[-1], "z", [(i, i - 1) for i in range(1, nz - k + 1)]))
    return [block] + [jnp.where(z >= k, rights[k], lefts[nz - k]) for k in range(1, nz)]


def line_scatter(blocks):
    nz = lax.axis_size("z")
    right = left = None
    for s in range(1, nz):
        up, down = blocks[s].astype(f32), blocks[nz - s].astype(f32)
        if right is not None:
            up, down = up + right.astype(f32), down + left.astype(f32)
        right = lax.ppermute(
            up.astype(bf16), "z", [(i, i + 1) for i in range(min(s, nz - 1))]
        )
        left = lax.ppermute(
            down.astype(bf16), "z", [(i, i - 1) for i in range(max(nz - s, 1), nz)]
        )
    return blocks[0].astype(f32) + right.astype(f32) + left.astype(f32)


def gather_rows(block):
    nz = lax.axis_size("z")
    z, x, c = lax.axis_index("z"), lax.axis_index("x"), lax.axis_index("c")
    rows, cols = block.shape
    half = jnp.zeros((nz, 2, rows, cols), block.dtype)
    for k, part in enumerate(line_gather(block)):
        at = lax.rem(z - k + nz, nz)
        half = lax.dynamic_update_slice(half, part[None, None], (at, x, 0, 0))
        half = lax.dynamic_update_slice(half, swap(part, "x")[None, None], (at, 1 - x, 0, 0))
    other = swap(half, "c")
    first = jnp.where(c == 0, half, other)
    second = jnp.where(c == 0, other, half)
    return jnp.stack([first, second], axis=2).reshape(nz * 4 * rows, cols)


def scatter_rows(total):
    nz = lax.axis_size("z")
    z, x, c = lax.axis_index("z"), lax.axis_index("x"), lax.axis_index("c")
    rows, cols = total.shape
    r = rows // (4 * nz)
    t = total.reshape(nz, 2, 2, r, cols)
    pick = lambda a, i, dim: lax.dynamic_index_in_dim(a, i, dim, False)
    mine, theirs = pick(t, c, 2), pick(t, 1 - c, 2)
    t = (mine.astype(f32) + swap(theirs, "c").astype(f32)).astype(bf16)
    mine, theirs = pick(t, x, 1), pick(t, 1 - x, 1)
    t = (mine.astype(f32) + swap(theirs, "x").astype(f32)).astype(bf16)
    return line_scatter([pick(t, lax.rem(z - k + nz, nz), 0) for k in range(nz)])


def both_replicas(part):
    low = part.astype(bf16)
    return low.astype(f32) + swap(low, "r").astype(f32)


def gather_tokens(block):
    out = []
    for part in line_gather(block):
        out += [part, swap(part, "c")]
    return jnp.concatenate(out, axis=0)


def scatter_tokens(total):
    nz = lax.axis_size("z")
    t = total.reshape(nz, 2, total.shape[0] // (2 * nz), total.shape[1])
    t = (t[:, 0].astype(f32) + swap(t[:, 1], "c").astype(f32)).astype(bf16)
    return line_scatter([t[k] for k in range(nz)])


def gather_gate_up(weight):
    nz = lax.axis_size("z")
    z, x, c = lax.axis_index("z"), lax.axis_index("x"), lax.axis_index("c")
    rows = weight.shape[0]
    loc = FF // (4 * nz)
    out = jnp.zeros((nz, 2, 2, rows, 4 * loc), weight.dtype)
    for k in range(nz):
        to = lax.rem(z + k, nz)
        part = jnp.concatenate(
            [
                lax.dynamic_slice(weight, (0, g * FF + to * 4 * loc), (rows, 4 * loc))
                for g in range(2)
            ],
            axis=1,
        )
        if k:
            part = lax.ppermute(part, "z", [(i, (i + k) % nz) for i in range(nz)])
        at = lax.rem(z - k + nz, nz)

        def columns(core):
            return jnp.concatenate(
                [
                    lax.dynamic_slice(part, (0, j * 2 * loc + core * loc), (rows, loc))
                    for j in range(4)
                ],
                axis=1,
            )

        mine = columns(c)
        theirs = swap(columns(1 - c), "c")
        pair = jnp.stack([jnp.where(c == 0, mine, theirs), jnp.where(c == 0, theirs, mine)])
        out = lax.dynamic_update_slice(out, pair[None, None], (at, x, 0, 0, 0))
        out = lax.dynamic_update_slice(
            out, swap(pair, "x")[None, None], (at, 1 - x, 0, 0, 0)
        )
    return out.reshape(nz * 4 * rows, 4 * loc)


def scatter_gate_up(total):
    nz = lax.axis_size("z")
    z, x, c = lax.axis_index("z"), lax.axis_index("x"), lax.axis_index("c")
    rows, loc = total.shape[0] // (4 * nz), total.shape[1] // 4
    pick = lambda a, i, dim: lax.dynamic_index_in_dim(a, i, dim, False)
    t = total.reshape(nz, 2, 2, rows, 4 * loc)
    t = (
        pick(t, x, 1).astype(f32) + swap(pick(t, 1 - x, 1), "x").astype(f32)
    ).astype(bf16)
    mine, theirs = pick(t, c, 1), swap(pick(t, 1 - c, 1), "c")
    first, second = jnp.where(c == 0, mine, theirs), jnp.where(c == 0, theirs, mine)
    pieces = []
    for j in range(4):
        pieces += [first[:, :, j * loc : (j + 1) * loc], second[:, :, j * loc : (j + 1) * loc]]
    t = jnp.concatenate(pieces, axis=2)
    out = jnp.zeros((rows, 2 * FF), bf16)
    for k in range(nz):
        part = pick(t, lax.rem(z + k, nz), 0)
        if k:
            part = lax.ppermute(part, "z", [(i, (i + k) % nz) for i in range(nz)])
        at = lax.rem(z - k + nz, nz)
        for g in range(2):
            out = lax.dynamic_update_slice(
                out, part[:, g * 4 * loc : (g + 1) * 4 * loc], (0, g * FF + at * 4 * loc)
            )
    return out


def turn(v, cosine, sine):
    lane = lax.broadcasted_iota(jnp.int32, v.shape, 1)
    low_half = (lane & 63) < 32
    other = jnp.where(low_half, pltpu.roll(v, 96, 1), pltpu.roll(v, 32, 1))
    return v * cosine + other * sine


def rope_kernel(v_ref, cos_ref, sin_ref, o_ref, *, turned):
    j = pl.program_id(0)

    @pl.when(j < turned)
    def _():
        for s in range(4):
            at = slice(s * 128, (s + 1) * 128)
            o_ref[:, at] = turn(v_ref[:, at], cos_ref[...], sin_ref[...]).astype(bf16)

    @pl.when(j >= turned)
    def _():
        o_ref[...] = v_ref[...].astype(bf16)


def rope(values, cosine, sine, turned):
    rows, cols = values.shape
    full = pl.BlockSpec((rows, 128), lambda j: (0, 0))
    return pl.pallas_call(
        lambda *refs: rope_kernel(*refs, turned=turned),
        out_shape=jax.ShapeDtypeStruct((rows, cols), bf16),
        grid=(cols // 512,),
        in_specs=[pl.BlockSpec((rows, 512), lambda j: (0, j)), full, full],
        out_specs=pl.BlockSpec((rows, 512), lambda j: (0, j)),
        cost_estimate=pl.CostEstimate(
            flops=6 * rows * cols, bytes_accessed=6 * rows * cols, transcendentals=0
        ),
        name="rope",
    )(values, cosine, sine)


def halves(shape):
    return lax.broadcasted_iota(jnp.int32, shape, 1) < 64


def feature(z2):
    first = halves(z2.shape)
    top = jnp.max(jnp.where(first, z2, -jnp.inf), axis=1, keepdims=True)
    low = jnp.max(jnp.where(first, -jnp.inf, z2), axis=1, keepdims=True)
    e = jnp.exp(z2 - jnp.where(first, top, low))
    s1 = jnp.sum(jnp.where(first, e, 0.0), axis=1, keepdims=True)
    s2 = jnp.sum(jnp.where(first, 0.0, e), axis=1, keepdims=True)
    return e * jnp.where(first, 1.0 / s1, 1.0 / s2)


def feature_grad(phi, dphi):
    first = halves(phi.shape)
    t = phi * dphi
    s1 = jnp.sum(jnp.where(first, t, 0.0), axis=1, keepdims=True)
    s2 = jnp.sum(jnp.where(first, 0.0, t), axis=1, keepdims=True)
    return t - phi * jnp.where(first, s1, s2)


def with_one(v):
    wide = jnp.concatenate([v, jnp.zeros_like(v)], axis=1)
    lane = lax.broadcasted_iota(jnp.int32, wide.shape, 1)
    return jnp.where(lane == 64, jnp.ones_like(wide), wide)


def tile(a):
    return jnp.concatenate([a] * GROUP, axis=0)


def attention_masks(row_ref, col_ref):
    rows, extent = row_ref.shape[0], col_ref.shape[1]
    offset = (
        lax.broadcasted_iota(jnp.int32, (rows, extent), 0)
        + WINDOW
        - lax.broadcasted_iota(jnp.int32, (rows, extent), 1)
    )
    same = row_ref[:, 0:1] == col_ref[0:1, :]
    live = col_ref[1:2, :] > 0
    window = (offset >= 0) & (offset < WINDOW) & same & (live | (offset == 0))
    far = (offset >= WINDOW) & same & live
    return tile(window.astype(f32)) > 0, tile(far.astype(f32)) > 0


def head_forward(q_ref, k, v, st, wq_ref, wk, hh, window, far, use):
    rows = q_ref.shape[0]
    qs = [q_ref[:, (hh * GROUP + i) * HD : (hh * GROUP + i + 1) * HD] for i in range(GROUP)]
    q4 = jnp.concatenate(qs, axis=0)
    s = mm_t(q4, k) * 0.125
    s = jnp.where(window, s, -1e30)
    top = jnp.max(s, axis=1, keepdims=True)
    p = jnp.exp(s - top)
    e = jnp.exp(-top)
    phi = feature(
        jnp.concatenate([mm(qs[i], wq_ref[hh * GROUP + i]) for i in range(GROUP)], axis=0)
    )
    phik = feature(mm(k, wk))
    phi_b, phik_b = phi.astype(bf16), phik.astype(bf16)
    a_b = (p + e * jnp.where(far, mm_t(phi_b, phik_b), 0.0)).astype(bf16)
    va = with_one(v)
    stp = jnp.concatenate([st, jnp.zeros((128 - SROWS, 128), bf16)], axis=0)
    eu = e * use
    nd = mm(a_b, va) + eu * mm_t(phi_b, stp)
    return qs, q4, p, e, eu, phi, phi_b, phik, phik_b, a_b, va, stp, nd


def attend_kernel(q_ref, k_ref, v_ref, st_ref, wq_ref, wk_ref, row_ref, col_ref, o_ref):
    rows = q_ref.shape[0]
    window, far = attention_masks(row_ref, col_ref)
    use, live = tile(row_ref[:, 1:2]), tile(row_ref[:, 2:3])
    for hh in range(2):
        at = slice(hh * HD, (hh + 1) * HD)
        nd = head_forward(
            q_ref, k_ref[:, at], v_ref[:, at], st_ref[hh], wq_ref, wk_ref[hh], hh, window, far, use
        )[-1]
        out = (nd[:, :HD] * (live / nd[:, HD : HD + 1])).astype(bf16)
        for i in range(GROUP):
            j = hh * GROUP + i
            o_ref[:, j * HD : (j + 1) * HD] = out[i * rows : (i + 1) * rows]


def attend_back_kernel(
    q_ref, k_ref, v_ref, st_ref, wq_ref, wk_ref, row_ref, col_ref, do_ref, cos_ref, sin_ref,
    dq_ref, dk_ref, dv_ref, dst_ref, dwq_ref, dwk_ref, scr_ref,
):
    rows = q_ref.shape[0]
    window, far = attention_masks(row_ref, col_ref)
    use, live = tile(row_ref[:, 1:2]), tile(row_ref[:, 2:3])
    for hh in range(2):
        at = slice(hh * HD, (hh + 1) * HD)
        k = k_ref[:, at]
        qs, q4, p, e, eu, phi, phi_b, phik, phik_b, a_b, va, stp, nd = head_forward(
            q_ref, k, v_ref[:, at], st_ref[hh], wq_ref, wk_ref[hh], hh, window, far, use
        )
        do4 = jnp.concatenate(
            [do_ref[:, (hh * GROUP + i) * HD : (hh * GROUP + i + 1) * HD] for i in range(GROUP)],
            axis=0,
        )
        inv = 1.0 / nd[:, HD : HD + 1]
        dnum = do4 * (live * inv)
        dden = -jnp.sum(dnum * nd[:, :HD], axis=1, keepdims=True) * inv
        dn = jnp.concatenate([dnum, jnp.zeros_like(dnum)], axis=1)
        lane = lax.broadcasted_iota(jnp.int32, dn.shape, 1)
        dn = jnp.where(lane == HD, dden, dn)
        dn_b = dn.astype(bf16)
        en_b = (eu * dn).astype(bf16)
        da = mm_t(dn_b, va)
        ds_b = (da * p * 0.125).astype(bf16)
        dl_b = jnp.where(far, e * da, 0.0).astype(bf16)
        dv_ref[:, at] = t_mm(a_b, dn_b)[:, :HD]
        dst_ref[hh] = t_mm(en_b, phi_b)[:SROWS].astype(bf16)
        dz = feature_grad(phi, mm(dl_b, phik_b) + mm(en_b, stp)).astype(bf16)
        dzk = feature_grad(phik, t_mm(dl_b, phi_b)).astype(bf16)
        dq4 = mm(ds_b, k)
        dk_ref[:, at] = t_mm(ds_b, q4) + mm_t(dzk, wk_ref[hh])
        dwk_ref[hh] = t_mm(k, dzk)
        for i in range(GROUP):
            j = hh * GROUP + i
            dzi = dz[i * rows : (i + 1) * rows]
            scr_ref[:, j * HD : (j + 1) * HD] = dq4[i * rows : (i + 1) * rows] + mm_t(
                dzi, wq_ref[j]
            )
            dwq_ref[j] = t_mm(qs[i], dzi)
    for s in range(4):
        at = slice(s * 128, (s + 1) * 128)
        dq_ref[:, at] = turn(scr_ref[:, at], cos_ref[...], -sin_ref[...]).astype(bf16)


def state_kernel(k_ref, v_ref, wk_ref, row_ref, add_ref):
    rows = row_ref.shape[0]
    chosen = row_ref[:, 3:4]
    for hh in range(2):
        at = slice(hh * HD, (hh + 1) * HD)
        phik = (feature(mm(k_ref[:rows, at], wk_ref[hh])) * chosen).astype(bf16)
        add_ref[hh] = t_mm(with_one(v_ref[:rows, at]), phik)[:SROWS].astype(bf16)


def state_back_kernel(
    k_ref, v_ref, wk_ref, row_ref, dadd_ref, dk_in, dv_in, dk_ref, dv_ref, dwk_ref
):
    rows = row_ref.shape[0]
    chosen = row_ref[:, 3:4]
    dk_ref[rows:] = dk_in[rows:]
    dv_ref[rows:] = dv_in[rows:]
    for hh in range(2):
        at = slice(hh * HD, (hh + 1) * HD)
        k = k_ref[:rows, at]
        phik = feature(mm(k, wk_ref[hh]))
        dadd = jnp.concatenate([dadd_ref[hh], jnp.zeros((128 - SROWS, 128), bf16)], axis=0)
        dphi = mm(with_one(v_ref[:rows, at]), dadd) * chosen
        dz = feature_grad(phik, dphi).astype(bf16)
        dk_ref[:rows, at] = dk_in[:rows, at] + mm_t(dz, wk_ref[hh])
        dv_ref[:rows, at] = dv_in[:rows, at] + mm_t((phik * chosen).astype(bf16), dadd)[:, :HD]
        dwk_ref[hh] = t_mm(k, dz)


def params():
    return pltpu.CompilerParams(vmem_limit_bytes=48 << 20)


def specs(rows, extent):
    return dict(
        q=pl.BlockSpec((rows, 512), lambda j: (0, j)),
        k=pl.BlockSpec((extent, 128), lambda j: (0, j)),
        v=pl.BlockSpec((extent, 128), lambda j: (0, 4 + j)),
        st=pl.BlockSpec((2, SROWS, 128), lambda j: (j, 0, 0)),
        wq=pl.BlockSpec((8, HD, 128), lambda j: (j, 0, 0)),
        wk=pl.BlockSpec((2, HD, 128), lambda j: (j, 0, 0)),
        row=pl.BlockSpec((rows, 128), lambda j: (0, 0)),
        col=pl.BlockSpec((8, extent), lambda j: (0, 0)),
    )


def attend(qkv, kv_ext, st, wq2, wk2, rowinfo, colinfo):
    rows, extent = qkv.shape[0], kv_ext.shape[0]
    s = specs(rows, extent)
    return pl.pallas_call(
        attend_kernel,
        out_shape=jax.ShapeDtypeStruct((rows, D), bf16),
        grid=(4,),
        in_specs=[s[n] for n in ("q", "k", "v", "st", "wq", "wk", "row", "col")],
        out_specs=s["q"],
        compiler_params=params(),
        cost_estimate=pl.CostEstimate(
            flops=HEADS * rows * extent * 1200, bytes_accessed=4 << 20, transcendentals=1 << 20
        ),
        name="attend",
    )(qkv, kv_ext, kv_ext, st, wq2, wk2, rowinfo, colinfo)


def attend_back(qkv, kv_ext, st, wq2, wk2, rowinfo, colinfo, d_attn, cosine, sine):
    rows, extent = qkv.shape[0], kv_ext.shape[0]
    s = specs(rows, extent)
    return pl.pallas_call(
        attend_back_kernel,
        out_shape=(
            jax.ShapeDtypeStruct((rows, D), bf16),
            jax.ShapeDtypeStruct((extent, KVW), f32),
            jax.ShapeDtypeStruct((extent, KVW), f32),
            jax.ShapeDtypeStruct((KV, SROWS, 128), bf16),
            jax.ShapeDtypeStruct((HEADS, HD, 128), f32),
            jax.ShapeDtypeStruct((KV, HD, 128), f32),
        ),
        grid=(4,),
        in_specs=[
            s[n] for n in ("q", "k", "v", "st", "wq", "wk", "row", "col", "q", "row", "row")
        ],
        out_specs=(s["q"], s["k"], s["k"], s["st"], s["wq"], s["wk"]),
        scratch_shapes=[pltpu.VMEM((rows, 512), f32)],
        compiler_params=params(),
        cost_estimate=pl.CostEstimate(
            flops=HEADS * rows * extent * 3200, bytes_accessed=8 << 20, transcendentals=1 << 20
        ),
        name="attend_back",
    )(qkv, kv_ext, kv_ext, st, wq2, wk2, rowinfo, colinfo, d_attn, cosine, sine)


def state_add(kv_ext, wk2, rowinfo):
    rows, extent = rowinfo.shape[0], kv_ext.shape[0]
    s = specs(rows, extent)
    return pl.pallas_call(
        state_kernel,
        out_shape=jax.ShapeDtypeStruct((KV, SROWS, 128), bf16),
        grid=(4,),
        in_specs=[s[n] for n in ("k", "v", "wk", "row")],
        out_specs=s["st"],
        cost_estimate=pl.CostEstimate(
            flops=KV * rows * 128 * 400, bytes_accessed=1 << 20, transcendentals=1 << 17
        ),
        name="state_add",
    )(kv_ext, kv_ext, wk2, rowinfo)


def state_back(kv_ext, wk2, rowinfo, dadd, dk, dv):
    rows, extent = rowinfo.shape[0], kv_ext.shape[0]
    s = specs(rows, extent)
    return pl.pallas_call(
        state_back_kernel,
        out_shape=(
            jax.ShapeDtypeStruct((extent, KVW), f32),
            jax.ShapeDtypeStruct((extent, KVW), f32),
            jax.ShapeDtypeStruct((KV, HD, 128), f32),
        ),
        grid=(4,),
        in_specs=[s[n] for n in ("k", "v", "wk", "row", "st", "k", "k")],
        out_specs=(s["k"], s["k"], s["wk"]),
        cost_estimate=pl.CostEstimate(
            flops=KV * rows * 128 * 800, bytes_accessed=3 << 20, transcendentals=1 << 17
        ),
        name="state_back",
    )(kv_ext, kv_ext, wk2, rowinfo, dadd, dk, dv)


def weigh(flag, a):
    return jnp.where(flag, a.astype(f32), 0.0)


def entering(add, tags, reach):
    nz = lax.axis_size("z")
    z, x, c = lax.axis_index("z"), lax.axis_index("x"), lax.axis_index("c")
    p = (z * 2 + x) * 2 + c
    tag = lambda i: lax.dynamic_index_in_dim(tags, jnp.clip(i, 0, 4 * nz - 1), 0, False)
    prev = tag(p - 1)
    chip = (z * 2 + x) * 2
    other = swap(add, "c")
    one = tag(chip) == tag(chip + 1)
    chip_sum = (weigh((c == 1) | one, add) + weigh((c == 0) | one, other)).astype(bf16)
    side = swap(chip_sum, "x")
    one = tag(z * 4 + 1) == tag(z * 4 + 3)
    layer = (weigh((x == 1) | one, chip_sum) + weigh((x == 0) | one, side)).astype(bf16)
    state = weigh(c == 1, other) + weigh((x == 1) & (tag(z * 4 + 1) == prev), side)
    for hop in range(1, min(reach, nz - 1) + 1):
        got = lax.ppermute(layer, "z", [(i, i + hop) for i in range(nz - hop)])
        state += weigh((z >= hop) & (tag((z - hop) * 4 + 3) == prev), got)
    return state.astype(bf16)


def leaving(dstate, tags, reach):
    nz = lax.axis_size("z")
    z, x, c = lax.axis_index("z"), lax.axis_index("x"), lax.axis_index("c")
    p = (z * 2 + x) * 2 + c
    tag = lambda i: lax.dynamic_index_in_dim(tags, jnp.clip(i, 0, 4 * nz - 1), 0, False)
    from_tag = lambda i: jnp.where(i > 0, tag(i - 1), -1)
    own = tag(p)
    chip = (z * 2 + x) * 2
    other = swap(dstate, "c")
    one = from_tag(chip) == from_tag(chip + 1)
    chip_sum = (weigh((c == 0) | one, dstate) + weigh((c == 1) | one, other)).astype(bf16)
    side = swap(chip_sum, "x")
    one = from_tag(z * 4) == from_tag(z * 4 + 2)
    layer = (weigh((x == 0) | one, chip_sum) + weigh((x == 1) | one, side)).astype(bf16)
    total = weigh(c == 0, other) + weigh((x == 0) & (from_tag(z * 4 + 2) == own), side)
    for hop in range(1, min(reach, nz - 1) + 1):
        got = lax.ppermute(layer, "z", [(i, i - hop) for i in range(hop, nz)])
        total += weigh((z + hop < nz) & (from_tag((z + hop) * 4) == own), got)
    return total.astype(bf16)


def per_device(
    inputs, cotangent, lengths, padding, gain_attn_own, wqkv_own, adown_own, aup_own, wout_own,
    odown_own, oup_own, featq_own, featk_own, gain_ffn_own, wgu_own, wd_own,
):
    nz = lax.axis_size("z")
    n = 4 * nz
    z, x, c = lax.axis_index("z"), lax.axis_index("x"), lax.axis_index("c")
    place_own = (z * 2 + x) * 2 + c
    micros, rows = inputs.shape[1], inputs.shape[2]
    reach = -(-MAXLEN // (4 * rows))
    chain = (("z", "x", "c"), [(i, i + 1) for i in range(n - 1)])
    unchain = (("z", "x", "c"), [(i, i - 1) for i in range(1, n)])
    r = D // n

    pack = jnp.concatenate(
        [
            gain_attn_own[:, None], adown_own, odown_own, oup_own.T, featq_own,
            gain_ffn_own[:, None], aup_own.reshape(r, 12), featk_own.reshape(r, 16),
        ],
        axis=1,
    )
    small = gather_rows(jnp.pad(pack, ((0, 0), (0, PACK - pack.shape[1]))))
    wqkv = gather_rows(wqkv_own)
    wout = gather_rows(wout_own)
    wgu = gather_gate_up(wgu_own)
    wd_other = swap(wd_own, "x")
    wd = jnp.concatenate(
        [jnp.where(x == 0, wd_own, wd_other), jnp.where(x == 0, wd_other, wd_own)], axis=0
    )
    gain_one = small[:, 0].astype(f32)[None]
    adown = small[:, 1:25]
    odown = small[:, 25:33]
    oup_t = small[:, 33:41]
    featq = small[:, 41:105].reshape(HEADS, HD, HD)
    gain_two = small[:, 105].astype(f32)[None]
    aup = small[:, 106:118].reshape(n, RANK, COLS // n).transpose(1, 0, 2).reshape(RANK, COLS)
    featk = small[:, 118:134].reshape(KV, HD, HD)
    wq2 = jnp.concatenate([featq, -featq], axis=2)
    wk2 = jnp.concatenate([featk, -featk], axis=2)
    column = jnp.arange(COLS)[None]
    owner = jnp.where(column < D, 0, jnp.where(column < D + KVW, 1, 2))
    aup_wide = jnp.concatenate(
        [jnp.where(owner == t, aup, jnp.zeros_like(aup)) for t in range(3)], axis=0
    )

    live_all = padding[0].astype(bf16)
    halo_live = lax.ppermute(live_all[:, rows - WINDOW :], *chain)

    saved = []
    for m in range(micros):
        act = inputs[0, m].astype(f32)
        doc_lengths = lengths[0, m]
        ends = jnp.cumsum(doc_lengths)
        seg_of = lambda t: jnp.sum((ends[None, :] <= t[:, None]).astype(jnp.int32), axis=1)
        places = place_own * rows - WINDOW + jnp.arange(rows + WINDOW, dtype=jnp.int32)
        done = ends[None, :] <= places[:, None]
        seg_ext = jnp.sum(done.astype(jnp.int32), axis=1)
        pos = (places - jnp.sum(jnp.where(done, doc_lengths[None, :], 0), axis=1))[WINDOW:]
        tags = seg_of(jnp.arange(n, dtype=jnp.int32) * rows + (rows - WINDOW - 1))
        live_ext = jnp.concatenate([halo_live[m], live_all[m]]).astype(f32)
        prev_tag = jnp.where(
            place_own > 0,
            lax.dynamic_index_in_dim(tags, jnp.maximum(place_own - 1, 0), 0, False),
            -1,
        )
        own_tag = lax.dynamic_index_in_dim(tags, place_own, 0, False)
        seg_own = seg_ext[WINDOW:]
        info = jnp.stack(
            [
                seg_own.astype(f32),
                (seg_own == prev_tag).astype(f32),
                live_ext[WINDOW:],
                ((seg_ext[:rows] == own_tag) & (live_ext[:rows] > 0)).astype(f32),
            ],
            axis=1,
        )
        rowinfo = jnp.pad(info, ((0, 0), (0, 124)))
        colinfo = jnp.pad(jnp.stack([seg_ext.astype(f32), live_ext]), ((0, 6), (0, 0)))
        lane = jnp.arange(128)
        frequency = ROPE_BASE ** (-((lane % 32).astype(f32) * 2.0) / HD)
        angles = pos.astype(f32)[:, None] * frequency[None, :]
        cosine = jnp.cos(angles)
        sine = jnp.where((lane % 64 < 32)[None], -1.0, 1.0) * jnp.sin(angles)

        inv_one = lax.rsqrt(jnp.mean(act * act, axis=-1, keepdims=True) + NORM_EPS)
        n1 = (act * inv_one * gain_one).astype(bf16)
        adapt = mm(n1, adown).astype(bf16)
        projected = mm(n1, wqkv) + SCALE * mm(adapt, aup_wide)
        qkv = rope(projected, cosine, sine, 5)
        halo = lax.ppermute(qkv[rows - WINDOW :, D:], *chain)
        kv_ext = jnp.concatenate([halo, qkv[:, D:]], axis=0)
        state = entering(state_add(kv_ext, wk2, rowinfo), tags, reach)
        attn = attend(qkv, kv_ext, state, wq2, wk2, rowinfo, colinfo)
        adapt_out = mm(attn, odown).astype(bf16)
        hidden = act + (mm(attn, wout) + SCALE * mm_t(adapt_out, oup_t))
        inv_two = lax.rsqrt(jnp.mean(hidden * hidden, axis=-1, keepdims=True) + NORM_EPS)
        n2 = (hidden * inv_two * gain_two).astype(bf16)
        saved.append(
            dict(
                act=act, tags=tags, rowinfo=rowinfo, colinfo=colinfo, cosine=cosine, sine=sine,
                inv_one=inv_one, n1=n1, adapt=adapt, qkv=qkv, kv_ext=kv_ext, state=state,
                attn=attn, adapt_out=adapt_out, hidden=hidden, inv_two=inv_two, n2=n2,
            )
        )

    half = 2 * FF // (4 * nz)
    ffn = []
    for m in range(micros):
        n2_all = gather_tokens(saved[m]["n2"])
        df_all = gather_tokens(cotangent[0, m])
        gate_up = mm(n2_all, wgu)
        gate, up = gate_up[:, :half], gate_up[:, half:]
        sig = jax.nn.sigmoid(gate)
        swish = gate * sig
        acted = (swish * up).astype(bf16)
        d_act = mm_t(df_all, wd)
        d_gu = jnp.concatenate(
            [d_act * up * (sig * (1.0 + gate * (1.0 - sig))), d_act * swish], axis=1
        ).astype(bf16)
        ffn.append(
            dict(
                n2=n2_all, df=df_all, acted=acted, d_gu=d_gu,
                d_n2=scatter_tokens(mm_t(d_gu, wgu).astype(bf16)),
                out=scatter_tokens(mm(acted, wd).astype(bf16)),
            )
        )
    cat = lambda items, key: jnp.concatenate([i[key] for i in items], axis=0)
    outputs = [(saved[m]["hidden"] + ffn[m]["out"]).astype(bf16) for m in range(micros)]
    g_wd = t_mm(cat(ffn, "acted"), cat(ffn, "df")).astype(bf16)
    loc = g_wd.shape[0] // 2
    g_wd_own = (
        lax.dynamic_slice(g_wd, (x * loc, 0), (loc, D)).astype(f32)
        + swap(lax.dynamic_slice(g_wd, ((1 - x) * loc, 0), (loc, D)), "x").astype(f32)
    )
    g_wd_own = both_replicas(g_wd_own)
    g_wgu = t_mm(cat(ffn, "n2"), cat(ffn, "d_gu")).astype(bf16)
    g_wgu_own = both_replicas(scatter_gate_up(g_wgu))

    back = []
    for m in range(micros):
        s, d_n2 = saved[m], ffn[m]["d_n2"]
        dout = cotangent[0, m].astype(f32)
        hidden, inv_two = s["hidden"], s["inv_two"]
        d_hidden = (
            dout
            + gain_two * inv_two * d_n2
            - hidden * inv_two**3 * jnp.mean(hidden * gain_two * d_n2, axis=-1, keepdims=True)
        )
        d_branch = d_hidden.astype(bf16)
        d_adapt_out = (SCALE * mm(d_branch, oup_t)).astype(bf16)
        d_attn = mm_t(d_branch, wout) + mm_t(d_adapt_out, odown)
        dq, dk, dv, dst, dwq, dwk = attend_back(
            s["qkv"], s["kv_ext"], s["state"], wq2, wk2, s["rowinfo"], s["colinfo"], d_attn,
            s["cosine"], s["sine"],
        )
        dadd = leaving(dst, s["tags"], reach)
        dk, dv, dwk_more = state_back(s["kv_ext"], wk2, s["rowinfo"], dadd, dk, dv)
        d_kv = jnp.concatenate([dk, dv], axis=1)
        sent = lax.ppermute(d_kv[:WINDOW].astype(bf16), *unchain).astype(f32)
        d_kv = jnp.concatenate([d_kv[WINDOW:rows], d_kv[rows:] + sent], axis=0)
        d_kv = rope(d_kv, s["cosine"], -s["sine"], 1)
        back.append(
            dict(
                d_hidden=d_hidden, d_branch=d_branch, d_adapt_out=d_adapt_out,
                d_proj=jnp.concatenate([dq, d_kv], axis=1), dwq=dwq, dwk=dwk + dwk_more,
                gain_two=jnp.sum(d_n2 * hidden * inv_two, axis=0),
            )
        )

    attn_all, d_branch = cat(saved, "attn"), cat(back, "d_branch")
    g_wout_own = both_replicas(scatter_rows(t_mm(attn_all, d_branch).astype(bf16)))
    n1_all, d_proj, adapt_all = cat(saved, "n1"), cat(back, "d_proj"), cat(saved, "adapt")
    g_wqkv_own = both_replicas(scatter_rows(t_mm(n1_all, d_proj).astype(bf16)))
    d_adapt = (SCALE * mm_t(d_proj, aup_wide)).astype(bf16)
    d_n1 = mm_t(d_proj, wqkv) + mm_t(d_adapt, adown)
    acts, inv_one = cat(saved, "act"), cat(saved, "inv_one")
    g_gain_one = jnp.sum(d_n1 * acts * inv_one, axis=0)
    grad_inputs = (
        cat(back, "d_hidden")
        + gain_one * inv_one * d_n1
        - acts * inv_one**3 * jnp.mean(acts * gain_one * d_n1, axis=-1, keepdims=True)
    ).astype(bf16)
    g_adown = t_mm(n1_all, d_adapt)
    wide = SCALE * t_mm(adapt_all, d_proj)
    g_aup = jnp.where(owner == 0, wide[:8], jnp.where(owner == 1, wide[8:16], wide[16:24]))
    g_odown = t_mm(attn_all, cat(back, "d_adapt_out"))
    g_oup_t = SCALE * t_mm(d_branch, cat(saved, "adapt_out"))
    fold = lambda a: a[:, :, :HD] - a[:, :, HD:]
    g_featq = fold(sum(b["dwq"] for b in back)).reshape(D, HD)
    g_featk = fold(sum(b["dwk"] for b in back))
    g_gain_two = sum(b["gain_two"] for b in back)
    g_pack = jnp.concatenate(
        [
            g_gain_one[:, None], g_adown, g_odown, g_oup_t, g_featq, g_gain_two[:, None],
            g_aup.reshape(RANK, n, COLS // n).transpose(1, 0, 2).reshape(D, 12),
            g_featk.reshape(D, 16),
        ],
        axis=1,
    )
    g_pack = jnp.pad(g_pack, ((0, 0), (0, PACK - g_pack.shape[1]))).astype(bf16)
    g_small = both_replicas(scatter_rows(g_pack))
    return (
        jnp.stack(outputs)[None],
        grad_inputs.reshape(1, micros, rows, D),
        g_small[:, 0],
        g_wqkv_own,
        g_small[:, 1:25],
        g_small[:, 106:118].reshape(RANK, COLS // n),
        g_wout_own,
        g_small[:, 25:33],
        g_small[:, 33:41].T,
        g_small[:, 41:105],
        g_small[:, 118:134].reshape(KVW // n, HD),
        g_small[:, 105],
        g_wgu_own,
        g_wd_own,
    )


def solution(mesh):
    n = mesh.shape["shard"]
    fine = Mesh(mesh.devices.reshape(mesh.shape["replica"], n // 4, 2, 2), ("r", "z", "x", "c"))
    shard = ("z", "x", "c")
    tokens, row, col = P("r", None, shard, None), P(shard, None), P(None, shard)
    return jax.shard_map(
        per_device,
        mesh=fine,
        in_specs=(
            tokens, tokens, P("r", None, None), P("r", None, shard), P(shard), row, row, col, row,
            row, col, row, row, P(shard), row, row,
        ),
        out_specs=(
            tokens, tokens, P(shard), row, row, col, row, row, col, row, row, P(shard), row, row,
        ),
        check_vma=False,
    )
```

```python
import jax
import jax.numpy as jnp
from jax import lax
from jax.experimental import pallas as pl
from jax.experimental.pallas import tpu as pltpu
from jax.sharding import Mesh, PartitionSpec as P

D = 2048
HEADS = 32
KV = 8
HD = 64
FF = 8192
RANK = 8
WINDOW = 64
MAXLEN = 1024
KVW = KV * HD
COLS = D + 2 * KVW
GROUP = HEADS // KV
NORM_EPS = 1e-05
SCALE = 2.0
ROPE_BASE = 500000.0
SROWS = 80
PACK = 256
bf16 = jnp.bfloat16
f32 = jnp.float32


def mm(a, b):
    return jnp.dot(a, b, preferred_element_type=f32)


def mm_t(a, b):
    return lax.dot_general(a, b, (((1,), (1,)), ((), ())), preferred_element_type=f32)


def t_mm(a, b):
    return lax.dot_general(a, b, (((0,), (0,)), ((), ())), preferred_element_type=f32)


class Links:
    def __init__(self):
        self.last = {}

    def move(self, a, axis, pairs, on=None):
        on = on or {"z": ("outer", "middle")}.get(axis, (axis,))
        before = [self.last[link] for link in on if link in self.last]
        if before:
            a = lax.optimization_barrier((a, *before))[0]
        out = lax.ppermute(a, axis, pairs)
        self.last.update({link: out for link in on})
        return out

    def swap(self, a, axis):
        return self.move(a, axis, [(0, 1), (1, 0)])

    def shift(self, a, k):
        nz = lax.axis_size("z")
        return self.move(a, "z", [(i, (i + k) % nz) for i in range(nz)])

    def slots(self):
        nz, z = lax.axis_size("z"), lax.axis_index("z")
        if nz == 4:
            low = z < 2
            return [z, z ^ 1, jnp.where(low, 2, 1), jnp.where(low, 3, 0)]
        return [lax.rem(z - k + nz, nz) for k in [0] + self.line_order()]

    def line_gather(self, block):
        z = lax.axis_index("z")
        if lax.axis_size("z") != 4:
            return [block] + [self.shift(block, k) for k in self.line_order()]
        ends, ends_out, middle = [(0, 1), (1, 0), (2, 3), (3, 2)], [(1, 0), (2, 3)], [(1, 2), (2, 1)]
        inner = (z == 1) | (z == 2)
        first = self.move(block, "z", ends, ("outer",))
        second = self.move(block, "z", middle, ("middle",))
        second_end = self.move(second, "z", ends_out, ("outer",))
        third = self.move(first, "z", middle, ("middle",))
        third_end = self.move(third, "z", ends_out, ("outer",))
        return [
            block,
            first,
            lambda: jnp.where(inner, second, second_end),
            lambda: jnp.where(inner, third, third_end),
        ]

    def line_scatter(self, parts, hold=()):
        if lax.axis_size("z") != 4:
            moved = [self.shift(parts[i + 1], -k) for i, k in enumerate(self.line_order())]
            return sum([m.astype(f32) for m in moved], parts[0].astype(f32))
        ends, ends_in, middle = [(0, 1), (1, 0), (2, 3), (3, 2)], [(0, 1), (3, 2)], [(1, 2), (2, 1)]
        add = lambda a, b: (a.astype(f32) + b.astype(f32)).astype(bf16)
        own, first, second, third = parts
        third_in = self.move(third, "z", ends_in, ("outer",))
        second_in = self.move(second, "z", ends_in, ("outer",))
        third_in = self.move(add(third, third_in), "z", middle, ("middle",))
        second_in = self.move(add(second, second_in), "z", middle, ("middle",))
        first_in = self.move(add(first, third_in), "z", ends, ("outer",))
        return own.astype(f32) + first_in.astype(f32) + second_in.astype(f32)

    def line_order(self):
        nz = lax.axis_size("z")
        return sorted(range(1, nz), key=lambda k: (min(k, nz - k), k))


def pick(a, i, dim):
    return lax.dynamic_index_in_dim(a, i, dim, False)


def after(a, *others):
    return lax.optimization_barrier((a,) + others)[0]


def by_owner(a):
    nz = lax.axis_size("z")
    z, x, c = lax.axis_index("z"), lax.axis_index("x"), lax.axis_index("c")
    width = a.shape[1] // (4 * nz)
    pieces = []
    for dc in range(2):
        for dx in range(2):
            for k in range(nz):
                at = (lax.rem(z - k + nz, nz) * 2 + (x ^ dx)) * 2 + (c ^ dc)
                pieces.append(lax.dynamic_slice_in_dim(a, at * width, width, 1))
    half = 2 * nz
    return jnp.concatenate(pieces[:half], axis=1), jnp.concatenate(pieces[half:], axis=1)


def core_product(links, mine, theirs, right):
    other = links.swap(t_mm(theirs, right).astype(bf16), "c")
    return lambda *late: (t_mm(mine, right) + after(other, *late).astype(f32)).astype(bf16)


def scatter_x(links, t):
    half = t.shape[0] // 2
    other = links.swap(t[half:], "x")
    return lambda *late: (t[:half].astype(f32) + after(other, *late).astype(f32)).astype(bf16)


def scatter_line(links, t):
    nz = lax.axis_size("z")
    mine, theirs = split_replica(t.reshape(nz, -1, t.shape[1]))
    other = links.swap(theirs, "r")

    def second(*late):
        half = (mine.astype(f32) + after(other, *late).astype(f32)).astype(bf16)
        moved = [links.shift(half[k], -k) for k in links.line_order()]

        def third(*late):
            own = sum([after(m, *late).astype(f32) for m in moved], half[0].astype(f32))
            own = own.astype(bf16)
            far = links.swap(own, "r")
            return lambda: join_replica(own, far)

        return third

    return second


def line_columns(links, weight):
    nz, z = lax.axis_size("z"), lax.axis_index("z")
    rows = weight.shape[0]
    wide = FF // nz
    parts = [None] * nz
    for k in [0] + links.line_order():
        to = lax.rem(z + k, nz)
        part = jnp.concatenate(
            [lax.dynamic_slice(weight, (0, g * FF + to * wide), (rows, wide)) for g in range(2)],
            axis=1,
        )
        parts[k] = links.shift(part, k) if k else part
    return parts


def core_columns(links, parts):
    c = lax.axis_index("c")
    loc = parts[0].shape[1] // 8

    def columns(core):
        return jnp.stack(
            [
                jnp.concatenate(
                    [
                        lax.dynamic_slice_in_dim(p, (4 * g + 2 * x + core) * loc, loc, 1)
                        for x in range(2)
                        for g in range(2)
                    ],
                    axis=1,
                )
                for p in parts
            ]
        )

    mine, theirs = columns(c), links.swap(columns(1 - c), "c")
    return jnp.stack([jnp.where(c == 0, mine, theirs), jnp.where(c == 0, theirs, mine)], axis=1)


def join_gate_up(near, far, near_other, far_other):
    nz = lax.axis_size("z")
    z, x, y = lax.axis_index("z"), lax.axis_index("x"), lax.axis_index("r")
    rows, wide = near.shape[2:]

    def body(at_ref, near_ref, far_ref, near_o_ref, far_o_ref, out_ref):
        h, d = at_ref[2], pl.program_id(1)
        for where, mine, other in ((0, near_ref, near_o_ref), (1, far_ref, far_o_ref)):

            @pl.when(d == where)
            def _():
                for c in range(2):
                    out_ref[0, 0, c, pl.ds(h, 1)] = mine[0, c][None]
                    out_ref[0, 0, c, pl.ds(1 - h, 1)] = other[0, c][None]

    block = pl.BlockSpec((1, 2, rows, wide), lambda k, d, at: (k, 0, 0, 0))
    place = lambda k, d, at: (lax.rem(at[0] - k + nz, nz), at[1] ^ d, 0, 0, 0, 0)
    out = pl.pallas_call(
        body,
        out_shape=jax.ShapeDtypeStruct((nz, 2, 2, 2, rows, wide), bf16),
        grid_spec=pltpu.PrefetchScalarGridSpec(
            num_scalar_prefetch=1,
            grid=(nz, 2),
            in_specs=[block] * 4,
            out_specs=pl.BlockSpec((1, 1, 2, 2, rows, wide), place),
        ),
        cost_estimate=pl.CostEstimate(
            flops=0, bytes_accessed=16 * near.size, transcendentals=0
        ),
        name="join_gate_up",
    )(jnp.stack([z, x, y]).astype(jnp.int32), near, far, near_other, far_other)
    return out.reshape(-1, wide)


def split_replica(t):
    y = lax.axis_index("r")
    t = t.reshape(t.shape[0], 2, -1, t.shape[2])
    return pick(t, y, 1), pick(t, 1 - y, 1)


def join_replica(mine, other):
    y = lax.axis_index("r")
    return jnp.concatenate(
        [jnp.where(y == 0, mine, other), jnp.where(y == 0, other, mine)], axis=0
    ).astype(f32)


def whole_rows(halves):
    rows, cols = halves[0][0].shape
    wide = min(cols, 2048)
    tiles = cols // wide

    def body(at_ref, *refs):
        out_ref, g, h = refs[-1], pl.program_id(0), at_ref[0]
        for i in range(len(halves)):

            @pl.when(g == i)
            def _():
                out_ref[pl.ds(h, 1)] = refs[2 * i][...].astype(f32)[None]
                out_ref[pl.ds(1 - h, 1)] = refs[2 * i + 1][...].astype(f32)[None]

    def block(i):
        return pl.BlockSpec(
            (rows, wide), lambda g, j, at: (0, jnp.where(g == i, j, jnp.where(g < i, 0, tiles - 1)))
        )

    out = pl.pallas_call(
        body,
        out_shape=jax.ShapeDtypeStruct((2, rows, len(halves) * cols), f32),
        grid_spec=pltpu.PrefetchScalarGridSpec(
            num_scalar_prefetch=1,
            grid=(len(halves), tiles),
            in_specs=[block(i) for i in range(len(halves)) for _ in range(2)],
            out_specs=pl.BlockSpec((2, rows, wide), lambda g, j, at: (0, 0, g * tiles + j)),
        ),
        cost_estimate=pl.CostEstimate(
            flops=0, bytes_accessed=12 * len(halves) * rows * cols, transcendentals=0
        ),
        name="whole_rows",
    )(lax.axis_index("r").astype(jnp.int32)[None], *[a for pair in halves for a in pair])
    return out.reshape(2 * rows, -1)


def split_core(links, t, *late):
    c = lax.axis_index("c")
    t = t.reshape(t.shape[0], 2, -1, t.shape[2])
    loc = t.shape[3] // 2
    mine, theirs = pick(t, c, 1), after(links.swap(pick(t, 1 - c, 1), "c"), *late)
    first, second = jnp.where(c == 0, mine, theirs), jnp.where(c == 0, theirs, mine)
    pieces = []
    for j in range(2):
        pieces += [first[:, :, j * loc : (j + 1) * loc], second[:, :, j * loc : (j + 1) * loc]]
    return jnp.concatenate(pieces, axis=2)


def split_line(links, t):
    nz, z = lax.axis_size("z"), lax.axis_index("z")
    parts = [pick(t, lax.rem(z + k, nz), 0) for k in range(nz)]
    for k in links.line_order():
        parts[k] = links.shift(parts[k], k)
    return parts


def join_line(parts):
    nz, z = lax.axis_size("z"), lax.axis_index("z")
    rows, wide = parts[0].shape
    out = jnp.zeros((rows, nz * wide), bf16)
    for k in range(nz):
        at = lax.rem(z - k + nz, nz)
        out = lax.dynamic_update_slice(out, parts[k], (0, at * wide))
    return out


def turn(v, cosine, sine):
    lane = lax.broadcasted_iota(jnp.int32, v.shape, 1)
    low_half = (lane & 63) < 32
    other = jnp.where(low_half, pltpu.roll(v, 96, 1), pltpu.roll(v, 32, 1))
    return v * cosine + other * sine


def rope_kernel(v_ref, cos_ref, sin_ref, o_ref, *, turned):
    j = pl.program_id(0)

    @pl.when(j < turned)
    def _():
        for s in range(4):
            at = slice(s * 128, (s + 1) * 128)
            o_ref[:, at] = turn(v_ref[:, at], cos_ref[...], sin_ref[...]).astype(bf16)

    @pl.when(j >= turned)
    def _():
        o_ref[...] = v_ref[...].astype(bf16)


def rope(values, cosine, sine, turned):
    rows, cols = values.shape
    full = pl.BlockSpec((rows, 128), lambda j: (0, 0))
    return pl.pallas_call(
        lambda *refs: rope_kernel(*refs, turned=turned),
        out_shape=jax.ShapeDtypeStruct((rows, cols), bf16),
        grid=(cols // 512,),
        in_specs=[pl.BlockSpec((rows, 512), lambda j: (0, j)), full, full],
        out_specs=pl.BlockSpec((rows, 512), lambda j: (0, j)),
        cost_estimate=pl.CostEstimate(
            flops=6 * rows * cols, bytes_accessed=6 * rows * cols, transcendentals=0
        ),
        name="rope",
    )(values, cosine, sine)


def halves(shape):
    return lax.broadcasted_iota(jnp.int32, shape, 1) < 64


def feature(z2):
    first = halves(z2.shape)
    top = jnp.max(jnp.where(first, z2, -jnp.inf), axis=1, keepdims=True)
    low = jnp.max(jnp.where(first, -jnp.inf, z2), axis=1, keepdims=True)
    e = jnp.exp(z2 - jnp.where(first, top, low))
    s1 = jnp.sum(jnp.where(first, e, 0.0), axis=1, keepdims=True)
    s2 = jnp.sum(jnp.where(first, 0.0, e), axis=1, keepdims=True)
    return e * jnp.where(first, 1.0 / s1, 1.0 / s2)


def feature_grad(phi, dphi):
    first = halves(phi.shape)
    t = phi * dphi
    s1 = jnp.sum(jnp.where(first, t, 0.0), axis=1, keepdims=True)
    s2 = jnp.sum(jnp.where(first, 0.0, t), axis=1, keepdims=True)
    return t - phi * jnp.where(first, s1, s2)


def with_one(v):
    wide = jnp.concatenate([v, jnp.zeros_like(v)], axis=1)
    lane = lax.broadcasted_iota(jnp.int32, wide.shape, 1)
    return jnp.where(lane == 64, jnp.ones_like(wide), wide)


def tile(a):
    return jnp.concatenate([a] * GROUP, axis=0)


def attention_masks(row_ref, col_ref):
    rows, extent = row_ref.shape[0], col_ref.shape[1]
    offset = (
        lax.broadcasted_iota(jnp.int32, (rows, extent), 0)
        + WINDOW
        - lax.broadcasted_iota(jnp.int32, (rows, extent), 1)
    )
    same = row_ref[:, 0:1] == col_ref[0:1, :]
    live = col_ref[1:2, :] > 0
    window = (offset >= 0) & (offset < WINDOW) & same & (live | (offset == 0))
    far = (offset >= WINDOW) & same & live
    return tile(window.astype(f32)) > 0, tile(far.astype(f32)) > 0


def query_heads(ref, hh):
    return [ref[:, (hh * GROUP + i) * HD : (hh * GROUP + i + 1) * HD] for i in range(GROUP)]


def head_forward(q_ref, k, wq_ref, wk, hh, window, far):
    qs = query_heads(q_ref, hh)
    q4 = jnp.concatenate(qs, axis=0)
    s = jnp.where(window, mm_t(q4, k) * 0.125, -1e30)
    top = jnp.max(s, axis=1, keepdims=True)
    p = jnp.exp(s - top)
    e = jnp.exp(-top)
    phi = feature(
        jnp.concatenate([mm(qs[i], wq_ref[hh * GROUP + i]) for i in range(GROUP)], axis=0)
    )
    phik = feature(mm(k, wk))
    phi_b, phik_b = phi.astype(bf16), phik.astype(bf16)
    a_b = (p + e * jnp.where(far, mm_t(phi_b, phik_b), 0.0)).astype(bf16)
    return qs, q4, p, e, phi, phi_b, phik, phik_b, a_b


def full_state(st):
    return jnp.concatenate([st, jnp.zeros((128 - SROWS, 128), bf16)], axis=0)


def attend_kernel(q_ref, k_ref, v_ref, wq_ref, wk_ref, row_ref, col_ref, nd_ref, phi_ref):
    window, far = attention_masks(row_ref, col_ref)
    use = tile(row_ref[:, 1:2])
    for hh in range(2):
        at = slice(hh * HD, (hh + 1) * HD)
        _, _, _, e, phi, _, _, _, a_b = head_forward(
            q_ref, k_ref[:, at], wq_ref, wk_ref[hh], hh, window, far
        )
        nd_ref[0, hh] = mm(a_b, with_one(v_ref[:, at]))
        phi_ref[0, hh] = ((e * use) * phi).astype(bf16)


def finish_kernel(nd_ref, phi_ref, st_ref, row_ref, nd_out, o_ref):
    rows = row_ref.shape[0]
    live = tile(row_ref[:, 2:3])
    for hh in range(2):
        nd = nd_ref[0, hh] + mm_t(phi_ref[0, hh], full_state(st_ref[0, hh]))
        nd_out[0, hh] = nd
        out = (nd[:, :HD] * (live / nd[:, HD : HD + 1])).astype(bf16)
        for i in range(GROUP):
            j = hh * GROUP + i
            o_ref[:, j * HD : (j + 1) * HD] = out[i * rows : (i + 1) * rows]


def numerator_grad(do_ref, nd, live, hh):
    do4 = jnp.concatenate(query_heads(do_ref, hh), axis=0)
    inv = 1.0 / nd[:, HD : HD + 1]
    dnum = do4 * (live * inv)
    dden = -jnp.sum(dnum * nd[:, :HD], axis=1, keepdims=True) * inv
    dn = jnp.concatenate([dnum, jnp.zeros_like(dnum)], axis=1)
    lane = lax.broadcasted_iota(jnp.int32, dn.shape, 1)
    return jnp.where(lane == HD, dden, dn)


def state_grad_kernel(do_ref, nd_ref, phi_ref, row_ref, dst_ref):
    live = tile(row_ref[:, 2:3])
    for hh in range(2):
        dn = numerator_grad(do_ref, nd_ref[0, hh], live, hh)
        dst_ref[0, hh] = t_mm(dn.astype(bf16), phi_ref[0, hh])[:SROWS].astype(bf16)


def attend_back_kernel(
    q_ref, k_ref, v_ref, st_ref, wq_ref, wk_ref, row_ref, col_ref, do_ref, nd_ref, cos_ref,
    sin_ref, dq_ref, dk_ref, dv_ref, dwq_ref, dwk_ref, scr_ref,
):
    rows = q_ref.shape[0]
    window, far = attention_masks(row_ref, col_ref)
    use, live = tile(row_ref[:, 1:2]), tile(row_ref[:, 2:3])
    for hh in range(2):
        at = slice(hh * HD, (hh + 1) * HD)
        k = k_ref[:, at]
        qs, q4, p, e, phi, phi_b, phik, phik_b, a_b = head_forward(
            q_ref, k, wq_ref, wk_ref[hh], hh, window, far
        )
        dn = numerator_grad(do_ref, nd_ref[0, hh], live, hh)
        dn_b = dn.astype(bf16)
        en_b = ((e * use) * dn).astype(bf16)
        da = mm_t(dn_b, with_one(v_ref[:, at]))
        ds_b = (da * p * 0.125).astype(bf16)
        dl_b = jnp.where(far, e * da, 0.0).astype(bf16)
        dv_ref[:, at] = t_mm(a_b, dn_b)[:, :HD]
        dphi = mm(dl_b, phik_b) + mm(en_b, full_state(st_ref[0, hh]))
        dz = feature_grad(phi, dphi).astype(bf16)
        dzk = feature_grad(phik, t_mm(dl_b, phi_b)).astype(bf16)
        dq4 = mm(ds_b, k)
        dk_ref[:, at] = t_mm(ds_b, q4) + mm_t(dzk, wk_ref[hh])
        dwk_ref[0, hh] = t_mm(k, dzk)
        for i in range(GROUP):
            j = hh * GROUP + i
            dzi = dz[i * rows : (i + 1) * rows]
            scr_ref[:, j * HD : (j + 1) * HD] = dq4[i * rows : (i + 1) * rows] + mm_t(
                dzi, wq_ref[j]
            )
            dwq_ref[0, j] = t_mm(qs[i], dzi)
    for s in range(4):
        at = slice(s * 128, (s + 1) * 128)
        dq_ref[:, at] = turn(scr_ref[:, at], cos_ref[...], -sin_ref[...]).astype(bf16)


def state_kernel(k_ref, v_ref, wk_ref, row_ref, add_ref):
    rows = row_ref.shape[0]
    chosen = row_ref[:, 3:4]
    for hh in range(2):
        at = slice(hh * HD, (hh + 1) * HD)
        phik = (feature(mm(k_ref[:rows, at], wk_ref[hh])) * chosen).astype(bf16)
        add_ref[0, hh] = t_mm(with_one(v_ref[:rows, at]), phik)[:SROWS].astype(bf16)


def state_back_kernel(
    k_ref, v_ref, wk_ref, row_ref, dadd_ref, dk_in, dv_in, dk_ref, dv_ref, dwk_ref
):
    rows = row_ref.shape[0]
    chosen = row_ref[:, 3:4]
    dk_ref[rows:] = dk_in[rows:]
    dv_ref[rows:] = dv_in[rows:]
    for hh in range(2):
        at = slice(hh * HD, (hh + 1) * HD)
        k = k_ref[:rows, at]
        phik = feature(mm(k, wk_ref[hh]))
        dadd = full_state(dadd_ref[0, hh])
        dphi = mm(with_one(v_ref[:rows, at]), dadd) * chosen
        dz = feature_grad(phik, dphi).astype(bf16)
        dk_ref[:rows, at] = dk_in[:rows, at] + mm_t(dz, wk_ref[hh])
        dv_ref[:rows, at] = dv_in[:rows, at] + mm_t((phik * chosen).astype(bf16), dadd)[:, :HD]
        dwk_ref[0, hh] = t_mm(k, dz)


def call(kernel, micros, rows, extent, ins, outs, args, flops, scratch=(), only=None, into=()):
    base, count, skip, pairs = (0, micros, 0, 4) if only is None else (only[0], 1, only[1], only[2])
    block = dict(
        q=((rows, 512), lambda m, j: (m + base, j + skip)),
        k=((extent, 128), lambda m, j: (m + base, j + skip)),
        v=((extent, 128), lambda m, j: (m + base, 4 + j + skip)),
        st=((1, 2, SROWS, 128), lambda m, j: (m + base, j + skip, 0, 0)),
        nd=((1, 2, GROUP * rows, 128), lambda m, j: (m + base, j + skip, 0, 0)),
        wq=((8, HD, 128), lambda m, j: (j + skip, 0, 0)),
        wk=((2, HD, 128), lambda m, j: (j + skip, 0, 0)),
        dwq=((1, 8, HD, 128), lambda m, j: (m + base, j + skip, 0, 0)),
        dwk=((1, 2, HD, 128), lambda m, j: (m + base, j + skip, 0, 0)),
        row=((rows, 128), lambda m, j: (m + base, 0)),
        col=((8, extent), lambda m, j: (m + base, 0)),
    )
    shapes = dict(
        q=(micros * rows, D),
        k=(micros * extent, KVW),
        st=(micros, KV, SROWS, 128),
        nd=(micros, KV, GROUP * rows, 128),
        dwq=(micros, HEADS, HD, 128),
        dwk=(micros, KV, HD, 128),
    )
    spec = lambda name: pl.BlockSpec(*block[name])
    size = lambda a: a.size * a.dtype.itemsize
    out_shape = tuple(jax.ShapeDtypeStruct(shapes[name], kind) for name, kind in outs)

    def body(*refs):
        kernel(*refs[: len(ins)], *refs[len(ins) + len(into) :])

    return pl.pallas_call(
        body,
        out_shape=out_shape,
        grid=(count, pairs),
        in_specs=[spec(name) for name in ins] + [pl.BlockSpec(memory_space=pl.ANY)] * len(into),
        out_specs=tuple(spec(name) for name, _ in outs),
        scratch_shapes=scratch,
        input_output_aliases={len(ins) + i: i for i in range(len(into))},
        compiler_params=pltpu.CompilerParams(vmem_limit_bytes=48 << 20),
        cost_estimate=pl.CostEstimate(
            flops=flops * count * pairs // (4 * micros),
            bytes_accessed=(sum(size(a) for a in args) + sum(size(a) for a in out_shape))
            * (count * pairs)
            // (4 * micros),
            transcendentals=count * pairs * HEADS * rows * extent // 4,
        ),
        name=kernel.__name__,
    )(*args, *into)


def ffn_kernel(at_ref, own_ref, other_ref, pair_ref, w_ref, wd_ref, *refs):
    act_ref, dg_ref, du_ref, n2_ref, df_ref, mine_ref, theirs_ref, out_ref, dn_acc, out_acc = refs[-10:]
    f, rows, width = pl.program_id(0), own_ref.shape[0], wd_ref.shape[0]
    here = pl.ds(pl.multiple_of(at_ref[1] * rows, rows), rows)
    there = pl.ds(pl.multiple_of((1 - at_ref[1]) * rows, rows), rows)

    @pl.when(f == 0)
    def _():
        n2_ref[here] = own_ref[...]
        n2_ref[there] = other_ref[...]
        df_ref[:rows] = pair_ref[0, 0]
        df_ref[rows:] = pair_ref[0, 1]

    gate_up = mm(n2_ref[...], w_ref[...])
    gate, up = gate_up[:, :width], gate_up[:, width:]
    d_act = mm_t(df_ref[...], wd_ref[...])
    sig = 1.0 / (1.0 + jnp.exp(-gate))
    swish = gate * sig
    acted = (swish * up).astype(bf16)
    d_gate = (d_act * up * (sig * (1.0 + gate * (1.0 - sig)))).astype(bf16)
    d_up = (d_act * swish).astype(bf16)
    act_ref[...] = acted
    dg_ref[...] = d_gate
    du_ref[...] = d_up
    d_n2 = mm_t(jnp.concatenate([d_gate, d_up], axis=1), w_ref[...])
    out = mm(acted, wd_ref[...])

    @pl.when(f == 0)
    def _():
        dn_acc[...] = d_n2
        out_acc[...] = out

    @pl.when(f > 0)
    def _():
        dn_acc[...] += d_n2
        out_acc[...] += out

    @pl.when(f == pl.num_programs(0) - 1)
    def _():
        mine_ref[...] = dn_acc[here]
        theirs_ref[...] = dn_acc[there].astype(bf16)
        out_ref[0, 0] = out_acc[:rows].astype(bf16)
        out_ref[0, 1] = out_acc[rows:].astype(bf16)


def ffn_chunk(k, at, own, other, df_all, wgu, wd, held):
    rows = own.shape[0]
    total, half = df_all.shape[0] * df_all.shape[1] * rows, wd.shape[0]
    width = half // 2
    tiles = half // width
    tokens = pl.BlockSpec((rows, D), lambda f, a: (0, 0))
    chunk = pl.BlockSpec((2 * rows, D), lambda f, a: (k, 0))
    hidden = pl.BlockSpec((2 * rows, width), lambda f, a: (k, f))
    pair = pl.BlockSpec((1, 2, rows, D), lambda f, a: (a[0], 0, 0, 0))
    whole = (total, D)
    outs = [((total, half), bf16)] * 3 + [(whole, bf16)] * 2
    outs += [((rows, D), f32), ((rows, D), bf16), (df_all.shape, bf16)]
    return pl.pallas_call(
        ffn_kernel,
        out_shape=tuple(jax.ShapeDtypeStruct(a, b) for a, b in outs),
        grid_spec=pltpu.PrefetchScalarGridSpec(
            num_scalar_prefetch=1,
            grid=(tiles,),
            in_specs=[
                tokens,
                tokens,
                pair,
                pl.BlockSpec((D, 2 * width), lambda f, a: (0, f)),
                pl.BlockSpec((width, D), lambda f, a: (f, 0)),
            ]
            + [pl.BlockSpec(memory_space=pl.ANY)] * len(held),
            out_specs=(
                hidden, hidden, hidden, chunk, chunk, tokens, tokens,
                pair,
            ),
            scratch_shapes=[pltpu.VMEM((2 * rows, D), f32)] * 2,
        ),
        input_output_aliases={6 + i: (i if i < 5 else 7) for i in range(len(held))},
        compiler_params=pltpu.CompilerParams(vmem_limit_bytes=56 << 20),
        cost_estimate=pl.CostEstimate(
            flops=24 * rows * D * half,
            bytes_accessed=6 * D * half + 40 * rows * D,
            transcendentals=2 * rows * half,
        ),
        name="ffn_chunk",
    )(at, own, other, df_all, wgu, wd, *held)


def weigh(flag, a):
    return jnp.where(flag[:, None, None, None], a.astype(f32), 0.0)


def entering(links, add, tags, reach):
    nz = lax.axis_size("z")
    z, x, c = lax.axis_index("z"), lax.axis_index("x"), lax.axis_index("c")
    p = (z * 2 + x) * 2 + c
    tag = lambda i: pick(tags, jnp.clip(i, 0, 4 * nz - 1), 1)
    prev = tag(p - 1)
    chip = (z * 2 + x) * 2
    other = links.swap(add, "c")
    other = after(other, (yield))
    one = tag(chip) == tag(chip + 1)
    chip_sum = (weigh((c == 1) | one, add) + weigh((c == 0) | one, other)).astype(bf16)
    side = links.swap(chip_sum, "x")
    side = after(side, (yield))
    one = tag(z * 4 + 1) == tag(z * 4 + 3)
    layer = (weigh((x == 1) | one, chip_sum) + weigh((x == 0) | one, side)).astype(bf16)
    state = weigh((c == 1) & (prev >= 0), other) + weigh((x == 1) & (tag(z * 4 + 1) == prev), side)
    got = [
        links.move(layer, "z", [(i, i + hop) for i in range(nz - hop)])
        for hop in range(1, min(reach, nz - 1) + 1)
    ]
    late = yield
    for hop, far in enumerate(got, 1):
        state += weigh((z >= hop) & (tag((z - hop) * 4 + 3) == prev), after(far, late))
    yield state.astype(bf16)


def leaving(links, dstate, tags, reach):
    nz = lax.axis_size("z")
    z, x, c = lax.axis_index("z"), lax.axis_index("x"), lax.axis_index("c")
    p = (z * 2 + x) * 2 + c
    tag = lambda i: pick(tags, jnp.clip(i, 0, 4 * nz - 1), 1)
    from_tag = lambda i: jnp.where(i > 0, tag(i - 1), -1)
    own = tag(p)
    chip = (z * 2 + x) * 2
    other = links.swap(dstate, "c")
    other = after(other, (yield))
    one = from_tag(chip) == from_tag(chip + 1)
    chip_sum = (weigh((c == 0) | one, dstate) + weigh((c == 1) | one, other)).astype(bf16)
    side = links.swap(chip_sum, "x")
    side = after(side, (yield))
    one = from_tag(z * 4) == from_tag(z * 4 + 2)
    layer = (weigh((x == 0) | one, chip_sum) + weigh((x == 1) | one, side)).astype(bf16)
    total = weigh((c == 0) & (own >= 0), other) + weigh(
        (x == 0) & (from_tag(z * 4 + 2) == own), side
    )
    got = [
        links.move(layer, "z", [(i, i - hop) for i in range(hop, nz)])
        for hop in range(1, min(reach, nz - 1) + 1)
    ]
    late = yield
    for hop, far in enumerate(got, 1):
        total += weigh((z + hop < nz) & (from_tag((z + hop) * 4) == own), after(far, late))
    yield total.astype(bf16)


def per_device(
    inputs, cotangent, lengths, padding, gain_attn_own, wqkv_own, adown_own, aup_own, wout_own,
    odown_own, oup_own, featq_own, featk_own, gain_ffn_own, wgu_own, wd_own,
):
    nz = lax.axis_size("z")
    n = 4 * nz
    z, x, c = lax.axis_index("z"), lax.axis_index("x"), lax.axis_index("c")
    place_own = (z * 2 + x) * 2 + c
    micros, rows = inputs.shape[1], inputs.shape[2]
    both = micros * rows
    extent = rows + WINDOW
    reach = -(-MAXLEN // (4 * rows))
    everyone = ("z", "x", "c")
    chain = (everyone, [(i, i + 1) for i in range(n - 1)])
    unchain = (everyone, [(i, i - 1) for i in range(1, n)])
    r = D // n

    pack = jnp.concatenate(
        [
            gain_attn_own[:, None], adown_own, odown_own, oup_own.T, featq_own,
            gain_ffn_own[:, None], aup_own.reshape(r, 12), featk_own.reshape(r, 16),
        ],
        axis=1,
    )
    pack = jnp.pad(pack, ((0, 0), (0, PACK - pack.shape[1])))
    links = Links()
    live_all = padding[0].astype(bf16)
    halo_live = lax.ppermute(live_all[:, rows - WINDOW :], *chain)
    first = lax.all_gather(
        jnp.concatenate([wqkv_own, wout_own, pack], axis=1), everyone, axis=0, tiled=True
    )
    wqkv, wout, small = first[:, :COLS], first[:, COLS : COLS + D], first[:, COLS + D :]
    cot = cotangent[0].reshape(both, D)
    y = lax.axis_index("r")
    wgu_half = lax.dynamic_slice_in_dim(wgu_own, y * (r // 2), r // 2, 0)
    wgu_near = core_columns(links, line_columns(links, wgu_half))
    wgu_near_other = links.swap(wgu_near, "r")
    small, wgu_send = lax.optimization_barrier((small, wgu_near, wgu_near_other))[:2]
    wgu_far = links.swap(wgu_send, "x")
    gain_one = small[:, 0].astype(f32)[None]
    adown = small[:, 1:25]
    odown = small[:, 25:33]
    oup_t = small[:, 33:41]
    featq = small[:, 41:105].reshape(HEADS, HD, HD)
    gain_two = small[:, 105].astype(f32)[None]
    aup = small[:, 106:118].reshape(n, RANK, COLS // n).transpose(1, 0, 2).reshape(RANK, COLS)
    featk = small[:, 118:134].reshape(KV, HD, HD)
    wq2 = jnp.concatenate([featq, -featq], axis=2)
    wk2 = jnp.concatenate([featk, -featk], axis=2)
    column = jnp.arange(COLS)[None]
    owner = jnp.where(column < D, 0, jnp.where(column < D + KVW, 1, 2))
    aup_wide = jnp.concatenate(
        [jnp.where(owner == t, aup, jnp.zeros_like(aup)) for t in range(3)], axis=0
    )

    doc_lengths = lengths[0]
    ends = jnp.cumsum(doc_lengths, axis=1)
    places = place_own * rows - WINDOW + jnp.arange(extent, dtype=jnp.int32)
    done = ends[:, None, :] <= places[None, :, None]
    seg_ext = jnp.sum(done.astype(jnp.int32), axis=2)
    pos = places[None] - jnp.sum(jnp.where(done, doc_lengths[:, None, :], 0), axis=2)
    pos = pos[:, WINDOW:].reshape(both)
    edges = jnp.arange(n, dtype=jnp.int32) * rows + (rows - WINDOW - 1)
    tags = jnp.sum((ends[:, None, :] <= edges[None, :, None]).astype(jnp.int32), axis=2)
    live_ext = jnp.concatenate([halo_live, live_all], axis=1).astype(f32)
    prev_tag = jnp.where(place_own > 0, pick(tags, jnp.maximum(place_own - 1, 0), 1), -1)
    own_tag = pick(tags, place_own, 1)
    seg_own = seg_ext[:, WINDOW:]
    info = jnp.stack(
        [
            seg_own.astype(f32),
            (seg_own == prev_tag[:, None]).astype(f32),
            live_ext[:, WINDOW:],
            ((seg_ext[:, :rows] == own_tag[:, None]) & (live_ext[:, :rows] > 0)).astype(f32),
        ],
        axis=2,
    ).reshape(both, 4)
    rowinfo = jnp.pad(info, ((0, 0), (0, 124)))
    colinfo = jnp.pad(
        jnp.stack([seg_ext.astype(f32), live_ext], axis=1), ((0, 0), (0, 6), (0, 0))
    ).reshape(micros * 8, extent)
    lane = jnp.arange(128)
    frequency = ROPE_BASE ** (-((lane % 32).astype(f32) * 2.0) / HD)
    angles = pos.astype(f32)[:, None] * frequency[None, :]
    cosine = jnp.cos(angles)
    sine = jnp.where((lane % 64 < 32)[None], -1.0, 1.0) * jnp.sin(angles)

    act = inputs[0].reshape(both, D).astype(f32)
    inv_one = lax.rsqrt(jnp.mean(act * act, axis=-1, keepdims=True) + NORM_EPS)
    n1 = (act * inv_one * gain_one).astype(bf16)
    adapt = mm(n1, adown).astype(bf16)
    projected = mm(n1, wqkv) + SCALE * mm(adapt, aup_wide)
    qkv = rope(projected, cosine, sine, 5)
    kv = qkv[:, D:].reshape(micros, rows, 2 * KVW)
    halo = lax.ppermute(kv[:, rows - WINDOW :], *chain)
    kv_ext = jnp.concatenate([halo, kv], axis=1).reshape(micros * extent, 2 * KVW)
    launch = lambda kernel, ins, outs, args, work, **k: call(
        kernel, micros, rows, extent, ins, outs, args, micros * HEADS * rows * work, **k
    )
    (add,) = launch(
        state_kernel, ("k", "v", "wk", "row"), [("st", bf16)], (kv_ext, kv_ext, wk2, rowinfo), 8192
    )
    df_all = lax.all_gather(after(cot, small), ("z", "c"), axis=0, tiled=True)
    df_all = df_all.reshape(nz, 2, both, D)
    wd = lax.all_gather(after(wd_own, df_all), "x", axis=0, tiled=True)
    parts = [(m, j, 2) for m in range(micros) for j in (0, 2)]
    travel = entering(links, add, tags, reach)
    next(travel)
    wgu_far, wk2_late = lax.optimization_barrier((wgu_far, wk2, add))[:2]
    wgu_far_other = links.swap(wgu_far, "r")
    local = ()
    for i, part in enumerate(parts):
        local = launch(
            attend_kernel,
            ("q", "k", "v", "wq", "wk", "row", "col"),
            [("nd", f32), ("nd", bf16)],
            (qkv, kv_ext, kv_ext, wq2, wk2_late, rowinfo, colinfo),
            1000 * extent,
            only=part,
            into=local,
        )
        if i < 2:
            travel.send(local[1])
    nd, phi = local
    state = travel.send(phi)
    nd, attn = launch(
        finish_kernel,
        ("nd", "nd", "st", "row"),
        [("nd", f32), ("q", bf16)],
        (nd, phi, state, rowinfo),
        32768,
    )
    adapt_out = mm(attn, odown).astype(bf16)
    hidden = act + (mm(attn, wout) + SCALE * mm_t(adapt_out, oup_t))
    inv_two = lax.rsqrt(jnp.mean(hidden * hidden, axis=-1, keepdims=True) + NORM_EPS)
    n2 = (hidden * inv_two * gain_two).astype(bf16)

    half = 2 * FF // n
    loc = half // 2
    n2_parts = links.line_gather(n2)
    late = lambda a: after(a, attn)
    wgu = join_gate_up(late(wgu_near), wgu_far, late(wgu_near_other), late(wgu_far_other))
    returned, held = [], ()
    for i, (place, part) in enumerate(zip(links.slots(), n2_parts)):
        at = jnp.stack([place, c]).astype(jnp.int32)
        part = part() if callable(part) else part
        if i:
            part = after(part, held[0])
        result = ffn_chunk(i, at, part, links.swap(part, "c"), df_all, wgu, wd, held)
        held = result[:5] + result[7:]
        d_n2_i = result[5] + links.swap(result[6], "c").astype(f32)
        returned.append(d_n2_i.astype(bf16) if i else d_n2_i)
    acted, d_gate, d_up, n2_all, df_held, out_parts = held
    d_n2 = links.line_scatter(returned)
    g_gate = t_mm(n2_all, d_gate).astype(bf16)
    g_up = t_mm(n2_all, d_up).astype(bf16)
    g_wd = t_mm(acted, df_held).astype(bf16)
    d_n2 = after(d_n2, g_gate, g_up, g_wd)
    plus = lambda a, b: (a.astype(f32) + b.astype(f32)).astype(bf16)
    out_sum = lax.psum_scatter(
        after(out_parts, d_n2).reshape(-1, D), ("z", "c"), scatter_dimension=0, tiled=True
    )
    g_gate, g_up = g_gate.reshape(n, r, half), g_up.reshape(n, r, half)
    g_wd = g_wd.reshape(2, loc, D)
    gu_mine, gu_other = [], []
    for g in (g_gate, g_up, g_wd):
        mine, theirs = split_replica(g)
        gu_mine.append(mine)
        gu_other.append(links.swap(theirs, "r"))

    def replica_sum(i, *late):
        return (gu_mine[i].astype(f32) + after(gu_other[i], *late).astype(f32)).astype(bf16)

    def x_parts(t):
        t = t.reshape(-1, 2, t.shape[-2] * (2 if t.shape[0] == n else 1), t.shape[-1])
        return pick(t, x, 1), pick(t, 1 - x, 1)

    d_hidden = (
        cot.astype(f32)
        + gain_two * inv_two * d_n2
        - hidden * inv_two**3 * jnp.mean(hidden * gain_two * d_n2, axis=-1, keepdims=True)
    )
    d_branch = d_hidden.astype(bf16)
    d_adapt_out = (SCALE * mm(d_branch, oup_t)).astype(bf16)
    d_attn = mm_t(d_branch, wout) + mm_t(d_adapt_out, odown)
    (dst,) = launch(
        state_grad_kernel,
        ("q", "nd", "nd", "row"),
        [("st", bf16)],
        (d_attn, nd, phi, rowinfo),
        32768,
    )
    attn_owner, n1_owner = by_owner(attn), by_owner(n1)
    gate_mine, gate_theirs = x_parts(replica_sum(0, d_attn))
    gate_side = links.swap(gate_theirs, "x")
    travel = leaving(links, dst, tags, reach)
    next(travel)
    wout_core = core_product(links, *attn_owner, d_branch)
    grads = ()
    d_attn_late = d_attn
    for i, part in enumerate(parts):
        grads = launch(
            attend_back_kernel,
            ("q", "k", "v", "st", "wq", "wk", "row", "col", "q", "nd", "row", "row"),
            [("q", bf16), ("k", f32), ("k", f32), ("dwq", f32), ("dwk", f32)],
            (qkv, kv_ext, kv_ext, state, wq2, wk2, rowinfo, colinfo, d_attn_late, nd, cosine, sine),
            2000 * extent,
            scratch=[pltpu.VMEM((rows, 512), f32)],
            only=part,
            into=grads,
        )
        done = grads[0]
        if i == 0:
            travel.send(done)
            wout_x = scatter_x(links, wout_core(done))
            gate_rows = split_core(links, plus(gate_mine, after(gate_side, done)))
        elif i == 1:
            travel.send(done)
            gate_line = split_line(links, gate_rows)
            up_mine, up_theirs = x_parts(replica_sum(1, done))
            up_side = links.swap(up_theirs, "x")
        elif i == 2:
            d_attn_late = after(d_attn_late, out_sum)
    dq, dk, dv, dwq, dwk = grads
    dadd = travel.send(dq)
    wout_line = scatter_line(links, wout_x(dq))
    q_core = core_product(links, *n1_owner, dq)
    dk, dv, dwk_more = launch(
        state_back_kernel,
        ("k", "v", "wk", "row", "st", "k", "k"),
        [("k", f32), ("k", f32), ("dwk", f32)],
        (kv_ext, kv_ext, wk2, rowinfo, dadd, dk, dv),
        16384,
    )
    d_kv = jnp.concatenate([dk, dv], axis=1).reshape(micros, extent, 2 * KVW)
    sent = lax.ppermute(d_kv[:, :WINDOW].astype(bf16), *unchain)
    gate_half = join_line([after(p, dk) for p in gate_line])
    gate_far = links.swap(gate_half, "r")
    q_sum, up_rows = lax.optimization_barrier(
        (q_core(dadd), plus(up_mine, after(up_side, dadd)), sent)
    )[:2]
    q_x = scatter_x(links, q_sum)
    wout_line = wout_line(dadd, sent)
    up_line = split_line(links, split_core(links, up_rows))
    sent = sent.astype(f32)
    d_kv = jnp.concatenate([d_kv[:, WINDOW:rows], d_kv[:, rows:] + sent], axis=1)
    d_kv = rope(d_kv.reshape(both, 2 * KVW), cosine, -sine, 1)
    kv_sum = core_product(links, *n1_owner, d_kv)()
    kv_x = scatter_x(links, kv_sum)
    wd_mine, wd_theirs = x_parts(replica_sum(2, kv_sum))
    wd_side = links.swap(wd_theirs, "x")
    d_proj = jnp.concatenate([dq, d_kv], axis=1)
    d_adapt = (SCALE * mm_t(d_proj, aup_wide)).astype(bf16)
    d_n1 = mm_t(d_proj, wqkv) + mm_t(d_adapt, adown)
    g_gain_one = jnp.sum(d_n1 * act * inv_one, axis=0)
    grad_inputs = (
        d_hidden
        + gain_one * inv_one * d_n1
        - act * inv_one**3 * jnp.mean(act * gain_one * d_n1, axis=-1, keepdims=True)
    ).astype(bf16)
    g_adown = t_mm(n1, d_adapt)
    wide = SCALE * t_mm(adapt, d_proj)
    g_aup = jnp.where(owner == 0, wide[:8], jnp.where(owner == 1, wide[8:16], wide[16:24]))
    g_odown = t_mm(attn, d_adapt_out)
    g_oup_t = SCALE * t_mm(d_branch, adapt_out)
    fold = lambda a: a[:, :, :HD] - a[:, :, HD:]
    g_featq = fold(jnp.sum(dwq, axis=0)).reshape(D, HD)
    g_featk = fold(jnp.sum(dwk + dwk_more, axis=0))
    g_gain_two = jnp.sum(d_n2 * hidden * inv_two, axis=0)
    g_pack = jnp.concatenate(
        [
            g_gain_one[:, None], g_adown, g_odown, g_oup_t, g_featq, g_gain_two[:, None],
            g_aup.reshape(RANK, n, COLS // n).transpose(1, 0, 2).reshape(D, 12),
            g_featk.reshape(D, 16),
        ],
        axis=1,
    )
    g_pack = jnp.pad(g_pack, ((0, 0), (0, PACK - g_pack.shape[1]))).astype(bf16)
    nat = g_pack.reshape(nz, 2, 2, r, PACK)
    mine, theirs = pick(nat, c, 2), pick(nat, 1 - c, 2)
    nat = plus(mine, links.swap(theirs, "c"))
    mine, theirs = pick(nat, x, 1), pick(nat, 1 - x, 1)
    pack_side = links.swap(theirs, "x")
    wout_line = wout_line(theirs)
    q_line = scatter_line(links, q_x(theirs))
    kv_line = scatter_line(links, kv_x(theirs))
    wd_half = plus(wd_mine, after(wd_side, theirs)).reshape(-1, D)
    nat = plus(mine, pack_side)
    nat = jnp.concatenate([pick(nat, lax.rem(z - k + nz, nz), 0) for k in range(nz)], axis=0)
    q_line = q_line()
    up_half = join_line([after(p, theirs) for p in up_line])
    up_far = links.swap(up_half, "r")
    kv_line = kv_line()
    pack_line = scatter_line(links, nat)
    wd_far = links.swap(wd_half, "r")
    pack_line = pack_line()
    output = (hidden + after(out_sum, nat).astype(f32)).astype(bf16)
    q_line, kv_line, pack_line = q_line(), kv_line(), pack_line()
    g_small = pack_line()
    g_wout_own = wout_line()
    g_wd_own = join_replica(wd_half, wd_far)
    g_wgu_own = whole_rows([(gate_half, gate_far), (up_half, up_far)])
    g_wqkv_own = jnp.concatenate([q_line(), kv_line()], axis=1)
    return (
        output.reshape(1, micros, rows, D),
        grad_inputs.reshape(1, micros, rows, D),
        g_small[:, 0],
        g_wqkv_own,
        g_small[:, 1:25],
        g_small[:, 106:118].reshape(RANK, COLS // n),
        g_wout_own,
        g_small[:, 25:33],
        g_small[:, 33:41].T,
        g_small[:, 41:105],
        g_small[:, 118:134].reshape(KVW // n, HD),
        g_small[:, 105],
        g_wgu_own,
        g_wd_own,
    )


def solution(mesh):
    n = mesh.shape["shard"]
    fine = Mesh(mesh.devices.reshape(mesh.shape["replica"], n // 4, 2, 2), ("r", "z", "x", "c"))
    shard = ("z", "x", "c")
    tokens, row, col = P("r", None, shard, None), P(shard, None), P(None, shard)
    return jax.shard_map(
        per_device,
        mesh=fine,
        in_specs=(
            tokens, tokens, P("r", None, None), P("r", None, shard), P(shard), row, row, col, row,
            row, col, row, row, P(shard), row, row,
        ),
        out_specs=(
            tokens, tokens, P(shard), row, row, col, row, row, col, row, row, P(shard), row, row,
        ),
        check_vma=False,
    )
```

```python
import jax
import jax.numpy as jnp
from jax import lax
from jax.experimental import pallas as pl
from jax.experimental.pallas import tpu as pltpu
from jax.sharding import Mesh, PartitionSpec as P

D = 2048
HEADS = 32
KV = 8
HD = 64
FF = 8192
RANK = 8
WINDOW = 64
MAXLEN = 1024
KVW = KV * HD
COLS = D + 2 * KVW
GROUP = HEADS // KV
NORM_EPS = 1e-05
SCALE = 2.0
ROPE_BASE = 500000.0
SROWS = 80
PACK = 256
bf16 = jnp.bfloat16
f32 = jnp.float32


def mm(a, b):
    return jnp.dot(a, b, preferred_element_type=f32)


def mm_t(a, b):
    return lax.dot_general(a, b, (((1,), (1,)), ((), ())), preferred_element_type=f32)


def t_mm(a, b):
    return lax.dot_general(a, b, (((0,), (0,)), ((), ())), preferred_element_type=f32)


class Links:
    def __init__(self):
        self.last = {}

    def move(self, a, axis, pairs, on=None):
        on = on or {"z": ("outer", "middle")}.get(axis, (axis,))
        before = [self.last[link] for link in on if link in self.last]
        if before:
            a = lax.optimization_barrier((a, *before))[0]
        out = lax.ppermute(a, axis, pairs)
        self.last.update({link: out for link in on})
        return out

    def swap(self, a, axis):
        return self.move(a, axis, [(0, 1), (1, 0)])

    def shift(self, a, k):
        nz = lax.axis_size("z")
        return self.move(a, "z", [(i, (i + k) % nz) for i in range(nz)])

    def slots(self):
        nz, z = lax.axis_size("z"), lax.axis_index("z")
        if nz == 4:
            low = z < 2
            return [z, z ^ 1, jnp.where(low, 2, 1), jnp.where(low, 3, 0)]
        return [lax.rem(z - k + nz, nz) for k in [0] + self.line_order()]

    def line_gather(self, block):
        z = lax.axis_index("z")
        if lax.axis_size("z") != 4:
            return [block] + [self.shift(block, k) for k in self.line_order()]
        ends, ends_out, middle = [(0, 1), (1, 0), (2, 3), (3, 2)], [(1, 0), (2, 3)], [(1, 2), (2, 1)]
        inner = (z == 1) | (z == 2)
        first = self.move(block, "z", ends, ("outer",))
        second = self.move(block, "z", middle, ("middle",))
        second_end = self.move(second, "z", ends_out, ("outer",))
        third = self.move(first, "z", middle, ("middle",))
        third_end = self.move(third, "z", ends_out, ("outer",))
        return [
            block,
            lambda *late: after(first, second),
            lambda *late: after(jnp.where(inner, second, second_end), third),
            lambda *late: jnp.where(inner, third, third_end),
        ]

    def line_scatter(self, parts, hold=()):
        if lax.axis_size("z") != 4:
            moved = [self.shift(parts[i + 1], -k) for i, k in enumerate(self.line_order())]
            return sum([m.astype(f32) for m in moved], parts[0].astype(f32))
        ends, ends_in, middle = [(0, 1), (1, 0), (2, 3), (3, 2)], [(0, 1), (3, 2)], [(1, 2), (2, 1)]
        add = lambda a, b: (a.astype(f32) + b.astype(f32)).astype(bf16)
        own, first, second, third = parts
        third_in = self.move(third, "z", ends_in, ("outer",))
        second_in = self.move(second, "z", ends_in, ("outer",))
        third_in = self.move(add(third, third_in), "z", middle, ("middle",))
        second_in = self.move(add(second, second_in), "z", middle, ("middle",))
        first_in = self.move(add(first, third_in), "z", ends, ("outer",))
        return own.astype(f32) + first_in.astype(f32) + second_in.astype(f32)

    def line_order(self):
        nz = lax.axis_size("z")
        return sorted(range(1, nz), key=lambda k: (min(k, nz - k), k))


def pick(a, i, dim):
    return lax.dynamic_index_in_dim(a, i, dim, False)


def after(a, *others):
    return lax.optimization_barrier((a,) + others)[0]


def by_owner(a):
    nz = lax.axis_size("z")
    z, x, c = lax.axis_index("z"), lax.axis_index("x"), lax.axis_index("c")
    width = a.shape[1] // (4 * nz)
    pieces = []
    for dc in range(2):
        for dx in range(2):
            for k in range(nz):
                at = (lax.rem(z - k + nz, nz) * 2 + (x ^ dx)) * 2 + (c ^ dc)
                pieces.append(lax.dynamic_slice_in_dim(a, at * width, width, 1))
    half = 2 * nz
    return jnp.concatenate(pieces[:half], axis=1), jnp.concatenate(pieces[half:], axis=1)


def core_product(links, mine, theirs, right):
    other = links.swap(t_mm(theirs, right).astype(bf16), "c")
    return lambda *late: (t_mm(mine, right) + after(other, *late).astype(f32)).astype(bf16)


def scatter_x(links, t):
    half = t.shape[0] // 2
    other = links.swap(t[half:], "x")
    return lambda *late: (t[:half].astype(f32) + after(other, *late).astype(f32)).astype(bf16)


def scatter_line(links, t):
    nz = lax.axis_size("z")
    mine, theirs = split_replica(t.reshape(nz, -1, t.shape[1]))
    other = links.swap(theirs, "r")

    def second(*late):
        half = (mine.astype(f32) + after(other, *late).astype(f32)).astype(bf16)
        moved = [links.shift(half[k], -k) for k in links.line_order()]

        def third(*late):
            own = sum([after(m, *late).astype(f32) for m in moved], half[0].astype(f32))
            own = own.astype(bf16)
            far = links.swap(own, "r")
            return lambda: join_replica(own, far)

        return third

    return second


def line_columns(links, weight):
    nz, z = lax.axis_size("z"), lax.axis_index("z")
    rows = weight.shape[0]
    wide = FF // nz
    parts = [None] * nz
    for k in [0] + links.line_order():
        to = lax.rem(z + k, nz)
        part = jnp.concatenate(
            [lax.dynamic_slice(weight, (0, g * FF + to * wide), (rows, wide)) for g in range(2)],
            axis=1,
        )
        parts[k] = links.shift(part, k) if k else part
    return parts


def core_columns(links, parts):
    c = lax.axis_index("c")
    loc = parts[0].shape[1] // 8

    def columns(core):
        return jnp.stack(
            [
                jnp.concatenate(
                    [
                        lax.dynamic_slice_in_dim(p, (4 * g + 2 * x + core) * loc, loc, 1)
                        for x in range(2)
                        for g in range(2)
                    ],
                    axis=1,
                )
                for p in parts
            ]
        )

    mine, theirs = columns(c), links.swap(columns(1 - c), "c")
    return jnp.stack([jnp.where(c == 0, mine, theirs), jnp.where(c == 0, theirs, mine)], axis=1)


def join_gate_up(near, near_other, far, far_other):
    nz = lax.axis_size("z")
    z, x, y = lax.axis_index("z"), lax.axis_index("x"), lax.axis_index("r")
    rows, wide = near.shape[2:]
    half = nz // 2

    def body(at_ref, *refs):
        out_ref, h = refs[-1], at_ref[2]
        k, d = pl.program_id(0), pl.program_id(1)
        cases = [(d == 0, refs[0], refs[1])]
        cases += [((d == 1) & (k // half == i), refs[2 + i], refs[4 + i]) for i in range(2)]
        for case, mine, other in cases:

            @pl.when(case)
            def _():
                for c in range(2):
                    out_ref[0, 0, c, pl.ds(h, 1)] = mine[0, c][None]
                    out_ref[0, 0, c, pl.ds(1 - h, 1)] = other[0, c][None]

    shape = (1, 2, rows, wide)
    block = pl.BlockSpec(shape, lambda k, d, at: (k, 0, 0, 0))
    pieces = [
        pl.BlockSpec(shape, lambda k, d, at, i=i: (jnp.clip(k - i * half, 0, half - 1), 0, 0, 0))
        for i in range(2)
    ]
    place = lambda k, d, at: (lax.rem(at[0] - k + nz, nz), at[1] ^ d, 0, 0, 0, 0)
    out = pl.pallas_call(
        body,
        out_shape=jax.ShapeDtypeStruct((nz, 2, 2, 2, rows, wide), bf16),
        grid_spec=pltpu.PrefetchScalarGridSpec(
            num_scalar_prefetch=1,
            grid=(nz, 2),
            in_specs=[block, block] + pieces + pieces,
            out_specs=pl.BlockSpec((1, 1, 2, 2, rows, wide), place),
        ),
        cost_estimate=pl.CostEstimate(
            flops=0, bytes_accessed=16 * near.size, transcendentals=0
        ),
        name="join_gate_up",
    )(jnp.stack([z, x, y]).astype(jnp.int32), near, near_other, *far, *far_other)
    return out.reshape(-1, wide)


def split_replica(t):
    y = lax.axis_index("r")
    t = t.reshape(t.shape[0], 2, -1, t.shape[2])
    return pick(t, y, 1), pick(t, 1 - y, 1)


def join_replica(mine, other):
    y = lax.axis_index("r")
    return jnp.concatenate(
        [jnp.where(y == 0, mine, other), jnp.where(y == 0, other, mine)], axis=0
    ).astype(f32)


def whole_rows(halves):
    nz = lax.axis_size("z")
    rows, cols = halves.shape[1:]
    wide = cols // (4 * nz)

    def body(in_ref, out_ref):
        out_ref[...] = in_ref[...].astype(f32)

    out = pl.pallas_call(
        body,
        out_shape=jax.ShapeDtypeStruct(halves.shape, f32),
        grid=(2, 2 * nz),
        in_specs=[pl.BlockSpec((2, rows, wide), lambda g, j: (0, 0, 2 * j + g))],
        out_specs=pl.BlockSpec((2, rows, wide), lambda g, j: (0, 0, g * 2 * nz + j)),
        cost_estimate=pl.CostEstimate(
            flops=0, bytes_accessed=12 * rows * cols, transcendentals=0
        ),
        name="whole_rows",
    )(halves)
    return out.reshape(2 * rows, cols)


def split_core(links, t, *late):
    c = lax.axis_index("c")
    t = t.reshape(t.shape[0], 2, -1, t.shape[2])
    loc = FF // (4 * lax.axis_size("z"))
    mine, theirs = pick(t, c, 1), after(links.swap(pick(t, 1 - c, 1), "c"), *late)
    first, second = jnp.where(c == 0, mine, theirs), jnp.where(c == 0, theirs, mine)
    pieces = []
    for j in range(t.shape[3] // loc):
        pieces += [first[:, :, j * loc : (j + 1) * loc], second[:, :, j * loc : (j + 1) * loc]]
    return jnp.concatenate(pieces, axis=2)


def split_line(links, t):
    nz, z = lax.axis_size("z"), lax.axis_index("z")
    parts = [pick(t, lax.rem(z + k, nz), 0) for k in range(nz)]
    for k in links.line_order():
        parts[k] = links.shift(parts[k], k)
    return parts


def join_line(parts):
    nz, z = lax.axis_size("z"), lax.axis_index("z")
    rows, wide = parts[0].shape
    out = jnp.zeros((rows, nz * wide), bf16)
    for k in range(nz):
        at = lax.rem(z - k + nz, nz)
        out = lax.dynamic_update_slice(out, parts[k], (0, at * wide))
    return out


def turn(v, cosine, sine):
    lane = lax.broadcasted_iota(jnp.int32, v.shape, 1)
    low_half = (lane & 63) < 32
    other = jnp.where(low_half, pltpu.roll(v, 96, 1), pltpu.roll(v, 32, 1))
    return v * cosine + other * sine


def rope_kernel(v_ref, cos_ref, sin_ref, o_ref, *, turned):
    j = pl.program_id(0)

    @pl.when(j < turned)
    def _():
        for s in range(4):
            at = slice(s * 128, (s + 1) * 128)
            o_ref[:, at] = turn(v_ref[:, at], cos_ref[...], sin_ref[...]).astype(bf16)

    @pl.when(j >= turned)
    def _():
        o_ref[...] = v_ref[...].astype(bf16)


def rope(values, cosine, sine, turned):
    rows, cols = values.shape
    full = pl.BlockSpec((rows, 128), lambda j: (0, 0))
    return pl.pallas_call(
        lambda *refs: rope_kernel(*refs, turned=turned),
        out_shape=jax.ShapeDtypeStruct((rows, cols), bf16),
        grid=(cols // 512,),
        in_specs=[pl.BlockSpec((rows, 512), lambda j: (0, j)), full, full],
        out_specs=pl.BlockSpec((rows, 512), lambda j: (0, j)),
        cost_estimate=pl.CostEstimate(
            flops=6 * rows * cols, bytes_accessed=6 * rows * cols, transcendentals=0
        ),
        name="rope",
    )(values, cosine, sine)


def halves(shape):
    return lax.broadcasted_iota(jnp.int32, shape, 1) < 64


def feature(z2):
    first = halves(z2.shape)
    top = jnp.max(jnp.where(first, z2, -jnp.inf), axis=1, keepdims=True)
    low = jnp.max(jnp.where(first, -jnp.inf, z2), axis=1, keepdims=True)
    e = jnp.exp(z2 - jnp.where(first, top, low))
    s1 = jnp.sum(jnp.where(first, e, 0.0), axis=1, keepdims=True)
    s2 = jnp.sum(jnp.where(first, 0.0, e), axis=1, keepdims=True)
    return e * jnp.where(first, 1.0 / s1, 1.0 / s2)


def feature_grad(phi, dphi):
    first = halves(phi.shape)
    t = phi * dphi
    s1 = jnp.sum(jnp.where(first, t, 0.0), axis=1, keepdims=True)
    s2 = jnp.sum(jnp.where(first, 0.0, t), axis=1, keepdims=True)
    return t - phi * jnp.where(first, s1, s2)


def with_one(v):
    wide = jnp.concatenate([v, jnp.zeros_like(v)], axis=1)
    lane = lax.broadcasted_iota(jnp.int32, wide.shape, 1)
    return jnp.where(lane == 64, jnp.ones_like(wide), wide)


def tile(a):
    return jnp.concatenate([a] * GROUP, axis=0)


def attention_masks(row_ref, col_ref):
    rows, extent = row_ref.shape[0], col_ref.shape[1]
    offset = (
        lax.broadcasted_iota(jnp.int32, (rows, extent), 0)
        + WINDOW
        - lax.broadcasted_iota(jnp.int32, (rows, extent), 1)
    )
    same = row_ref[:, 0:1] == col_ref[0:1, :]
    live = col_ref[1:2, :] > 0
    window = (offset >= 0) & (offset < WINDOW) & same & (live | (offset == 0))
    far = (offset >= WINDOW) & same & live
    return tile(window.astype(f32)) > 0, tile(far.astype(f32)) > 0


def query_heads(ref, hh):
    return [ref[:, (hh * GROUP + i) * HD : (hh * GROUP + i + 1) * HD] for i in range(GROUP)]


def head_forward(q_ref, k, wq_ref, wk, hh, window, far):
    qs = query_heads(q_ref, hh)
    q4 = jnp.concatenate(qs, axis=0)
    s = jnp.where(window, mm_t(q4, k) * 0.125, -1e30)
    top = jnp.max(s, axis=1, keepdims=True)
    p = jnp.exp(s - top)
    e = jnp.exp(-top)
    phi = feature(
        jnp.concatenate([mm(qs[i], wq_ref[hh * GROUP + i]) for i in range(GROUP)], axis=0)
    )
    phik = feature(mm(k, wk))
    phi_b, phik_b = phi.astype(bf16), phik.astype(bf16)
    a_b = (p + e * jnp.where(far, mm_t(phi_b, phik_b), 0.0)).astype(bf16)
    return qs, q4, p, e, phi, phi_b, phik, phik_b, a_b


def full_state(st):
    return jnp.concatenate([st, jnp.zeros((128 - SROWS, 128), bf16)], axis=0)


def attend_kernel(q_ref, k_ref, v_ref, wq_ref, wk_ref, row_ref, col_ref, nd_ref, phi_ref):
    window, far = attention_masks(row_ref, col_ref)
    use = tile(row_ref[:, 1:2])
    for hh in range(2):
        at = slice(hh * HD, (hh + 1) * HD)
        _, _, _, e, phi, _, _, _, a_b = head_forward(
            q_ref, k_ref[:, at], wq_ref, wk_ref[hh], hh, window, far
        )
        nd_ref[0, hh] = mm(a_b, with_one(v_ref[:, at]))
        phi_ref[0, hh] = ((e * use) * phi).astype(bf16)


def finish_kernel(nd_ref, phi_ref, st_ref, row_ref, nd_out, o_ref):
    rows = row_ref.shape[0]
    live = tile(row_ref[:, 2:3])
    for hh in range(2):
        nd = nd_ref[0, hh] + mm_t(phi_ref[0, hh], full_state(st_ref[0, hh]))
        nd_out[0, hh] = nd
        out = (nd[:, :HD] * (live / nd[:, HD : HD + 1])).astype(bf16)
        for i in range(GROUP):
            j = hh * GROUP + i
            o_ref[:, j * HD : (j + 1) * HD] = out[i * rows : (i + 1) * rows]


def numerator_grad(do_ref, nd, live, hh):
    do4 = jnp.concatenate(query_heads(do_ref, hh), axis=0)
    inv = 1.0 / nd[:, HD : HD + 1]
    dnum = do4 * (live * inv)
    dden = -jnp.sum(dnum * nd[:, :HD], axis=1, keepdims=True) * inv
    dn = jnp.concatenate([dnum, jnp.zeros_like(dnum)], axis=1)
    lane = lax.broadcasted_iota(jnp.int32, dn.shape, 1)
    return jnp.where(lane == HD, dden, dn)


def state_grad_kernel(do_ref, nd_ref, phi_ref, row_ref, dst_ref):
    live = tile(row_ref[:, 2:3])
    for hh in range(2):
        dn = numerator_grad(do_ref, nd_ref[0, hh], live, hh)
        dst_ref[0, hh] = t_mm(dn.astype(bf16), phi_ref[0, hh])[:SROWS].astype(bf16)


def attend_back_kernel(
    q_ref, k_ref, v_ref, st_ref, wq_ref, wk_ref, row_ref, col_ref, do_ref, nd_ref, cos_ref,
    sin_ref, dq_ref, dk_ref, dv_ref, dwq_ref, dwk_ref, scr_ref,
):
    rows = q_ref.shape[0]
    window, far = attention_masks(row_ref, col_ref)
    use, live = tile(row_ref[:, 1:2]), tile(row_ref[:, 2:3])
    for hh in range(2):
        at = slice(hh * HD, (hh + 1) * HD)
        k = k_ref[:, at]
        qs, q4, p, e, phi, phi_b, phik, phik_b, a_b = head_forward(
            q_ref, k, wq_ref, wk_ref[hh], hh, window, far
        )
        dn = numerator_grad(do_ref, nd_ref[0, hh], live, hh)
        dn_b = dn.astype(bf16)
        en_b = ((e * use) * dn).astype(bf16)
        da = mm_t(dn_b, with_one(v_ref[:, at]))
        ds_b = (da * p * 0.125).astype(bf16)
        dl_b = jnp.where(far, e * da, 0.0).astype(bf16)
        dv_ref[:, at] = t_mm(a_b, dn_b)[:, :HD]
        dphi = mm(dl_b, phik_b) + mm(en_b, full_state(st_ref[0, hh]))
        dz = feature_grad(phi, dphi).astype(bf16)
        dzk = feature_grad(phik, t_mm(dl_b, phi_b)).astype(bf16)
        dq4 = mm(ds_b, k)
        dk_ref[:, at] = t_mm(ds_b, q4) + mm_t(dzk, wk_ref[hh])
        dwk_ref[0, hh] = t_mm(k, dzk)
        for i in range(GROUP):
            j = hh * GROUP + i
            dzi = dz[i * rows : (i + 1) * rows]
            scr_ref[:, j * HD : (j + 1) * HD] = dq4[i * rows : (i + 1) * rows] + mm_t(
                dzi, wq_ref[j]
            )
            dwq_ref[0, j] = t_mm(qs[i], dzi)
    for s in range(4):
        at = slice(s * 128, (s + 1) * 128)
        dq_ref[:, at] = turn(scr_ref[:, at], cos_ref[...], -sin_ref[...]).astype(bf16)


def state_kernel(k_ref, v_ref, wk_ref, row_ref, add_ref):
    rows = row_ref.shape[0]
    chosen = row_ref[:, 3:4]
    for hh in range(2):
        at = slice(hh * HD, (hh + 1) * HD)
        phik = (feature(mm(k_ref[:rows, at], wk_ref[hh])) * chosen).astype(bf16)
        add_ref[0, hh] = t_mm(with_one(v_ref[:rows, at]), phik)[:SROWS].astype(bf16)


def state_back_kernel(
    k_ref, v_ref, wk_ref, row_ref, dadd_ref, dk_in, dv_in, dk_ref, dv_ref, dwk_ref
):
    rows = row_ref.shape[0]
    chosen = row_ref[:, 3:4]
    dk_ref[rows:] = dk_in[rows:]
    dv_ref[rows:] = dv_in[rows:]
    for hh in range(2):
        at = slice(hh * HD, (hh + 1) * HD)
        k = k_ref[:rows, at]
        phik = feature(mm(k, wk_ref[hh]))
        dadd = full_state(dadd_ref[0, hh])
        dphi = mm(with_one(v_ref[:rows, at]), dadd) * chosen
        dz = feature_grad(phik, dphi).astype(bf16)
        dk_ref[:rows, at] = dk_in[:rows, at] + mm_t(dz, wk_ref[hh])
        dv_ref[:rows, at] = dv_in[:rows, at] + mm_t((phik * chosen).astype(bf16), dadd)[:, :HD]
        dwk_ref[0, hh] = t_mm(k, dz)


def call(kernel, micros, rows, extent, ins, outs, args, flops, scratch=(), only=None, into=()):
    base, count, skip, pairs = (0, micros, 0, 4) if only is None else (only[0], 1, only[1], only[2])
    block = dict(
        q=((rows, 512), lambda m, j: (m + base, j + skip)),
        k=((extent, 128), lambda m, j: (m + base, j + skip)),
        v=((extent, 128), lambda m, j: (m + base, 4 + j + skip)),
        st=((1, 2, SROWS, 128), lambda m, j: (m + base, j + skip, 0, 0)),
        nd=((1, 2, GROUP * rows, 128), lambda m, j: (m + base, j + skip, 0, 0)),
        wq=((8, HD, 128), lambda m, j: (j + skip, 0, 0)),
        wk=((2, HD, 128), lambda m, j: (j + skip, 0, 0)),
        dwq=((1, 8, HD, 128), lambda m, j: (m + base, j + skip, 0, 0)),
        dwk=((1, 2, HD, 128), lambda m, j: (m + base, j + skip, 0, 0)),
        row=((rows, 128), lambda m, j: (m + base, 0)),
        col=((8, extent), lambda m, j: (m + base, 0)),
    )
    shapes = dict(
        q=(micros * rows, D),
        k=(micros * extent, KVW),
        st=(micros, KV, SROWS, 128),
        nd=(micros, KV, GROUP * rows, 128),
        dwq=(micros, HEADS, HD, 128),
        dwk=(micros, KV, HD, 128),
    )
    spec = lambda name: pl.BlockSpec(*block[name])
    size = lambda a: a.size * a.dtype.itemsize
    out_shape = tuple(jax.ShapeDtypeStruct(shapes[name], kind) for name, kind in outs)

    def body(*refs):
        kernel(*refs[: len(ins)], *refs[len(ins) + len(into) :])

    return pl.pallas_call(
        body,
        out_shape=out_shape,
        grid=(count, pairs),
        in_specs=[spec(name) for name in ins] + [pl.BlockSpec(memory_space=pl.ANY)] * len(into),
        out_specs=tuple(spec(name) for name, _ in outs),
        scratch_shapes=scratch,
        input_output_aliases={len(ins) + i: i for i in range(len(into))},
        compiler_params=pltpu.CompilerParams(vmem_limit_bytes=48 << 20),
        cost_estimate=pl.CostEstimate(
            flops=flops * count * pairs // (4 * micros),
            bytes_accessed=(sum(size(a) for a in args) + sum(size(a) for a in out_shape))
            * (count * pairs)
            // (4 * micros),
            transcendentals=count * pairs * HEADS * rows * extent // 4,
        ),
        name=kernel.__name__,
    )(*args, *into)


def ffn_kernel(at_ref, own_ref, other_ref, pair_ref, w_ref, wd_ref, *refs):
    act_ref, dgu_ref, n2_ref, df_ref, mine_ref, theirs_ref, out_ref, dn_acc, out_acc = refs[-9:]
    f, rows, width = pl.program_id(0), own_ref.shape[0], wd_ref.shape[0]
    here = pl.ds(pl.multiple_of(at_ref[1] * rows, rows), rows)
    there = pl.ds(pl.multiple_of((1 - at_ref[1]) * rows, rows), rows)

    @pl.when(f == 0)
    def _():
        n2_ref[here] = own_ref[...]
        n2_ref[there] = other_ref[...]
        df_ref[:rows] = pair_ref[0, 0]
        df_ref[rows:] = pair_ref[0, 1]

    gate_up = mm(n2_ref[...], w_ref[...])
    gate, up = gate_up[:, :width], gate_up[:, width:]
    d_act = mm_t(df_ref[...], wd_ref[...])
    sig = 1.0 / (1.0 + jnp.exp(-gate))
    swish = gate * sig
    acted = (swish * up).astype(bf16)
    d_gate = (d_act * up * (sig * (1.0 + gate * (1.0 - sig)))).astype(bf16)
    d_up = (d_act * swish).astype(bf16)
    act_ref[...] = acted
    d_gu = jnp.concatenate([d_gate, d_up], axis=1)
    dgu_ref[...] = d_gu
    d_n2 = mm_t(d_gu, w_ref[...])
    out = mm(acted, wd_ref[...])

    @pl.when(f == 0)
    def _():
        dn_acc[...] = d_n2
        out_acc[...] = out

    @pl.when(f > 0)
    def _():
        dn_acc[...] += d_n2
        out_acc[...] += out

    @pl.when(f == pl.num_programs(0) - 1)
    def _():
        mine_ref[...] = dn_acc[here]
        theirs_ref[...] = dn_acc[there].astype(bf16)
        out_ref[0, 0] = out_acc[:rows].astype(bf16)
        out_ref[0, 1] = out_acc[rows:].astype(bf16)


def ffn_chunk(k, at, own, other, df_all, wgu, wd, held):
    rows = own.shape[0]
    total, half = df_all.shape[0] * df_all.shape[1] * rows, wd.shape[0]
    width = half // 2
    tiles = half // width
    tokens = pl.BlockSpec((rows, D), lambda f, a: (0, 0))
    chunk = pl.BlockSpec((2 * rows, D), lambda f, a: (k, 0))
    hidden = pl.BlockSpec((2 * rows, width), lambda f, a: (k, f))
    pair = pl.BlockSpec((1, 2, rows, D), lambda f, a: (a[0], 0, 0, 0))
    whole = (total, D)
    outs = [((total, half), bf16), ((total, 2 * half), bf16)] + [(whole, bf16)] * 2
    outs += [((rows, D), f32), ((rows, D), bf16), (df_all.shape, bf16)]
    return pl.pallas_call(
        ffn_kernel,
        out_shape=tuple(jax.ShapeDtypeStruct(a, b) for a, b in outs),
        grid_spec=pltpu.PrefetchScalarGridSpec(
            num_scalar_prefetch=1,
            grid=(tiles,),
            in_specs=[
                tokens,
                tokens,
                pair,
                pl.BlockSpec((D, 2 * width), lambda f, a: (0, f)),
                pl.BlockSpec((width, D), lambda f, a: (f, 0)),
            ]
            + [pl.BlockSpec(memory_space=pl.ANY)] * len(held),
            out_specs=(
                hidden, pl.BlockSpec((2 * rows, 2 * width), lambda f, a: (k, f)), chunk, chunk,
                tokens, tokens,
                pair,
            ),
            scratch_shapes=[pltpu.VMEM((2 * rows, D), f32)] * 2,
        ),
        input_output_aliases={6 + i: (i if i < 4 else 6) for i in range(len(held))},
        compiler_params=pltpu.CompilerParams(vmem_limit_bytes=56 << 20),
        cost_estimate=pl.CostEstimate(
            flops=24 * rows * D * half,
            bytes_accessed=6 * D * half + 40 * rows * D,
            transcendentals=2 * rows * half,
        ),
        name="ffn_chunk",
    )(at, own, other, df_all, wgu, wd, *held)


def weigh(flag, a):
    return jnp.where(flag[:, None, None, None], a.astype(f32), 0.0)


def entering(links, add, tags, reach):
    nz = lax.axis_size("z")
    z, x, c = lax.axis_index("z"), lax.axis_index("x"), lax.axis_index("c")
    p = (z * 2 + x) * 2 + c
    tag = lambda i: pick(tags, jnp.clip(i, 0, 4 * nz - 1), 1)
    prev = tag(p - 1)
    chip = (z * 2 + x) * 2
    other = links.swap(add, "c")
    other = after(other, (yield))
    one = tag(chip) == tag(chip + 1)
    chip_sum = (weigh((c == 1) | one, add) + weigh((c == 0) | one, other)).astype(bf16)
    side = links.swap(chip_sum, "x")
    side = after(side, (yield))
    one = tag(z * 4 + 1) == tag(z * 4 + 3)
    layer = (weigh((x == 1) | one, chip_sum) + weigh((x == 0) | one, side)).astype(bf16)
    state = weigh((c == 1) & (prev >= 0), other) + weigh((x == 1) & (tag(z * 4 + 1) == prev), side)
    got = [
        links.move(layer, "z", [(i, i + hop) for i in range(nz - hop)])
        for hop in range(1, min(reach, nz - 1) + 1)
    ]
    late = yield
    for hop, far in enumerate(got, 1):
        state += weigh((z >= hop) & (tag((z - hop) * 4 + 3) == prev), after(far, late))
    yield state.astype(bf16)


def leaving(links, dstate, tags, reach):
    nz = lax.axis_size("z")
    z, x, c = lax.axis_index("z"), lax.axis_index("x"), lax.axis_index("c")
    p = (z * 2 + x) * 2 + c
    tag = lambda i: pick(tags, jnp.clip(i, 0, 4 * nz - 1), 1)
    from_tag = lambda i: jnp.where(i > 0, tag(i - 1), -1)
    own = tag(p)
    chip = (z * 2 + x) * 2
    other = links.swap(dstate, "c")
    other = after(other, (yield))
    one = from_tag(chip) == from_tag(chip + 1)
    chip_sum = (weigh((c == 0) | one, dstate) + weigh((c == 1) | one, other)).astype(bf16)
    side = links.swap(chip_sum, "x")
    side = after(side, (yield))
    one = from_tag(z * 4) == from_tag(z * 4 + 2)
    layer = (weigh((x == 0) | one, chip_sum) + weigh((x == 1) | one, side)).astype(bf16)
    total = weigh((c == 0) & (own >= 0), other) + weigh(
        (x == 0) & (from_tag(z * 4 + 2) == own), side
    )
    got = [
        links.move(layer, "z", [(i, i - hop) for i in range(hop, nz)])
        for hop in range(1, min(reach, nz - 1) + 1)
    ]
    late = yield
    for hop, far in enumerate(got, 1):
        total += weigh((z + hop < nz) & (from_tag((z + hop) * 4) == own), after(far, late))
    yield total.astype(bf16)


def per_device(
    inputs, cotangent, lengths, padding, gain_attn_own, wqkv_own, adown_own, aup_own, wout_own,
    odown_own, oup_own, featq_own, featk_own, gain_ffn_own, wgu_own, wd_own,
):
    nz = lax.axis_size("z")
    n = 4 * nz
    z, x, c = lax.axis_index("z"), lax.axis_index("x"), lax.axis_index("c")
    place_own = (z * 2 + x) * 2 + c
    micros, rows = inputs.shape[1], inputs.shape[2]
    both = micros * rows
    extent = rows + WINDOW
    reach = -(-MAXLEN // (4 * rows))
    everyone = ("z", "x", "c")
    chain = (everyone, [(i, i + 1) for i in range(n - 1)])
    unchain = (everyone, [(i, i - 1) for i in range(1, n)])
    r = D // n

    pack = jnp.concatenate(
        [
            gain_attn_own[:, None], adown_own, odown_own, oup_own.T, featq_own,
            gain_ffn_own[:, None], aup_own.reshape(r, 12), featk_own.reshape(r, 16),
        ],
        axis=1,
    )
    pack = jnp.pad(pack, ((0, 0), (0, PACK - pack.shape[1])))
    links = Links()
    live_all = padding[0].astype(bf16)
    halo_live = lax.ppermute(live_all[:, rows - WINDOW :], *chain)
    first = lax.all_gather(
        jnp.concatenate([wqkv_own, wout_own, pack], axis=1), everyone, axis=0, tiled=True
    )
    wqkv, wout, small = first[:, :COLS], first[:, COLS : COLS + D], first[:, COLS + D :]
    cot = cotangent[0].reshape(both, D)
    y = lax.axis_index("r")
    wgu_half = lax.dynamic_slice_in_dim(wgu_own, y * (r // 2), r // 2, 0)
    wgu_near = core_columns(links, line_columns(links, wgu_half))
    wgu_near_other = links.swap(wgu_near, "r")
    small, wgu_send = lax.optimization_barrier((small, wgu_near, wgu_near_other))[:2]
    wgu_far = [links.swap(wgu_send[: nz // 2], "x")]
    gain_one = small[:, 0].astype(f32)[None]
    adown = small[:, 1:25]
    odown = small[:, 25:33]
    oup_t = small[:, 33:41]
    featq = small[:, 41:105].reshape(HEADS, HD, HD)
    gain_two = small[:, 105].astype(f32)[None]
    aup = small[:, 106:118].reshape(n, RANK, COLS // n).transpose(1, 0, 2).reshape(RANK, COLS)
    featk = small[:, 118:134].reshape(KV, HD, HD)
    wq2 = jnp.concatenate([featq, -featq], axis=2)
    wk2 = jnp.concatenate([featk, -featk], axis=2)
    column = jnp.arange(COLS)[None]
    owner = jnp.where(column < D, 0, jnp.where(column < D + KVW, 1, 2))
    aup_wide = jnp.concatenate(
        [jnp.where(owner == t, aup, jnp.zeros_like(aup)) for t in range(3)], axis=0
    )

    doc_lengths = lengths[0]
    ends = jnp.cumsum(doc_lengths, axis=1)
    places = place_own * rows - WINDOW + jnp.arange(extent, dtype=jnp.int32)
    done = ends[:, None, :] <= places[None, :, None]
    seg_ext = jnp.sum(done.astype(jnp.int32), axis=2)
    pos = places[None] - jnp.sum(jnp.where(done, doc_lengths[:, None, :], 0), axis=2)
    pos = pos[:, WINDOW:].reshape(both)
    edges = jnp.arange(n, dtype=jnp.int32) * rows + (rows - WINDOW - 1)
    tags = jnp.sum((ends[:, None, :] <= edges[None, :, None]).astype(jnp.int32), axis=2)
    live_ext = jnp.concatenate([halo_live, live_all], axis=1).astype(f32)
    prev_tag = jnp.where(place_own > 0, pick(tags, jnp.maximum(place_own - 1, 0), 1), -1)
    own_tag = pick(tags, place_own, 1)
    seg_own = seg_ext[:, WINDOW:]
    info = jnp.stack(
        [
            seg_own.astype(f32),
            (seg_own == prev_tag[:, None]).astype(f32),
            live_ext[:, WINDOW:],
            ((seg_ext[:, :rows] == own_tag[:, None]) & (live_ext[:, :rows] > 0)).astype(f32),
        ],
        axis=2,
    ).reshape(both, 4)
    rowinfo = jnp.pad(info, ((0, 0), (0, 124)))
    colinfo = jnp.pad(
        jnp.stack([seg_ext.astype(f32), live_ext], axis=1), ((0, 0), (0, 6), (0, 0))
    ).reshape(micros * 8, extent)
    lane = jnp.arange(128)
    frequency = ROPE_BASE ** (-((lane % 32).astype(f32) * 2.0) / HD)
    angles = pos.astype(f32)[:, None] * frequency[None, :]
    cosine = jnp.cos(angles)
    sine = jnp.where((lane % 64 < 32)[None], -1.0, 1.0) * jnp.sin(angles)

    act = inputs[0].reshape(both, D).astype(f32)
    inv_one = lax.rsqrt(jnp.mean(act * act, axis=-1, keepdims=True) + NORM_EPS)
    n1 = (act * inv_one * gain_one).astype(bf16)
    adapt = mm(n1, adown).astype(bf16)
    projected = mm(n1, wqkv) + SCALE * mm(adapt, aup_wide)
    qkv = rope(projected, cosine, sine, 5)
    kv = qkv[:, D:].reshape(micros, rows, 2 * KVW)
    crossing = ("x", "outer", "middle", "c")
    halo = links.move(kv[:, rows - WINDOW :], *chain, crossing)
    kv_ext = jnp.concatenate([halo, kv], axis=1).reshape(micros * extent, 2 * KVW)
    launch = lambda kernel, ins, outs, args, work, **k: call(
        kernel, micros, rows, extent, ins, outs, args, micros * HEADS * rows * work, **k
    )
    (add,) = launch(
        state_kernel, ("k", "v", "wk", "row"), [("st", bf16)], (kv_ext, kv_ext, wk2, rowinfo), 8192
    )
    df_all = lax.all_gather(after(cot, small), ("z", "c"), axis=0, tiled=True)
    df_all = df_all.reshape(nz, 2, both, D)
    parts = [(m, j, 2) for m in range(micros) for j in (0, 2)]
    travel = entering(links, add, tags, reach)
    next(travel)
    wgu_far[0], wk2_late = lax.optimization_barrier((wgu_far[0], wk2, add))[:2]
    wgu_far_other = [links.swap(wgu_far[0], "r")]
    local = ()
    for i, part in enumerate(parts):
        local = launch(
            attend_kernel,
            ("q", "k", "v", "wq", "wk", "row", "col"),
            [("nd", f32), ("nd", bf16)],
            (qkv, kv_ext, kv_ext, wq2, wk2_late, rowinfo, colinfo),
            1000 * extent,
            only=part,
            into=local,
        )
        if i == 0:
            travel.send(local[1])
            wgu_far.append(links.swap(wgu_near[nz // 2 :], "x"))
            wd_other = links.swap(wd_own, "x")
        elif i == 1:
            travel.send(local[1])
        elif i == 2:
            state = travel.send(local[1])
            wk2_late = after(wk2_late, state)
    nd, phi = local
    wgu_far[1], nd = lax.optimization_barrier((wgu_far[1], nd, wgu_far_other[0]))[:2]
    wgu_far_other.append(links.swap(wgu_far[1], "r"))
    nd, attn = launch(
        finish_kernel,
        ("nd", "nd", "st", "row"),
        [("nd", f32), ("q", bf16)],
        (nd, phi, state, rowinfo),
        32768,
    )
    adapt_out = mm(attn, odown).astype(bf16)
    hidden = act + (mm(attn, wout) + SCALE * mm_t(adapt_out, oup_t))
    inv_two = lax.rsqrt(jnp.mean(hidden * hidden, axis=-1, keepdims=True) + NORM_EPS)
    n2 = (hidden * inv_two * gain_two).astype(bf16)

    half = 2 * FF // n
    loc = half // 2
    n2_parts = links.line_gather(n2)
    late = lambda a: after(a, attn)
    wgu = join_gate_up(*[late(a) for a in (wgu_near, wgu_near_other)], wgu_far, [late(a) for a in wgu_far_other])
    wd = jnp.concatenate(
        [jnp.where(x == 0, wd_own, wd_other), jnp.where(x == 0, wd_other, wd_own)], axis=0
    )
    returned, held = [], ()
    for i, (place, part) in enumerate(zip(links.slots(), n2_parts)):
        at = jnp.stack([place, c]).astype(jnp.int32)
        part = part() if callable(part) else part
        if i:
            part = after(part, held[0])
        result = ffn_chunk(i, at, part, links.swap(part, "c"), df_all, wgu, wd, held)
        held = result[:4] + result[6:]
        d_n2_i = result[4] + links.swap(result[5], "c").astype(f32)
        returned.append(d_n2_i.astype(bf16) if i else d_n2_i)
    acted, d_gu, n2_all, df_held, out_parts = held
    d_n2 = links.line_scatter(returned)
    g_wgu = t_mm(n2_all, d_gu).astype(bf16)
    g_wd = t_mm(acted, df_held).astype(bf16)
    d_n2 = after(d_n2, g_wgu, g_wd)
    plus = lambda a, b: (a.astype(f32) + b.astype(f32)).astype(bf16)

    def replica_sum(g):
        halves = g.reshape(g.shape[0], 2, -1, g.shape[2]).transpose(1, 0, 2, 3)
        return lax.psum_scatter(halves, "r", scatter_dimension=0, tiled=False)

    def x_parts(t):
        return pick(t, x, 1), pick(t, 1 - x, 1)

    g_wgu = replica_sum(g_wgu.reshape(n, r, 2 * half))
    out_sum = lax.psum_scatter(
        after(out_parts, d_n2).reshape(-1, D), ("z", "c"), scatter_dimension=0, tiled=True
    )
    g_wd = replica_sum(after(g_wd, out_sum).reshape(2, loc, D))

    d_hidden = (
        cot.astype(f32)
        + gain_two * inv_two * d_n2
        - hidden * inv_two**3 * jnp.mean(hidden * gain_two * d_n2, axis=-1, keepdims=True)
    )
    d_branch = d_hidden.astype(bf16)
    d_adapt_out = (SCALE * mm(d_branch, oup_t)).astype(bf16)
    d_attn = mm_t(d_branch, wout) + mm_t(d_adapt_out, odown)
    (dst,) = launch(
        state_grad_kernel,
        ("q", "nd", "nd", "row"),
        [("st", bf16)],
        (d_attn, nd, phi, rowinfo),
        32768,
    )
    attn_owner, n1_owner = by_owner(attn), by_owner(n1)
    travel = leaving(links, dst, tags, reach)
    next(travel)
    wout_core = core_product(links, *attn_owner, d_branch)
    grads = ()
    d_attn_late = d_attn
    for i, part in enumerate(parts):
        grads = launch(
            attend_back_kernel,
            ("q", "k", "v", "st", "wq", "wk", "row", "col", "q", "nd", "row", "row"),
            [("q", bf16), ("k", f32), ("k", f32), ("dwq", f32), ("dwk", f32)],
            (qkv, kv_ext, kv_ext, state, wq2, wk2, rowinfo, colinfo, d_attn_late, nd, cosine, sine),
            2000 * extent,
            scratch=[pltpu.VMEM((rows, 512), f32)],
            only=part,
            into=grads,
        )
        done = grads[0]
        if i == 0:
            travel.send(done)
            gu_mine, gu_theirs = x_parts(after(g_wgu, done).reshape(nz, 2, r, 2 * half))
            gu_side = links.swap(gu_theirs, "x")
            wout_x = scatter_x(links, wout_core(done))
        elif i == 1:
            travel.send(done)
        elif i == 2:
            dadd = travel.send(done)
            d_attn_late = after(d_attn_late, dadd, out_sum)
    dq, dk, dv, dwq, dwk = grads
    gu_rows = split_core(links, plus(gu_mine, after(gu_side, dq)))
    wout_line = scatter_line(links, wout_x(dq))
    q_core = core_product(links, *n1_owner, dq)
    dk, dv, dwk_more = launch(
        state_back_kernel,
        ("k", "v", "wk", "row", "st", "k", "k"),
        [("k", f32), ("k", f32), ("dwk", f32)],
        (kv_ext, kv_ext, wk2, rowinfo, dadd, dk, dv),
        16384,
    )
    d_kv = jnp.concatenate([dk, dv], axis=1).reshape(micros, extent, 2 * KVW)
    sent = links.move(d_kv[:, :WINDOW].astype(bf16), *unchain, crossing)
    q_sum, gu_rows, sent = lax.optimization_barrier((q_core(dadd), gu_rows, sent))
    q_x = scatter_x(links, q_sum)
    gu_line = split_line(links, gu_rows)
    wout_line = wout_line(dadd, sent)
    sent = sent.astype(f32)
    d_kv = jnp.concatenate([d_kv[:, WINDOW:rows], d_kv[:, rows:] + sent], axis=1)
    d_kv = rope(d_kv.reshape(both, 2 * KVW), cosine, -sine, 1)
    kv_sum = core_product(links, *n1_owner, d_kv)()
    d_proj = jnp.concatenate([dq, d_kv], axis=1)
    d_adapt = (SCALE * mm_t(d_proj, aup_wide)).astype(bf16)
    d_n1 = mm_t(d_proj, wqkv) + mm_t(d_adapt, adown)
    g_gain_one = jnp.sum(d_n1 * act * inv_one, axis=0)
    grad_inputs = (
        d_hidden
        + gain_one * inv_one * d_n1
        - act * inv_one**3 * jnp.mean(act * gain_one * d_n1, axis=-1, keepdims=True)
    ).astype(bf16)
    g_adown = t_mm(n1, d_adapt)
    wide = SCALE * t_mm(adapt, d_proj)
    g_aup = jnp.where(owner == 0, wide[:8], jnp.where(owner == 1, wide[8:16], wide[16:24]))
    g_odown = t_mm(attn, d_adapt_out)
    g_oup_t = SCALE * t_mm(d_branch, adapt_out)
    fold = lambda a: a[:, :, :HD] - a[:, :, HD:]
    g_featq = fold(jnp.sum(dwq, axis=0)).reshape(D, HD)
    g_featk = fold(jnp.sum(dwk + dwk_more, axis=0))
    g_gain_two = jnp.sum(d_n2 * hidden * inv_two, axis=0)
    g_pack = jnp.concatenate(
        [
            g_gain_one[:, None], g_adown, g_odown, g_oup_t, g_featq, g_gain_two[:, None],
            g_aup.reshape(RANK, n, COLS // n).transpose(1, 0, 2).reshape(D, 12),
            g_featk.reshape(D, 16),
        ],
        axis=1,
    )
    g_pack = jnp.pad(g_pack, ((0, 0), (0, PACK - g_pack.shape[1]))).astype(bf16)
    nat = g_pack.reshape(nz, 2, 2, r, PACK)
    mine, theirs = pick(nat, c, 2), pick(nat, 1 - c, 2)
    nat = plus(mine, links.swap(theirs, "c"))
    nat = jnp.concatenate(
        [pick(pick(nat, x ^ dx, 1), lax.rem(z - k + nz, nz), 0) for dx in range(2) for k in range(nz)],
        axis=0,
    )
    kv_x = scatter_x(links, jnp.concatenate([kv_sum, nat], axis=1))
    wd_mine, wd_theirs = x_parts(after(g_wd, nat)[None])
    wd_side = links.swap(wd_theirs[0], "x")
    q_line = scatter_line(links, q_x(nat))
    gu_half = join_line([after(p, nat) for p in gu_line])
    gu_both = lax.all_gather(gu_half, "r", axis=0)
    wout_line = wout_line(nat)
    kv_line = scatter_line(links, kv_x(nat))
    q_line = q_line()
    wd_both = lax.all_gather(plus(wd_mine[0], wd_side), "r", axis=0, tiled=True)
    kv_line = kv_line()
    output = (hidden + after(out_sum, nat).astype(f32)).astype(bf16)
    q_line, kv_line = q_line(), kv_line()
    g_wout_own, g_q_own, g_kv_own = wout_line(), q_line(), kv_line()
    g_small = g_kv_own[:, 2 * KVW :]
    g_wd_own = wd_both.astype(f32)
    g_wgu_own = whole_rows(gu_both)
    g_wqkv_own = jnp.concatenate([g_q_own, g_kv_own[:, : 2 * KVW]], axis=1)
    return (
        output.reshape(1, micros, rows, D),
        grad_inputs.reshape(1, micros, rows, D),
        g_small[:, 0],
        g_wqkv_own,
        g_small[:, 1:25],
        g_small[:, 106:118].reshape(RANK, COLS // n),
        g_wout_own,
        g_small[:, 25:33],
        g_small[:, 33:41].T,
        g_small[:, 41:105],
        g_small[:, 118:134].reshape(KVW // n, HD),
        g_small[:, 105],
        g_wgu_own,
        g_wd_own,
    )


def solution(mesh):
    n = mesh.shape["shard"]
    fine = Mesh(mesh.devices.reshape(mesh.shape["replica"], n // 4, 2, 2), ("r", "z", "x", "c"))
    shard = ("z", "x", "c")
    tokens, row, col = P("r", None, shard, None), P(shard, None), P(None, shard)
    return jax.shard_map(
        per_device,
        mesh=fine,
        in_specs=(
            tokens, tokens, P("r", None, None), P("r", None, shard), P(shard), row, row, col, row,
            row, col, row, row, P(shard), row, row,
        ),
        out_specs=(
            tokens, tokens, P(shard), row, row, col, row, row, col, row, row, P(shard), row, row,
        ),
        check_vma=False,
    )
```

```python
import jax
import jax.numpy as jnp
from jax import lax
from jax.experimental import pallas as pl
from jax.experimental.pallas import tpu as pltpu
from jax.sharding import Mesh, PartitionSpec as P

D = 2048
HEADS = 32
KV = 8
HD = 64
FF = 8192
RANK = 8
WINDOW = 64
MAXLEN = 1024
KVW = KV * HD
COLS = D + 2 * KVW
GROUP = HEADS // KV
NORM_EPS = 1e-05
SCALE = 2.0
ROPE_BASE = 500000.0
SROWS = 80
PACK = 256
bf16 = jnp.bfloat16
f32 = jnp.float32


def mm(a, b):
    return jnp.dot(a, b, preferred_element_type=f32)


def mm_t(a, b):
    return lax.dot_general(a, b, (((1,), (1,)), ((), ())), preferred_element_type=f32)


def t_mm(a, b):
    return lax.dot_general(a, b, (((0,), (0,)), ((), ())), preferred_element_type=f32)


class Links:
    def __init__(self):
        self.last = {}

    def move(self, a, axis, pairs, on=None):
        on = on or {"z": ("outer", "middle")}.get(axis, (axis,))
        before = [self.last[link] for link in on if link in self.last]
        if before:
            a = lax.optimization_barrier((a, *before))[0]
        out = lax.ppermute(a, axis, pairs)
        self.last.update({link: out for link in on})
        return out

    def swap(self, a, axis):
        return self.move(a, axis, [(0, 1), (1, 0)])

    def shift(self, a, k):
        nz = lax.axis_size("z")
        return self.move(a, "z", [(i, (i + k) % nz) for i in range(nz)])

    def slots(self):
        nz, z = lax.axis_size("z"), lax.axis_index("z")
        if nz == 4:
            low = z < 2
            return [z, z ^ 1, jnp.where(low, 2, 1), jnp.where(low, 3, 0)]
        return [lax.rem(z - k + nz, nz) for k in [0] + self.line_order()]

    def line_gather(self, block):
        z = lax.axis_index("z")
        if lax.axis_size("z") != 4:
            return [block] + [self.shift(block, k) for k in self.line_order()]
        ends, ends_out, middle = [(0, 1), (1, 0), (2, 3), (3, 2)], [(1, 0), (2, 3)], [(1, 2), (2, 1)]
        inner = (z == 1) | (z == 2)
        first = self.move(block, "z", ends, ("outer",))
        second = self.move(block, "z", middle, ("middle",))
        second_end = self.move(second, "z", ends_out, ("outer",))
        third = self.move(first, "z", middle, ("middle",))
        third_end = self.move(third, "z", ends_out, ("outer",))
        return [
            block,
            lambda *late: after(first, second),
            lambda *late: after(jnp.where(inner, second, second_end), third),
            lambda *late: jnp.where(inner, third, third_end),
        ]

    def line_scatter(self, parts, hold=()):
        if lax.axis_size("z") != 4:
            moved = [self.shift(parts[i + 1], -k) for i, k in enumerate(self.line_order())]
            return sum([m.astype(f32) for m in moved], parts[0].astype(f32))
        ends, ends_in, middle = [(0, 1), (1, 0), (2, 3), (3, 2)], [(0, 1), (3, 2)], [(1, 2), (2, 1)]
        add = lambda a, b: (a.astype(f32) + b.astype(f32)).astype(bf16)
        own, first, second, third = parts
        third_in = self.move(third, "z", ends_in, ("outer",))
        second_in = self.move(second, "z", ends_in, ("outer",))
        third_in = self.move(add(third, third_in), "z", middle, ("middle",))
        second_in = self.move(add(second, second_in), "z", middle, ("middle",))
        first_in = self.move(add(first, third_in), "z", ends, ("outer",))
        return own.astype(f32) + first_in.astype(f32) + second_in.astype(f32)

    def line_order(self):
        nz = lax.axis_size("z")
        return sorted(range(1, nz), key=lambda k: (min(k, nz - k), k))


def pick(a, i, dim):
    return lax.dynamic_index_in_dim(a, i, dim, False)


def after(a, *others):
    return lax.optimization_barrier((a,) + others)[0]


def by_owner(a):
    nz = lax.axis_size("z")
    z, x, c = lax.axis_index("z"), lax.axis_index("x"), lax.axis_index("c")
    width = a.shape[1] // (4 * nz)
    pieces = []
    for dc in range(2):
        for dx in range(2):
            for k in range(nz):
                at = (lax.rem(z - k + nz, nz) * 2 + (x ^ dx)) * 2 + (c ^ dc)
                pieces.append(lax.dynamic_slice_in_dim(a, at * width, width, 1))
    half = 2 * nz
    return jnp.concatenate(pieces[:half], axis=1), jnp.concatenate(pieces[half:], axis=1)


def core_product(links, mine, theirs, right):
    other = links.swap(t_mm(theirs, right).astype(bf16), "c")
    return lambda *late: (t_mm(mine, right) + after(other, *late).astype(f32)).astype(bf16)


def scatter_x(links, t):
    half = t.shape[0] // 2
    other = links.swap(t[half:], "x")
    return lambda *late: (t[:half].astype(f32) + after(other, *late).astype(f32)).astype(bf16)


def scatter_line(links, t):
    nz = lax.axis_size("z")
    mine, theirs = split_replica(t.reshape(nz, -1, t.shape[1]))
    other = links.swap(theirs, "r")

    def second(*late):
        half = (mine.astype(f32) + after(other, *late).astype(f32)).astype(bf16)
        moved = [links.shift(half[k], -k) for k in links.line_order()]

        def third(*late):
            own = sum([after(m, *late).astype(f32) for m in moved], half[0].astype(f32))
            own = own.astype(bf16)
            far = links.swap(own, "r")
            return lambda: join_replica(own, far)

        return third

    return second


def line_columns(links, weight):
    nz, z = lax.axis_size("z"), lax.axis_index("z")
    rows = weight.shape[0]
    wide = FF // nz
    parts = [None] * nz
    for k in [0] + links.line_order():
        to = lax.rem(z + k, nz)
        part = jnp.concatenate(
            [lax.dynamic_slice(weight, (0, g * FF + to * wide), (rows, wide)) for g in range(2)],
            axis=1,
        )
        parts[k] = links.shift(part, k) if k else part
    return parts


def core_columns(links, parts):
    c = lax.axis_index("c")
    loc = parts[0].shape[1] // 8

    def columns(core):
        return jnp.stack(
            [
                jnp.concatenate(
                    [
                        lax.dynamic_slice_in_dim(p, (4 * g + 2 * x + core) * loc, loc, 1)
                        for x in range(2)
                        for g in range(2)
                    ],
                    axis=1,
                )
                for p in parts
            ]
        )

    mine, theirs = columns(c), links.swap(columns(1 - c), "c")
    return jnp.stack([jnp.where(c == 0, mine, theirs), jnp.where(c == 0, theirs, mine)], axis=1)


def join_gate_up(near, near_other, far, far_other):
    nz = lax.axis_size("z")
    z, x, y = lax.axis_index("z"), lax.axis_index("x"), lax.axis_index("r")
    rows, wide = near.shape[2:]
    half = nz // 2

    def body(at_ref, *refs):
        out_ref, h = refs[-1], at_ref[2]
        k, d = pl.program_id(0), pl.program_id(1)
        cases = [(d == 0, refs[0], refs[1])]
        cases += [((d == 1) & (k // half == i), refs[2 + i], refs[4 + i]) for i in range(2)]
        for case, mine, other in cases:

            @pl.when(case)
            def _():
                for c in range(2):
                    out_ref[0, 0, c, pl.ds(h, 1)] = mine[0, c][None]
                    out_ref[0, 0, c, pl.ds(1 - h, 1)] = other[0, c][None]

    shape = (1, 2, rows, wide)
    block = pl.BlockSpec(shape, lambda k, d, at: (k, 0, 0, 0))
    pieces = [
        pl.BlockSpec(shape, lambda k, d, at, i=i: (jnp.clip(k - i * half, 0, half - 1), 0, 0, 0))
        for i in range(2)
    ]
    place = lambda k, d, at: (lax.rem(at[0] - k + nz, nz), at[1] ^ d, 0, 0, 0, 0)
    out = pl.pallas_call(
        body,
        out_shape=jax.ShapeDtypeStruct((nz, 2, 2, 2, rows, wide), bf16),
        grid_spec=pltpu.PrefetchScalarGridSpec(
            num_scalar_prefetch=1,
            grid=(nz, 2),
            in_specs=[block, block] + pieces + pieces,
            out_specs=pl.BlockSpec((1, 1, 2, 2, rows, wide), place),
        ),
        cost_estimate=pl.CostEstimate(
            flops=0, bytes_accessed=16 * near.size, transcendentals=0
        ),
        name="join_gate_up",
    )(jnp.stack([z, x, y]).astype(jnp.int32), near, near_other, *far, *far_other)
    return out.reshape(-1, wide)


def split_replica(t):
    y = lax.axis_index("r")
    t = t.reshape(t.shape[0], 2, -1, t.shape[2])
    return pick(t, y, 1), pick(t, 1 - y, 1)


def join_replica(mine, other):
    y = lax.axis_index("r")
    return jnp.concatenate(
        [jnp.where(y == 0, mine, other), jnp.where(y == 0, other, mine)], axis=0
    ).astype(f32)


def whole_rows(halves):
    nz = lax.axis_size("z")
    rows, cols = halves.shape[1:]
    wide = cols // (4 * nz)

    def body(in_ref, out_ref):
        out_ref[...] = in_ref[...].astype(f32)

    out = pl.pallas_call(
        body,
        out_shape=jax.ShapeDtypeStruct(halves.shape, f32),
        grid=(2, 2 * nz),
        in_specs=[pl.BlockSpec((2, rows, wide), lambda g, j: (0, 0, 2 * j + g))],
        out_specs=pl.BlockSpec((2, rows, wide), lambda g, j: (0, 0, g * 2 * nz + j)),
        cost_estimate=pl.CostEstimate(
            flops=0, bytes_accessed=12 * rows * cols, transcendentals=0
        ),
        name="whole_rows",
    )(halves)
    return out.reshape(2 * rows, cols)


def split_core(links, t, *late):
    c = lax.axis_index("c")
    t = t.reshape(t.shape[0], 2, -1, t.shape[2])
    loc = FF // (4 * lax.axis_size("z"))
    mine, theirs = pick(t, c, 1), after(links.swap(pick(t, 1 - c, 1), "c"), *late)
    first, second = jnp.where(c == 0, mine, theirs), jnp.where(c == 0, theirs, mine)
    pieces = []
    for j in range(t.shape[3] // loc):
        pieces += [first[:, :, j * loc : (j + 1) * loc], second[:, :, j * loc : (j + 1) * loc]]
    return jnp.concatenate(pieces, axis=2)


def split_line(links, t):
    nz, z = lax.axis_size("z"), lax.axis_index("z")
    parts = [pick(t, lax.rem(z + k, nz), 0) for k in range(nz)]
    for k in links.line_order():
        parts[k] = links.shift(parts[k], k)
    return parts


def join_line(parts):
    nz, z = lax.axis_size("z"), lax.axis_index("z")
    rows, wide = parts[0].shape
    out = jnp.zeros((rows, nz * wide), bf16)
    for k in range(nz):
        at = lax.rem(z - k + nz, nz)
        out = lax.dynamic_update_slice(out, parts[k], (0, at * wide))
    return out


def turn(v, cosine, sine):
    lane = lax.broadcasted_iota(jnp.int32, v.shape, 1)
    low_half = (lane & 63) < 32
    other = jnp.where(low_half, pltpu.roll(v, 96, 1), pltpu.roll(v, 32, 1))
    return v * cosine + other * sine


def rope_kernel(v_ref, cos_ref, sin_ref, o_ref, *, turned):
    j = pl.program_id(0)

    @pl.when(j < turned)
    def _():
        for s in range(4):
            at = slice(s * 128, (s + 1) * 128)
            o_ref[:, at] = turn(v_ref[:, at], cos_ref[...], sin_ref[...]).astype(bf16)

    @pl.when(j >= turned)
    def _():
        o_ref[...] = v_ref[...].astype(bf16)


def rope(values, cosine, sine, turned):
    rows, cols = values.shape
    full = pl.BlockSpec((rows, 128), lambda j: (0, 0))
    return pl.pallas_call(
        lambda *refs: rope_kernel(*refs, turned=turned),
        out_shape=jax.ShapeDtypeStruct((rows, cols), bf16),
        grid=(cols // 512,),
        in_specs=[pl.BlockSpec((rows, 512), lambda j: (0, j)), full, full],
        out_specs=pl.BlockSpec((rows, 512), lambda j: (0, j)),
        cost_estimate=pl.CostEstimate(
            flops=6 * rows * cols, bytes_accessed=6 * rows * cols, transcendentals=0
        ),
        name="rope",
    )(values, cosine, sine)


def halves(shape):
    return lax.broadcasted_iota(jnp.int32, shape, 1) < 64


def feature(z2):
    first = halves(z2.shape)
    top = jnp.max(jnp.where(first, z2, -jnp.inf), axis=1, keepdims=True)
    low = jnp.max(jnp.where(first, -jnp.inf, z2), axis=1, keepdims=True)
    e = jnp.exp(z2 - jnp.where(first, top, low))
    s1 = jnp.sum(jnp.where(first, e, 0.0), axis=1, keepdims=True)
    s2 = jnp.sum(jnp.where(first, 0.0, e), axis=1, keepdims=True)
    return e * jnp.where(first, 1.0 / s1, 1.0 / s2)


def feature_grad(phi, dphi):
    first = halves(phi.shape)
    t = phi * dphi
    s1 = jnp.sum(jnp.where(first, t, 0.0), axis=1, keepdims=True)
    s2 = jnp.sum(jnp.where(first, 0.0, t), axis=1, keepdims=True)
    return t - phi * jnp.where(first, s1, s2)


def with_one(v):
    wide = jnp.concatenate([v, jnp.zeros_like(v)], axis=1)
    lane = lax.broadcasted_iota(jnp.int32, wide.shape, 1)
    return jnp.where(lane == 64, jnp.ones_like(wide), wide)


def tile(a):
    return jnp.concatenate([a] * GROUP, axis=0)


def attention_masks(row_ref, col_ref):
    rows, extent = row_ref.shape[0], col_ref.shape[1]
    offset = (
        lax.broadcasted_iota(jnp.int32, (rows, extent), 0)
        + WINDOW
        - lax.broadcasted_iota(jnp.int32, (rows, extent), 1)
    )
    same = row_ref[:, 0:1] == col_ref[0:1, :]
    live = col_ref[1:2, :] > 0
    window = (offset >= 0) & (offset < WINDOW) & same & (live | (offset == 0))
    far = (offset >= WINDOW) & same & live
    return tile(window.astype(f32)) > 0, tile(far.astype(f32)) > 0


def query_heads(ref, hh):
    return [ref[:, (hh * GROUP + i) * HD : (hh * GROUP + i + 1) * HD] for i in range(GROUP)]


def head_forward(q_ref, k, wq_ref, wk, hh, window, far):
    qs = query_heads(q_ref, hh)
    q4 = jnp.concatenate(qs, axis=0)
    s = jnp.where(window, mm_t(q4, k) * 0.125, -1e30)
    top = jnp.max(s, axis=1, keepdims=True)
    p = jnp.exp(s - top)
    e = jnp.exp(-top)
    phi = feature(
        jnp.concatenate([mm(qs[i], wq_ref[hh * GROUP + i]) for i in range(GROUP)], axis=0)
    )
    phik = feature(mm(k, wk))
    phi_b, phik_b = phi.astype(bf16), phik.astype(bf16)
    a_b = (p + e * jnp.where(far, mm_t(phi_b, phik_b), 0.0)).astype(bf16)
    return qs, q4, p, e, phi, phi_b, phik, phik_b, a_b


def full_state(st):
    return jnp.concatenate([st, jnp.zeros((128 - SROWS, 128), bf16)], axis=0)


def attend_kernel(q_ref, k_ref, v_ref, wq_ref, wk_ref, row_ref, col_ref, nd_ref, phi_ref):
    window, far = attention_masks(row_ref, col_ref)
    use = tile(row_ref[:, 1:2])
    for hh in range(2):
        at = slice(hh * HD, (hh + 1) * HD)
        _, _, _, e, phi, _, _, _, a_b = head_forward(
            q_ref, k_ref[:, at], wq_ref, wk_ref[hh], hh, window, far
        )
        nd_ref[0, hh] = mm(a_b, with_one(v_ref[:, at]))
        phi_ref[0, hh] = ((e * use) * phi).astype(bf16)


def finish_kernel(nd_ref, phi_ref, st_ref, row_ref, nd_out, o_ref):
    rows = row_ref.shape[0]
    live = tile(row_ref[:, 2:3])
    for hh in range(2):
        nd = nd_ref[0, hh] + mm_t(phi_ref[0, hh], full_state(st_ref[0, hh]))
        nd_out[0, hh] = nd
        out = (nd[:, :HD] * (live / nd[:, HD : HD + 1])).astype(bf16)
        for i in range(GROUP):
            j = hh * GROUP + i
            o_ref[:, j * HD : (j + 1) * HD] = out[i * rows : (i + 1) * rows]


def numerator_grad(do_ref, nd, live, hh):
    do4 = jnp.concatenate(query_heads(do_ref, hh), axis=0)
    inv = 1.0 / nd[:, HD : HD + 1]
    dnum = do4 * (live * inv)
    dden = -jnp.sum(dnum * nd[:, :HD], axis=1, keepdims=True) * inv
    dn = jnp.concatenate([dnum, jnp.zeros_like(dnum)], axis=1)
    lane = lax.broadcasted_iota(jnp.int32, dn.shape, 1)
    return jnp.where(lane == HD, dden, dn)


def state_grad_kernel(do_ref, nd_ref, phi_ref, row_ref, dst_ref):
    live = tile(row_ref[:, 2:3])
    for hh in range(2):
        dn = numerator_grad(do_ref, nd_ref[0, hh], live, hh)
        dst_ref[0, hh] = t_mm(dn.astype(bf16), phi_ref[0, hh])[:SROWS].astype(bf16)


def attend_back_kernel(
    q_ref, k_ref, v_ref, st_ref, wq_ref, wk_ref, row_ref, col_ref, do_ref, nd_ref, cos_ref,
    sin_ref, dq_ref, dk_ref, dv_ref, dwq_ref, dwk_ref, scr_ref,
):
    rows = q_ref.shape[0]
    window, far = attention_masks(row_ref, col_ref)
    use, live = tile(row_ref[:, 1:2]), tile(row_ref[:, 2:3])
    for hh in range(2):
        at = slice(hh * HD, (hh + 1) * HD)
        k = k_ref[:, at]
        qs, q4, p, e, phi, phi_b, phik, phik_b, a_b = head_forward(
            q_ref, k, wq_ref, wk_ref[hh], hh, window, far
        )
        dn = numerator_grad(do_ref, nd_ref[0, hh], live, hh)
        dn_b = dn.astype(bf16)
        en_b = ((e * use) * dn).astype(bf16)
        da = mm_t(dn_b, with_one(v_ref[:, at]))
        ds_b = (da * p * 0.125).astype(bf16)
        dl_b = jnp.where(far, e * da, 0.0).astype(bf16)
        dv_ref[:, at] = t_mm(a_b, dn_b)[:, :HD]
        dphi = mm(dl_b, phik_b) + mm(en_b, full_state(st_ref[0, hh]))
        dz = feature_grad(phi, dphi).astype(bf16)
        dzk = feature_grad(phik, t_mm(dl_b, phi_b)).astype(bf16)
        dq4 = mm(ds_b, k)
        dk_ref[:, at] = t_mm(ds_b, q4) + mm_t(dzk, wk_ref[hh])
        dwk_ref[0, hh] = t_mm(k, dzk)
        for i in range(GROUP):
            j = hh * GROUP + i
            dzi = dz[i * rows : (i + 1) * rows]
            scr_ref[:, j * HD : (j + 1) * HD] = dq4[i * rows : (i + 1) * rows] + mm_t(
                dzi, wq_ref[j]
            )
            dwq_ref[0, j] = t_mm(qs[i], dzi)
    for s in range(4):
        at = slice(s * 128, (s + 1) * 128)
        dq_ref[:, at] = turn(scr_ref[:, at], cos_ref[...], -sin_ref[...]).astype(bf16)


def state_kernel(k_ref, v_ref, wk_ref, row_ref, add_ref):
    rows = row_ref.shape[0]
    chosen = row_ref[:, 3:4]
    for hh in range(2):
        at = slice(hh * HD, (hh + 1) * HD)
        phik = (feature(mm(k_ref[:rows, at], wk_ref[hh])) * chosen).astype(bf16)
        add_ref[0, hh] = t_mm(with_one(v_ref[:rows, at]), phik)[:SROWS].astype(bf16)


def state_back_kernel(
    k_ref, v_ref, wk_ref, row_ref, dadd_ref, dk_in, dv_in, dk_ref, dv_ref, dwk_ref
):
    rows = row_ref.shape[0]
    chosen = row_ref[:, 3:4]
    dk_ref[rows:] = dk_in[rows:]
    dv_ref[rows:] = dv_in[rows:]
    for hh in range(2):
        at = slice(hh * HD, (hh + 1) * HD)
        k = k_ref[:rows, at]
        phik = feature(mm(k, wk_ref[hh]))
        dadd = full_state(dadd_ref[0, hh])
        dphi = mm(with_one(v_ref[:rows, at]), dadd) * chosen
        dz = feature_grad(phik, dphi).astype(bf16)
        dk_ref[:rows, at] = dk_in[:rows, at] + mm_t(dz, wk_ref[hh])
        dv_ref[:rows, at] = dv_in[:rows, at] + mm_t((phik * chosen).astype(bf16), dadd)[:, :HD]
        dwk_ref[0, hh] = t_mm(k, dz)


def call(kernel, micros, rows, extent, ins, outs, args, flops, scratch=(), only=None, into=()):
    base, count, skip, pairs = (0, micros, 0, 4) if only is None else (only[0], 1, only[1], only[2])
    block = dict(
        q=((rows, 512), lambda m, j: (m + base, j + skip)),
        k=((extent, 128), lambda m, j: (m + base, j + skip)),
        v=((extent, 128), lambda m, j: (m + base, 4 + j + skip)),
        st=((1, 2, SROWS, 128), lambda m, j: (m + base, j + skip, 0, 0)),
        nd=((1, 2, GROUP * rows, 128), lambda m, j: (m + base, j + skip, 0, 0)),
        wq=((8, HD, 128), lambda m, j: (j + skip, 0, 0)),
        wk=((2, HD, 128), lambda m, j: (j + skip, 0, 0)),
        dwq=((1, 8, HD, 128), lambda m, j: (m + base, j + skip, 0, 0)),
        dwk=((1, 2, HD, 128), lambda m, j: (m + base, j + skip, 0, 0)),
        row=((rows, 128), lambda m, j: (m + base, 0)),
        col=((8, extent), lambda m, j: (m + base, 0)),
    )
    shapes = dict(
        q=(micros * rows, D),
        k=(micros * extent, KVW),
        st=(micros, KV, SROWS, 128),
        nd=(micros, KV, GROUP * rows, 128),
        dwq=(micros, HEADS, HD, 128),
        dwk=(micros, KV, HD, 128),
    )
    spec = lambda name: pl.BlockSpec(*block[name])
    size = lambda a: a.size * a.dtype.itemsize
    out_shape = tuple(jax.ShapeDtypeStruct(shapes[name], kind) for name, kind in outs)

    def body(*refs):
        kernel(*refs[: len(ins)], *refs[len(ins) + len(into) :])

    return pl.pallas_call(
        body,
        out_shape=out_shape,
        grid=(count, pairs),
        in_specs=[spec(name) for name in ins] + [pl.BlockSpec(memory_space=pl.ANY)] * len(into),
        out_specs=tuple(spec(name) for name, _ in outs),
        scratch_shapes=scratch,
        input_output_aliases={len(ins) + i: i for i in range(len(into))},
        compiler_params=pltpu.CompilerParams(vmem_limit_bytes=48 << 20),
        cost_estimate=pl.CostEstimate(
            flops=flops * count * pairs // (4 * micros),
            bytes_accessed=(sum(size(a) for a in args) + sum(size(a) for a in out_shape))
            * (count * pairs)
            // (4 * micros),
            transcendentals=count * pairs * HEADS * rows * extent // 4,
        ),
        name=kernel.__name__,
    )(*args, *into)


def ffn_kernel(at_ref, own_ref, other_ref, pair_ref, w_ref, wd_ref, *refs):
    act_ref, dgu_ref, n2_ref, df_ref, mine_ref, theirs_ref, out_ref, dn_acc, out_acc = refs[-9:]
    f, rows, width = pl.program_id(0), own_ref.shape[0], wd_ref.shape[0]
    here = pl.ds(pl.multiple_of(at_ref[1] * rows, rows), rows)
    there = pl.ds(pl.multiple_of((1 - at_ref[1]) * rows, rows), rows)

    @pl.when(f == 0)
    def _():
        n2_ref[here] = own_ref[...]
        n2_ref[there] = other_ref[...]
        df_ref[:rows] = pair_ref[0, 0]
        df_ref[rows:] = pair_ref[0, 1]

    gate_up = mm(n2_ref[...], w_ref[...])
    gate, up = gate_up[:, :width], gate_up[:, width:]
    d_act = mm_t(df_ref[...], wd_ref[...])
    sig = 1.0 / (1.0 + jnp.exp(-gate))
    swish = gate * sig
    acted = (swish * up).astype(bf16)
    d_gate = (d_act * up * (sig * (1.0 + gate * (1.0 - sig)))).astype(bf16)
    d_up = (d_act * swish).astype(bf16)
    act_ref[...] = acted
    d_gu = jnp.concatenate([d_gate, d_up], axis=1)
    dgu_ref[...] = d_gu
    d_n2 = mm_t(d_gu, w_ref[...])
    out = mm(acted, wd_ref[...])

    @pl.when(f == 0)
    def _():
        dn_acc[...] = d_n2
        out_acc[...] = out

    @pl.when(f > 0)
    def _():
        dn_acc[...] += d_n2
        out_acc[...] += out

    @pl.when(f == pl.num_programs(0) - 1)
    def _():
        mine_ref[...] = dn_acc[here]
        theirs_ref[...] = dn_acc[there].astype(bf16)
        out_ref[0, 0] = out_acc[:rows].astype(bf16)
        out_ref[0, 1] = out_acc[rows:].astype(bf16)


def ffn_chunk(k, at, own, other, df_all, wgu, wd, held):
    rows = own.shape[0]
    total, half = df_all.shape[0] * df_all.shape[1] * rows, wd.shape[0]
    width = half // 2
    tiles = half // width
    tokens = pl.BlockSpec((rows, D), lambda f, a: (0, 0))
    chunk = pl.BlockSpec((2 * rows, D), lambda f, a: (k, 0))
    hidden = pl.BlockSpec((2 * rows, width), lambda f, a: (k, f))
    pair = pl.BlockSpec((1, 2, rows, D), lambda f, a: (a[0], 0, 0, 0))
    whole = (total, D)
    outs = [((total, half), bf16), ((total, 2 * half), bf16)] + [(whole, bf16)] * 2
    outs += [((rows, D), f32), ((rows, D), bf16), (df_all.shape, bf16)]
    return pl.pallas_call(
        ffn_kernel,
        out_shape=tuple(jax.ShapeDtypeStruct(a, b) for a, b in outs),
        grid_spec=pltpu.PrefetchScalarGridSpec(
            num_scalar_prefetch=1,
            grid=(tiles,),
            in_specs=[
                tokens,
                tokens,
                pair,
                pl.BlockSpec((D, 2 * width), lambda f, a: (0, f)),
                pl.BlockSpec((width, D), lambda f, a: (f, 0)),
            ]
            + [pl.BlockSpec(memory_space=pl.ANY)] * len(held),
            out_specs=(
                hidden, pl.BlockSpec((2 * rows, 2 * width), lambda f, a: (k, f)), chunk, chunk,
                tokens, tokens,
                pair,
            ),
            scratch_shapes=[pltpu.VMEM((2 * rows, D), f32)] * 2,
        ),
        input_output_aliases={6 + i: (i if i < 4 else 6) for i in range(len(held))},
        compiler_params=pltpu.CompilerParams(vmem_limit_bytes=56 << 20),
        cost_estimate=pl.CostEstimate(
            flops=24 * rows * D * half,
            bytes_accessed=6 * D * half + 40 * rows * D,
            transcendentals=2 * rows * half,
        ),
        name="ffn_chunk",
    )(at, own, other, df_all, wgu, wd, *held)


def weigh(flag, a):
    return jnp.where(flag[:, None, None, None], a.astype(f32), 0.0)


def entering(links, add, tags, reach):
    nz = lax.axis_size("z")
    z, x, c = lax.axis_index("z"), lax.axis_index("x"), lax.axis_index("c")
    p = (z * 2 + x) * 2 + c
    tag = lambda i: pick(tags, jnp.clip(i, 0, 4 * nz - 1), 1)
    prev = tag(p - 1)
    chip = (z * 2 + x) * 2
    other = links.swap(add, "c")
    other = after(other, (yield))
    one = tag(chip) == tag(chip + 1)
    chip_sum = (weigh((c == 1) | one, add) + weigh((c == 0) | one, other)).astype(bf16)
    side = links.swap(chip_sum, "x")
    side = after(side, (yield))
    one = tag(z * 4 + 1) == tag(z * 4 + 3)
    layer = (weigh((x == 1) | one, chip_sum) + weigh((x == 0) | one, side)).astype(bf16)
    state = weigh((c == 1) & (prev >= 0), other) + weigh((x == 1) & (tag(z * 4 + 1) == prev), side)
    got = [
        links.move(layer, "z", [(i, i + hop) for i in range(nz - hop)])
        for hop in range(1, min(reach, nz - 1) + 1)
    ]
    late = yield
    for hop, far in enumerate(got, 1):
        state += weigh((z >= hop) & (tag((z - hop) * 4 + 3) == prev), after(far, late))
    yield state.astype(bf16)


def leaving(links, dstate, tags, reach):
    nz = lax.axis_size("z")
    z, x, c = lax.axis_index("z"), lax.axis_index("x"), lax.axis_index("c")
    p = (z * 2 + x) * 2 + c
    tag = lambda i: pick(tags, jnp.clip(i, 0, 4 * nz - 1), 1)
    from_tag = lambda i: jnp.where(i > 0, tag(i - 1), -1)
    own = tag(p)
    chip = (z * 2 + x) * 2
    other = links.swap(dstate, "c")
    other = after(other, (yield))
    one = from_tag(chip) == from_tag(chip + 1)
    chip_sum = (weigh((c == 0) | one, dstate) + weigh((c == 1) | one, other)).astype(bf16)
    side = links.swap(chip_sum, "x")
    side = after(side, (yield))
    one = from_tag(z * 4) == from_tag(z * 4 + 2)
    layer = (weigh((x == 0) | one, chip_sum) + weigh((x == 1) | one, side)).astype(bf16)
    total = weigh((c == 0) & (own >= 0), other) + weigh(
        (x == 0) & (from_tag(z * 4 + 2) == own), side
    )
    got = [
        links.move(layer, "z", [(i, i - hop) for i in range(hop, nz)])
        for hop in range(1, min(reach, nz - 1) + 1)
    ]
    late = yield
    for hop, far in enumerate(got, 1):
        total += weigh((z + hop < nz) & (from_tag((z + hop) * 4) == own), after(far, late))
    yield total.astype(bf16)


def per_device(
    inputs, cotangent, lengths, padding, gain_attn_own, wqkv_own, adown_own, aup_own, wout_own,
    odown_own, oup_own, featq_own, featk_own, gain_ffn_own, wgu_own, wd_own,
):
    nz = lax.axis_size("z")
    n = 4 * nz
    z, x, c = lax.axis_index("z"), lax.axis_index("x"), lax.axis_index("c")
    place_own = (z * 2 + x) * 2 + c
    micros, rows = inputs.shape[1], inputs.shape[2]
    both = micros * rows
    extent = rows + WINDOW
    reach = -(-MAXLEN // (4 * rows))
    everyone = ("z", "x", "c")
    chain = (everyone, [(i, i + 1) for i in range(n - 1)])
    unchain = (everyone, [(i, i - 1) for i in range(1, n)])
    r = D // n

    pack = jnp.concatenate(
        [
            gain_attn_own[:, None], adown_own, odown_own, oup_own.T, featq_own,
            gain_ffn_own[:, None], aup_own.reshape(r, 12), featk_own.reshape(r, 16),
        ],
        axis=1,
    )
    pack = jnp.pad(pack, ((0, 0), (0, PACK - pack.shape[1])))
    links = Links()
    live_all = padding[0].astype(bf16)
    halo_live = lax.ppermute(live_all[:, rows - WINDOW :], *chain)
    first = lax.all_gather(
        jnp.concatenate([wqkv_own, wout_own, pack], axis=1), everyone, axis=0, tiled=True
    )
    wqkv, wout, small = first[:, :COLS], first[:, COLS : COLS + D], first[:, COLS + D :]
    cot = cotangent[0].reshape(both, D)
    y = lax.axis_index("r")
    wgu_half = lax.dynamic_slice_in_dim(wgu_own, y * (r // 2), r // 2, 0)
    wgu_near = core_columns(links, line_columns(links, wgu_half))
    wgu_near_other = links.swap(wgu_near, "r")
    small, wgu_send = lax.optimization_barrier((small, wgu_near, wgu_near_other))[:2]
    wgu_far = [links.swap(wgu_send[: nz // 2], "x")]
    gain_one = small[:, 0].astype(f32)[None]
    adown = small[:, 1:25]
    odown = small[:, 25:33]
    oup_t = small[:, 33:41]
    featq = small[:, 41:105].reshape(HEADS, HD, HD)
    gain_two = small[:, 105].astype(f32)[None]
    aup = small[:, 106:118].reshape(n, RANK, COLS // n).transpose(1, 0, 2).reshape(RANK, COLS)
    featk = small[:, 118:134].reshape(KV, HD, HD)
    wq2 = jnp.concatenate([featq, -featq], axis=2)
    wk2 = jnp.concatenate([featk, -featk], axis=2)
    column = jnp.arange(COLS)[None]
    owner = jnp.where(column < D, 0, jnp.where(column < D + KVW, 1, 2))
    aup_wide = jnp.concatenate(
        [jnp.where(owner == t, aup, jnp.zeros_like(aup)) for t in range(3)], axis=0
    )

    doc_lengths = lengths[0]
    ends = jnp.cumsum(doc_lengths, axis=1)
    places = place_own * rows - WINDOW + jnp.arange(extent, dtype=jnp.int32)
    done = ends[:, None, :] <= places[None, :, None]
    seg_ext = jnp.sum(done.astype(jnp.int32), axis=2)
    pos = places[None] - jnp.sum(jnp.where(done, doc_lengths[:, None, :], 0), axis=2)
    pos = pos[:, WINDOW:].reshape(both)
    edges = jnp.arange(n, dtype=jnp.int32) * rows + (rows - WINDOW - 1)
    tags = jnp.sum((ends[:, None, :] <= edges[None, :, None]).astype(jnp.int32), axis=2)
    live_ext = jnp.concatenate([halo_live, live_all], axis=1).astype(f32)
    prev_tag = jnp.where(place_own > 0, pick(tags, jnp.maximum(place_own - 1, 0), 1), -1)
    own_tag = pick(tags, place_own, 1)
    seg_own = seg_ext[:, WINDOW:]
    info = jnp.stack(
        [
            seg_own.astype(f32),
            (seg_own == prev_tag[:, None]).astype(f32),
            live_ext[:, WINDOW:],
            ((seg_ext[:, :rows] == own_tag[:, None]) & (live_ext[:, :rows] > 0)).astype(f32),
        ],
        axis=2,
    ).reshape(both, 4)
    rowinfo = jnp.pad(info, ((0, 0), (0, 124)))
    colinfo = jnp.pad(
        jnp.stack([seg_ext.astype(f32), live_ext], axis=1), ((0, 0), (0, 6), (0, 0))
    ).reshape(micros * 8, extent)
    lane = jnp.arange(128)
    frequency = ROPE_BASE ** (-((lane % 32).astype(f32) * 2.0) / HD)
    angles = pos.astype(f32)[:, None] * frequency[None, :]
    cosine = jnp.cos(angles)
    sine = jnp.where((lane % 64 < 32)[None], -1.0, 1.0) * jnp.sin(angles)

    act = inputs[0].reshape(both, D).astype(f32)
    inv_one = lax.rsqrt(jnp.mean(act * act, axis=-1, keepdims=True) + NORM_EPS)
    n1 = (act * inv_one * gain_one).astype(bf16)
    adapt = mm(n1, adown).astype(bf16)
    projected = mm(n1, wqkv) + SCALE * mm(adapt, aup_wide)
    qkv = rope(projected, cosine, sine, 5)
    kv = qkv[:, D:].reshape(micros, rows, 2 * KVW)
    crossing = ("x", "outer", "middle")
    halo = links.move(kv[:, rows - WINDOW :], *chain, crossing)
    kv_ext = jnp.concatenate([halo, kv], axis=1).reshape(micros * extent, 2 * KVW)
    launch = lambda kernel, ins, outs, args, work, **k: call(
        kernel, micros, rows, extent, ins, outs, args, micros * HEADS * rows * work, **k
    )
    (add,) = launch(
        state_kernel, ("k", "v", "wk", "row"), [("st", bf16)], (kv_ext, kv_ext, wk2, rowinfo), 8192
    )
    df_all = lax.all_gather(after(cot, small), ("z", "c"), axis=0, tiled=True)
    df_all = df_all.reshape(nz, 2, both, D)
    parts = [(m, j, 2) for m in range(micros) for j in (0, 2)]
    travel = entering(links, add, tags, reach)
    next(travel)
    wgu_far[0], wk2_late = lax.optimization_barrier((wgu_far[0], wk2, add))[:2]
    wgu_far_other = [links.swap(wgu_far[0], "r")]
    local = ()
    for i, part in enumerate(parts):
        local = launch(
            attend_kernel,
            ("q", "k", "v", "wq", "wk", "row", "col"),
            [("nd", f32), ("nd", bf16)],
            (qkv, kv_ext, kv_ext, wq2, wk2_late, rowinfo, colinfo),
            1000 * extent,
            only=part,
            into=local,
        )
        if i == 0:
            travel.send(local[1])
            wgu_far.append(links.swap(wgu_near[nz // 2 :], "x"))
            wd_other = links.swap(wd_own, "x")
        elif i == 1:
            travel.send(local[1])
        elif i == 2:
            state = travel.send(local[1])
            wk2_late = after(wk2_late, state)
    nd, phi = local
    wgu_far[1], nd = lax.optimization_barrier((wgu_far[1], nd, wgu_far_other[0]))[:2]
    wgu_far_other.append(links.swap(wgu_far[1], "r"))
    nd, attn = launch(
        finish_kernel,
        ("nd", "nd", "st", "row"),
        [("nd", f32), ("q", bf16)],
        (nd, phi, state, rowinfo),
        32768,
    )
    adapt_out = mm(attn, odown).astype(bf16)
    hidden = act + (mm(attn, wout) + SCALE * mm_t(adapt_out, oup_t))
    inv_two = lax.rsqrt(jnp.mean(hidden * hidden, axis=-1, keepdims=True) + NORM_EPS)
    n2 = (hidden * inv_two * gain_two).astype(bf16)

    half = 2 * FF // n
    loc = half // 2
    n2_parts = links.line_gather(n2)
    late = lambda a: after(a, attn)
    wgu = join_gate_up(*[late(a) for a in (wgu_near, wgu_near_other)], wgu_far, [late(a) for a in wgu_far_other])
    wd = jnp.concatenate(
        [jnp.where(x == 0, wd_own, wd_other), jnp.where(x == 0, wd_other, wd_own)], axis=0
    )
    returned, held = [], ()
    for i, (place, part) in enumerate(zip(links.slots(), n2_parts)):
        at = jnp.stack([place, c]).astype(jnp.int32)
        part = part() if callable(part) else part
        if i:
            part = after(part, held[0])
        result = ffn_chunk(i, at, part, links.swap(part, "c"), df_all, wgu, wd, held)
        held = result[:4] + result[6:]
        d_n2_i = result[4] + links.swap(result[5], "c").astype(f32)
        returned.append(d_n2_i.astype(bf16) if i else d_n2_i)
    acted, d_gu, n2_all, df_held, out_parts = held
    d_n2 = links.line_scatter(returned)
    g_wgu = t_mm(n2_all, d_gu).astype(bf16)
    g_wd = t_mm(acted, df_held).astype(bf16)
    d_n2 = after(d_n2, g_wgu, g_wd)
    plus = lambda a, b: (a.astype(f32) + b.astype(f32)).astype(bf16)

    def replica_sum(g):
        halves = g.reshape(g.shape[0], 2, -1, g.shape[2]).transpose(1, 0, 2, 3)
        return lax.psum_scatter(halves, "r", scatter_dimension=0, tiled=False)

    def x_parts(t):
        return pick(t, x, 1), pick(t, 1 - x, 1)

    g_wgu = replica_sum(g_wgu.reshape(n, r, 2 * half))
    out_sum = lax.psum_scatter(
        after(out_parts, d_n2).reshape(-1, D), ("z", "c"), scatter_dimension=0, tiled=True
    )
    g_wd = replica_sum(after(g_wd, out_sum).reshape(2, loc, D))

    d_hidden = (
        cot.astype(f32)
        + gain_two * inv_two * d_n2
        - hidden * inv_two**3 * jnp.mean(hidden * gain_two * d_n2, axis=-1, keepdims=True)
    )
    d_branch = d_hidden.astype(bf16)
    d_adapt_out = (SCALE * mm(d_branch, oup_t)).astype(bf16)
    d_attn = mm_t(d_branch, wout) + mm_t(d_adapt_out, odown)
    (dst,) = launch(
        state_grad_kernel,
        ("q", "nd", "nd", "row"),
        [("st", bf16)],
        (d_attn, nd, phi, rowinfo),
        32768,
    )
    attn_owner, n1_owner = by_owner(attn), by_owner(n1)
    travel = leaving(links, dst, tags, reach)
    next(travel)
    wout_core = core_product(links, *attn_owner, d_branch)
    grads = ()
    d_attn_late = d_attn
    for i, part in enumerate(parts):
        grads = launch(
            attend_back_kernel,
            ("q", "k", "v", "st", "wq", "wk", "row", "col", "q", "nd", "row", "row"),
            [("q", bf16), ("k", f32), ("k", f32), ("dwq", f32), ("dwk", f32)],
            (qkv, kv_ext, kv_ext, state, wq2, wk2, rowinfo, colinfo, d_attn_late, nd, cosine, sine),
            2000 * extent,
            scratch=[pltpu.VMEM((rows, 512), f32)],
            only=part,
            into=grads,
        )
        done = grads[0]
        if i == 0:
            travel.send(done)
            gu_mine, gu_theirs = x_parts(after(g_wgu, done).reshape(nz, 2, r, 2 * half))
            gu_side = links.swap(gu_theirs, "x")
            wout_x = scatter_x(links, wout_core(done))
        elif i == 1:
            travel.send(done)
        elif i == 2:
            dadd = travel.send(done)
            d_attn_late = after(d_attn_late, dadd, out_sum)
    dq, dk, dv, dwq, dwk = grads
    gu_rows = split_core(links, plus(gu_mine, after(gu_side, dq)))
    wout_line = scatter_line(links, wout_x(dq))
    q_core = core_product(links, *n1_owner, dq)
    dk, dv, dwk_more = launch(
        state_back_kernel,
        ("k", "v", "wk", "row", "st", "k", "k"),
        [("k", f32), ("k", f32), ("dwk", f32)],
        (kv_ext, kv_ext, wk2, rowinfo, dadd, dk, dv),
        16384,
    )
    d_kv = jnp.concatenate([dk, dv], axis=1).reshape(micros, extent, 2 * KVW)
    sent = links.move(d_kv[:, :WINDOW].astype(bf16), *unchain, crossing)
    q_sum, gu_rows, sent = lax.optimization_barrier((q_core(dadd), gu_rows, sent))
    q_x = scatter_x(links, q_sum)
    gu_line = split_line(links, gu_rows)
    wout_line = wout_line(dadd, sent)
    sent = sent.astype(f32)
    d_kv = jnp.concatenate([d_kv[:, WINDOW:rows], d_kv[:, rows:] + sent], axis=1)
    d_kv = rope(d_kv.reshape(both, 2 * KVW), cosine, -sine, 1)
    kv_sum = core_product(links, *n1_owner, d_kv)()
    d_proj = jnp.concatenate([dq, d_kv], axis=1)
    d_adapt = (SCALE * mm_t(d_proj, aup_wide)).astype(bf16)
    d_n1 = mm_t(d_proj, wqkv) + mm_t(d_adapt, adown)
    g_gain_one = jnp.sum(d_n1 * act * inv_one, axis=0)
    grad_inputs = (
        d_hidden
        + gain_one * inv_one * d_n1
        - act * inv_one**3 * jnp.mean(act * gain_one * d_n1, axis=-1, keepdims=True)
    ).astype(bf16)
    g_adown = t_mm(n1, d_adapt)
    wide = SCALE * t_mm(adapt, d_proj)
    g_aup = jnp.where(owner == 0, wide[:8], jnp.where(owner == 1, wide[8:16], wide[16:24]))
    g_odown = t_mm(attn, d_adapt_out)
    g_oup_t = SCALE * t_mm(d_branch, adapt_out)
    fold = lambda a: a[:, :, :HD] - a[:, :, HD:]
    g_featq = fold(jnp.sum(dwq, axis=0)).reshape(D, HD)
    g_featk = fold(jnp.sum(dwk + dwk_more, axis=0))
    g_gain_two = jnp.sum(d_n2 * hidden * inv_two, axis=0)
    g_pack = jnp.concatenate(
        [
            g_gain_one[:, None], g_adown, g_odown, g_oup_t, g_featq, g_gain_two[:, None],
            g_aup.reshape(RANK, n, COLS // n).transpose(1, 0, 2).reshape(D, 12),
            g_featk.reshape(D, 16),
        ],
        axis=1,
    )
    g_pack = jnp.pad(g_pack, ((0, 0), (0, PACK - g_pack.shape[1]))).astype(bf16)
    nat = g_pack.reshape(nz, 2, 2, r, PACK)
    mine, theirs = pick(nat, c, 2), pick(nat, 1 - c, 2)
    nat = plus(mine, links.swap(theirs, "c"))
    nat = jnp.concatenate(
        [pick(pick(nat, x ^ dx, 1), lax.rem(z - k + nz, nz), 0) for dx in range(2) for k in range(nz)],
        axis=0,
    )
    kv_x = scatter_x(links, jnp.concatenate([kv_sum, nat], axis=1))
    wd_mine, wd_theirs = x_parts(after(g_wd, nat)[None])
    wd_side = links.swap(wd_theirs[0], "x")
    q_line = scatter_line(links, q_x(nat))
    gu_half = join_line([after(p, nat) for p in gu_line])
    gu_both = lax.all_gather(gu_half, "r", axis=0)
    wout_line = wout_line(nat)
    kv_line = scatter_line(links, kv_x(nat))
    q_line = q_line()
    wd_both = lax.all_gather(plus(wd_mine[0], wd_side), "r", axis=0, tiled=True)
    kv_line = kv_line()
    output = (hidden + after(out_sum, nat).astype(f32)).astype(bf16)
    q_line, kv_line = q_line(), kv_line()
    g_wout_own, g_q_own, g_kv_own = wout_line(), q_line(), kv_line()
    g_small = g_kv_own[:, 2 * KVW :]
    g_wd_own = wd_both.astype(f32)
    g_wgu_own = whole_rows(gu_both)
    g_wqkv_own = jnp.concatenate([g_q_own, g_kv_own[:, : 2 * KVW]], axis=1)
    return (
        output.reshape(1, micros, rows, D),
        grad_inputs.reshape(1, micros, rows, D),
        g_small[:, 0],
        g_wqkv_own,
        g_small[:, 1:25],
        g_small[:, 106:118].reshape(RANK, COLS // n),
        g_wout_own,
        g_small[:, 25:33],
        g_small[:, 33:41].T,
        g_small[:, 41:105],
        g_small[:, 118:134].reshape(KVW // n, HD),
        g_small[:, 105],
        g_wgu_own,
        g_wd_own,
    )


def solution(mesh):
    n = mesh.shape["shard"]
    fine = Mesh(mesh.devices.reshape(mesh.shape["replica"], n // 4, 2, 2), ("r", "z", "x", "c"))
    shard = ("z", "x", "c")
    tokens, row, col = P("r", None, shard, None), P(shard, None), P(None, shard)
    return jax.shard_map(
        per_device,
        mesh=fine,
        in_specs=(
            tokens, tokens, P("r", None, None), P("r", None, shard), P(shard), row, row, col, row,
            row, col, row, row, P(shard), row, row,
        ),
        out_specs=(
            tokens, tokens, P(shard), row, row, col, row, row, col, row, row, P(shard), row, row,
        ),
        check_vma=False,
    )
```
